32 devices in a mesh: dp: 4 (over z), krow: 8 (over y, x, core).
Axes of the slice: x: 2, y: 2, z: 4, core: 2. Of those that a mesh axis runs over, the one named last changes fastest.
Arguments:
- tokens: bfloat16 [12, 2048, 768], P('dp', 'krow'), may hold values from -6 to 6
- lengths: int32 [12], P('dp'), may hold values from 65 to 2048, as said below
- attn_gain: float32 [768], replicated, may hold values from 0.5 to 1.5
- attn_bias: float32 [768], replicated, may hold values from -1 to 1
- query_weight: bfloat16 [768, 768], replicated, may hold values from -0.4375 to 0.4375
- key_weight: bfloat16 [768, 768], replicated, may hold values from -0.21875 to 0.21875
- value_weight: bfloat16 [768, 768], replicated, may hold values from -0.21875 to 0.21875
- out_weight: bfloat16 [768, 768], replicated, may hold values from -3.5 to 3.5
- compress: bfloat16 [256, 2048], P('krow'), may hold values from -0.125 to 0.125
- ffn_gain: float32 [768], replicated, may hold values from 0.5 to 1.5
- ffn_bias: float32 [768], replicated, may hold values from -1 to 1
- up_weight: bfloat16 [768, 3072], replicated, may hold values from -0.21875 to 0.21875
- down_weight: bfloat16 [3072, 768], replicated, may hold values from -0.109375 to 0.109375
- cotangent: bfloat16 [12, 2048, 768], P('dp', 'krow'), may hold values from -6 to 6
Outputs:
- block_out: bfloat16 [12, 2048, 768], P('dp', 'krow')
- tokens_grad: bfloat16 [12, 2048, 768], P('dp', 'krow')
- attn_gain_grad: float32 [768], replicated
- attn_bias_grad: float32 [768], replicated
- query_weight_grad: float32 [768, 768], replicated
- key_weight_grad: float32 [768, 768], replicated
- value_weight_grad: float32 [768, 768], replicated
- out_weight_grad: float32 [768, 768], replicated
- compress_grad: float32 [256, 2048], P('krow')
- ffn_gain_grad: float32 [768], replicated
- ffn_bias_grad: float32 [768], replicated
- up_weight_grad: float32 [768, 3072], replicated
- down_weight_grad: float32 [3072, 768], replicated
- grad_norm: float32 [], replicated
The draws below stay inside these ranges and needn't reach their ends.
Inputs may be any that keep to these rules, and one draw needn't show every extreme that they name: `lengths`: at least one sequence is 2048 positions long; positions at or past a sequence's length are padding.
All inputs are finite; a program needn't handle non-finite values.
Results may differ from the reference program's by a relative error of at most 0.019.
Values may be sent and summed in bfloat16 or wider, within the bound.
No kernel may reach another device: no remote copies, remote signals or barrier semaphores. Data moves between devices by JAX's collectives and lax.ppermute only.
A program may use at most 256 MiB of HBM per device.

```python
import jax
import jax.numpy as jnp
from jax import lax

D = 768
HEADS = 12
HEAD_DIM = 64
FF = 3072
KPROJ = 256
PADLEN = 2048
SEQS = 12


def draw_lengths(key, part):
    length_key, full_key = jax.random.split(key)
    drawn_lengths = jax.random.randint(length_key, (SEQS,), PADLEN // 32 + 1, PADLEN + 1)
    full_length = jax.random.randint(full_key, (SEQS,), 0, 4) == 0
    full_length = full_length.at[0].set(True)
    return jnp.where(full_length, PADLEN, drawn_lengths).astype(jnp.int32)


def levels(key, shape, cuts, low, largest):
    def one(axis_at, shards_of):
        heights = jax.random.uniform(jax.random.fold_in(jax.random.fold_in(key, 6), axis_at), (shards_of,), jnp.float32, low / len(cuts), largest / len(cuts))
        return jnp.repeat(jnp.exp(heights), shape[axis_at] // shards_of).reshape((-1,) + (1,) * (len(shape) - axis_at - 1))

    level = one(*cuts[0])
    for cut in cuts[1:]:
        level = level * one(*cut)
    return level


def bell_draw(key, dims, scale, reach, shards=(), kind=jnp.bfloat16):
    values = jax.random.normal(key, dims, jnp.float32) * scale
    if len(shards) > 0:
        values = levels(key, dims, shards, -0.22, 0.18) * values
    return jnp.clip(values, min=-reach, max=reach).astype(kind)


def setup_inputs(seed: int = 0) -> dict:
    splits = jax.random.split(jax.random.key(seed), 15)
    tokens = bell_draw(splits[0], (SEQS, PADLEN, D), 1.0, 6.0, ((0, 4), (1, 8)))
    lengths = draw_lengths(jax.random.fold_in(splits[14], 71), 0)
    attn_gain = jnp.clip(1.0 + 0.1 * jax.random.normal(splits[2], (D,), jnp.float32), 0.5, 1.5)
    attn_bias = bell_draw(splits[3], (D,), 0.2, 1.0, (), jnp.float32)
    query_weight = bell_draw(splits[4], (D, D), (D // 4) ** -0.5, 0.4375)
    key_weight = bell_draw(splits[5], (D, D), D ** -0.5, 0.21875)
    value_weight = bell_draw(splits[6], (D, D), D ** -0.5, 0.21875)
    out_weight = bell_draw(splits[7], (D, D), (D // KPROJ) ** -0.5, 3.5)
    compress = bell_draw(splits[8], (KPROJ, PADLEN), PADLEN ** -0.5, 0.125, ((0, 8),))
    ffn_gain = jnp.clip(1.0 + 0.1 * jax.random.normal(splits[9], (D,), jnp.float32), 0.5, 1.5)
    ffn_bias = bell_draw(splits[10], (D,), 0.2, 1.0, (), jnp.float32)
    up_weight = bell_draw(splits[11], (D, FF), D ** -0.5, 0.21875)
    down_weight = bell_draw(splits[12], (FF, D), FF ** -0.5, 0.109375)
    cotangent = bell_draw(splits[13], (SEQS, PADLEN, D), 1.0, 6.0, ((0, 4), (1, 8)))
    return {"tokens": tokens, "lengths": lengths, "attn_gain": attn_gain, "attn_bias": attn_bias, "query_weight": query_weight, "key_weight": key_weight, "value_weight": value_weight, "out_weight": out_weight, "compress": compress, "ffn_gain": ffn_gain, "ffn_bias": ffn_bias, "up_weight": up_weight, "down_weight": down_weight, "cotangent": cotangent}


@jax.custom_vjp
def low(v):
    return lax.optimization_barrier(v.astype(jnp.bfloat16)).astype(jnp.float32)

@jax.custom_vjp
def low_back(v):
    return v

def low_keep(v):
    return (low(v), None)

def low_pass(kept, grad):
    return (grad,)

def back_keep(v):
    return (v, None)

def back_low(kept, grad):
    return (low(grad),)
low.defvjp(low_keep, low_pass)
low_back.defvjp(back_keep, back_low)
EPSILON = 1e-05
PRECISE = lax.Precision.HIGHEST

def normalize(values, scale_vec, shift_vec):
    centred = values - lax.optimization_barrier(jnp.mean(values, axis=-1, keepdims=True))
    spread = lax.optimization_barrier(jnp.mean(centred * centred, axis=-1, keepdims=True))
    return centred * lax.rsqrt(spread + EPSILON) * scale_vec + shift_vec

def block_layer(params, inputs, valid_mask):
    attn_gain, attn_bias, query_weight, key_weight, value_weight, out_weight, compress, ffn_gain, ffn_bias, up_weight, down_weight = params
    row_count = inputs.shape[0]
    normed = low(normalize(inputs, attn_gain, attn_bias))
    queries = low(low_back(jnp.dot(normed, query_weight, precision=PRECISE)))
    masked = compress * valid_mask[None, :]
    summary = low(low_back(jnp.dot(masked, normed, precision=PRECISE)))
    key_rows = low(low_back(jnp.dot(summary, key_weight, precision=PRECISE)))
    value_rows = low(low_back(jnp.dot(summary, value_weight, precision=PRECISE)))
    query_heads = queries.reshape(row_count, HEADS, HEAD_DIM)
    key_heads = key_rows.reshape(KPROJ, HEADS, HEAD_DIM)
    value_heads = value_rows.reshape(KPROJ, HEADS, HEAD_DIM)
    scores = low_back(jnp.einsum('thd,jhd->hjt', query_heads, key_heads, precision=PRECISE) * HEAD_DIM ** (-0.5))
    attn_probs = jax.nn.softmax(scores, axis=1)
    mixed_rows = jnp.einsum('hjt,jhd->thd', low(attn_probs), value_heads, precision=PRECISE).reshape(row_count, D)
    mixed_rows = low(low_back(mixed_rows))
    attended = inputs + low_back(jnp.dot(mixed_rows, out_weight, precision=PRECISE))
    lifted = low(normalize(attended, ffn_gain, ffn_bias))
    hidden = low_back(jnp.dot(lifted, up_weight, precision=PRECISE))
    active = low(jax.nn.gelu(hidden, approximate=False))
    return attended + jnp.dot(active, down_weight, precision=PRECISE)

def reference(tokens, lengths, attn_gain, attn_bias, query_weight, key_weight, value_weight, out_weight, compress, ffn_gain, ffn_bias, up_weight, down_weight, cotangent):
    params = (attn_gain.astype(jnp.float32), attn_bias.astype(jnp.float32), query_weight.astype(jnp.float32), key_weight.astype(jnp.float32), value_weight.astype(jnp.float32), out_weight.astype(jnp.float32), compress.astype(jnp.float32), ffn_gain.astype(jnp.float32), ffn_bias.astype(jnp.float32), up_weight.astype(jnp.float32), down_weight.astype(jnp.float32))
    positions = jnp.arange(PADLEN, dtype=jnp.int32)

    def accumulate(totals, element):
        sequence, length, seq_cotangent = element
        valid_mask = (positions < length).astype(jnp.float32)

        def forward(weights, inputs):
            return block_layer(weights, inputs, valid_mask)
        result, pullback = jax.vjp(forward, params, sequence.astype(jnp.float32))
        gradients, input_grad = pullback(seq_cotangent.astype(jnp.float32))
        totals = jax.tree.map(jnp.add, totals, gradients)
        return (totals, (result.astype(jnp.bfloat16), input_grad.astype(jnp.bfloat16)))
    initial = jax.tree.map(jnp.zeros_like, params)
    totals, (block_out, tokens_grad) = lax.scan(accumulate, initial, (tokens, lengths, cotangent))
    squares = jnp.sum(totals[0] * totals[0])
    for member in (totals[1], totals[2], totals[3], totals[4], totals[5], totals[7], totals[8], totals[9], totals[10]):
        squares = squares + jnp.sum(member * member)
    grad_norm = jnp.sqrt(squares)
    return (block_out, tokens_grad, totals[0], totals[1], totals[2], totals[3], totals[4], totals[5], totals[6], totals[7], totals[8], totals[9], totals[10], grad_norm)
```

```python
import jax
import jax.numpy as jnp
from jax import lax
from jax.sharding import PartitionSpec as P

D = 768
HEADS = 12
HEAD_DIM = 64
FF = 3072
EPSILON = 1e-05
SCALE = HEAD_DIM ** (-0.5)
LOW = jnp.bfloat16


def swap(value, axis, mask):
    size = lax.axis_size(axis)
    return lax.ppermute(value, axis, [(i, i ^ mask) for i in range(size)])


def pick(value, at):
    return lax.dynamic_index_in_dim(value, at, 0, keepdims=False)


def bits_of(axis):
    return (lax.axis_size(axis) - 1).bit_length()


def bit(axis, at):
    return (lax.axis_index(axis) >> at) & 1


def in_order(mine, other, at):
    return jnp.where(at == 0, jnp.stack([mine, other]), jnp.stack([other, mine]))


def fold(value, axis, at):
    mine = bit(axis, at)
    return pick(value, mine) + swap(pick(value, 1 - mine), axis, 1 << at)


def unfold(value, axis, at):
    return in_order(value, swap(value, axis, 1 << at), bit(axis, at))


def sum_everywhere(part):
    count = bits_of("krow")
    rows, columns = part.shape
    half = fold(part.reshape(2, rows // 2, columns), "krow", 0)
    orders = [list(range(1, count)), list(range(count - 1, 0, -1))]
    pieces = []
    for color in range(2):
        piece = half.reshape(2, rows // 4, columns)[color]
        for at in orders[color]:
            piece = fold(piece.reshape(2, piece.shape[0] // 2, columns), "krow", at)
        pieces.append(piece)
    both = jnp.stack(pieces)
    for at in range(bits_of("dp")):
        both = both + swap(both, "dp", 1 << at)
    gathered = []
    for color in range(2):
        piece = both[color]
        for at in reversed(orders[color]):
            piece = unfold(piece, "krow", at).reshape(-1, columns)
        gathered.append(piece)
    half = jnp.stack(gathered).reshape(rows // 2, columns)
    return unfold(half, "krow", 0).reshape(rows, columns)


def sum_krow(part):
    size = lax.axis_size("krow")
    pairs = size // 2
    rows, columns = part.shape
    mine, place = bit("krow", 0), lax.axis_index("krow") >> 1
    parts = part.reshape(2, pairs, rows // size, columns)
    half = pick(parts, mine) + swap(pick(parts, 1 - mine).astype(LOW), "krow", 1).astype(
        jnp.float32
    )
    total = pick(half, place)
    for other in range(1, pairs):
        total = total + swap(pick(half, place ^ other).astype(LOW), "krow", 2 * other).astype(
            jnp.float32
        )
    total = total.astype(LOW)
    everyone = jnp.stack([total] + [swap(total, "krow", 2 * other) for other in range(1, pairs)])
    half = jnp.stack([pick(everyone, place ^ at) for at in range(pairs)])
    return unfold(half, "krow", 0).reshape(rows, columns)


def sum_small(value):
    for axis in ("krow", "dp"):
        for at in range(bits_of(axis)):
            value = value + swap(value, axis, 1 << at)
    return value


def normalize(values, scale_vec, shift_vec):
    centred = values - jnp.mean(values, axis=-1, keepdims=True)
    spread = jnp.mean(centred * centred, axis=-1, keepdims=True)
    return centred * lax.rsqrt(spread + EPSILON) * scale_vec + shift_vec


def activate(hidden):
    return jax.nn.gelu(hidden, approximate=False)


def product(left_side, right_side):
    return jnp.dot(left_side, right_side, preferred_element_type=jnp.float32)


def product_back(grad_rows, weight):
    return lax.dot_general(
        grad_rows,
        weight,
        (((grad_rows.ndim - 1,), (1,)), ((), ())),
        preferred_element_type=jnp.float32,
    )


def contract_rows(left_side, right_side):
    left_flat = left_side.reshape(-1, left_side.shape[-1])
    right_flat = right_side.reshape(-1, right_side.shape[-1])
    return lax.dot_general(
        left_flat, right_flat, (((0,), (0,)), ((), ())), preferred_element_type=jnp.float32
    ).astype(LOW)


def heads(matrix):
    return matrix.reshape(matrix.shape[0], matrix.shape[1], HEADS, HEAD_DIM)


def einsum(text, left_side, right_side):
    return jnp.einsum(text, left_side, right_side, preferred_element_type=jnp.float32)


def local(
    tokens,
    lengths,
    attn_gain,
    attn_bias,
    query_weight,
    key_weight,
    value_weight,
    out_weight,
    compress,
    ffn_gain,
    ffn_bias,
    up_weight,
    down_weight,
    cotangent,
):
    seqs, span, _ = tokens.shape
    ring = lax.axis_size("krow")
    rows = compress.shape[0] * ring
    columns = lax.all_to_all(
        compress.reshape(compress.shape[0], ring, span), "krow", 1, 0, tiled=False
    ).reshape(rows, span)
    positions = lax.axis_index("krow") * span + jnp.arange(span, dtype=jnp.int32)
    valid = positions[None, :] < lengths[:, None]
    masked = columns[None] * valid.astype(LOW)[:, None, :]
    inputs = tokens.astype(jnp.float32)
    normed, normed_back = jax.vjp(normalize, inputs, attn_gain, attn_bias)
    normed_low = normed.astype(LOW)
    summary_part = einsum("sjt,std->sjd", masked, normed_low)
    summary = sum_krow(summary_part.reshape(seqs * rows, D)).reshape(seqs, rows, D)
    queries = product(normed_low, query_weight).astype(LOW)
    key_rows = product(summary, key_weight).astype(LOW)
    value_rows = product(summary, value_weight).astype(LOW)
    scores = einsum("sthd,sjhd->shjt", heads(queries), heads(key_rows)) * SCALE
    attn_probs = jax.nn.softmax(scores, axis=2)
    probs_low = attn_probs.astype(LOW)
    mixed_low = einsum("shjt,sjhd->sthd", probs_low, heads(value_rows)).reshape(
        seqs, span, D
    ).astype(LOW)
    attended = inputs + product(mixed_low, out_weight)
    lifted, lifted_back = jax.vjp(normalize, attended, ffn_gain, ffn_bias)
    lifted_low = lifted.astype(LOW)
    active, active_back = jax.vjp(activate, product(lifted_low, up_weight))
    active_low = active.astype(LOW)
    block_out = (attended + product(active_low, down_weight)).astype(LOW)
    down_grad = sum_everywhere(contract_rows(active_low, cotangent))
    (grad_hidden,) = active_back(product_back(cotangent, down_weight))
    grad_hidden = grad_hidden.astype(LOW)
    up_grad = sum_everywhere(contract_rows(lifted_low, grad_hidden))
    lifted_input_grad, ffn_gain_grad, ffn_bias_grad = lifted_back(
        product_back(grad_hidden, up_weight)
    )
    grad_attended = cotangent.astype(jnp.float32) + lifted_input_grad
    grad_branch = grad_attended.astype(LOW)
    out_grad = contract_rows(mixed_low, grad_branch)
    grad_mixed = product_back(grad_branch, out_weight).astype(LOW)
    grad_probs = einsum("sthd,sjhd->shjt", heads(grad_mixed), heads(value_rows))
    row_dot = jnp.sum(attn_probs * grad_probs, axis=2, keepdims=True)
    grad_scores = (attn_probs * (grad_probs - row_dot)).astype(LOW)
    grad_values = einsum("shjt,sthd->sjhd", probs_low, heads(grad_mixed)).reshape(seqs, rows, D)
    grad_values = grad_values.astype(LOW)
    grad_keys = einsum("shjt,sthd->sjhd", grad_scores, heads(queries)) * SCALE
    grad_keys = grad_keys.reshape(seqs, rows, D).astype(LOW)
    grad_queries = einsum("shjt,sjhd->sthd", grad_scores, heads(key_rows)) * SCALE
    grad_queries = grad_queries.reshape(seqs, span, D).astype(LOW)
    grad_summary = product_back(grad_keys, key_weight) + product_back(grad_values, value_weight)
    grad_summary = sum_krow(grad_summary.reshape(seqs * rows, D)).reshape(seqs, rows, D)
    attn_grads = sum_everywhere(
        jnp.concatenate(
            [
                contract_rows(normed_low, grad_queries),
                contract_rows(summary, grad_keys),
                contract_rows(summary, grad_values),
                out_grad,
            ]
        )
    )
    compress_terms = einsum("sjd,std->sjt", grad_summary, normed_low)
    compress_part = jnp.sum(compress_terms * valid.astype(jnp.float32)[:, None, :], axis=0)
    compress_grad = lax.all_to_all(
        compress_part.astype(LOW).reshape(ring, rows // ring, span), "krow", 0, 1, tiled=False
    ).reshape(rows // ring, ring * span)
    for at in range(bits_of("dp")):
        compress_grad = compress_grad + swap(compress_grad, "dp", 1 << at)
    grad_normed = product_back(grad_queries, query_weight) + einsum(
        "sjt,sjd->std", masked, grad_summary
    )
    normed_input_grad, attn_gain_grad, attn_bias_grad = normed_back(grad_normed)
    tokens_grad = (grad_attended + normed_input_grad).astype(LOW)
    norms = sum_small(jnp.stack([attn_gain_grad, attn_bias_grad, ffn_gain_grad, ffn_bias_grad]))
    down_grad, up_grad, attn_grads = (
        g.astype(jnp.float32) for g in (down_grad, up_grad.reshape(D, FF), attn_grads)
    )
    grad_norm = jnp.sqrt(
        sum(jnp.sum(member * member) for member in (down_grad, up_grad, attn_grads, norms))
    )
    attn_grads = attn_grads.reshape(4, D, D)
    return (
        block_out,
        tokens_grad,
        norms[0],
        norms[1],
        attn_grads[0],
        attn_grads[1],
        attn_grads[2],
        attn_grads[3],
        compress_grad.astype(jnp.float32),
        norms[2],
        norms[3],
        up_grad,
        down_grad,
        grad_norm,
    )


def solution(mesh):
    rows, held = P("dp", "krow", None), P("krow", None)
    in_specs = (rows, P("dp"), P(), P(), P(), P(), P(), P(), held, P(), P(), P(), P(), rows)
    out_specs = (rows, rows, P(), P(), P(), P(), P(), P(), held, P(), P(), P(), P(), P())
    return jax.shard_map(local, mesh=mesh, in_specs=in_specs, out_specs=out_specs, check_vma=False)
```

```python
import functools

import jax
import jax.numpy as jnp
from jax import lax
from jax.experimental import pallas as pl
from jax.experimental.pallas import tpu as pltpu
from jax.sharding import PartitionSpec as P

HEAD_DIM = 64
QUAD = 256
EPSILON = 1e-05
SCALE = HEAD_DIM ** (-0.5)
LOW = jnp.bfloat16
F32 = jnp.float32


def dot(left_side, right_side, contract):
    return lax.dot_general(
        left_side, right_side, (contract, ((), ())), preferred_element_type=F32
    )


def nn(left_side, right_side):
    return dot(left_side, right_side, ((1,), (0,)))


def nt(left_side, right_side):
    return dot(left_side, right_side, ((1,), (1,)))


def shape(dims, kind=LOW):
    return jax.ShapeDtypeStruct(dims, kind)


def whole(*dims):
    return pl.BlockSpec(dims, lambda *_: (0,) * len(dims))


def per_seq(*dims):
    return pl.BlockSpec((None, *dims), lambda s, *_: (s, *(0,) * len(dims)))


def call(body, grid, ins, outs, out_specs, in_specs, scratch=(), scalars=0, flops=0):
    made = outs if isinstance(outs, list) else [outs]
    moved = sum(x.size * x.dtype.itemsize for x in (*ins, *made))
    return pl.pallas_call(
        body,
        grid_spec=pltpu.PrefetchScalarGridSpec(
            num_scalar_prefetch=scalars,
            grid=grid,
            in_specs=in_specs,
            out_specs=out_specs,
            scratch_shapes=scratch,
        ),
        out_shape=outs,
        compiler_params=pltpu.CompilerParams(vmem_limit_bytes=56 << 20),
        cost_estimate=pl.CostEstimate(flops=flops, bytes_accessed=moved, transcendentals=0),
    )(*ins)


def centre(values):
    centred = values - jnp.mean(values, axis=-1, keepdims=True)
    spread = jnp.mean(centred * centred, axis=-1, keepdims=True)
    inverse = lax.rsqrt(spread + EPSILON)
    return centred * inverse, inverse


def normalize_back(grad, unit, inverse, gain):
    scaled = grad * gain
    return inverse * (
        scaled
        - jnp.mean(scaled, axis=-1, keepdims=True)
        - unit * jnp.mean(scaled * unit, axis=-1, keepdims=True)
    )


def enter_body(tokens, gain, bias, weight, normed, queries):
    unit, _ = centre(tokens[...].astype(F32))
    low = (unit * gain[...] + bias[...]).astype(LOW)
    normed[...] = low
    queries[...] = (nn(low, weight[...]) * SCALE).astype(LOW)


def enter(tokens, gain, bias, weight):
    seqs, span, width = tokens.shape
    block = per_seq(span, width)
    return call(
        enter_body,
        (seqs,),
        (tokens, gain, bias, weight),
        [shape(tokens.shape)] * 2,
        [block] * 2,
        [block, whole(1, width), whole(1, width), whole(width, width)],
        flops=2 * seqs * span * width * width,
    )


def summarize_body(meta, columns, normed, out):
    seq = pl.program_id(0)
    rows, span = columns.shape
    at = meta[0] + lax.broadcasted_iota(jnp.int32, (rows, span), 1)
    masked = jnp.where(at < meta[1 + seq], columns[...].astype(F32), 0.0).astype(LOW)
    out[...] = nn(masked, normed[...]).astype(LOW)


def summarize(meta, columns, normed):
    seqs, span, width = normed.shape
    rows = columns.shape[0]
    return call(
        summarize_body,
        (seqs,),
        (meta, columns, normed),
        shape((seqs, rows, width)),
        per_seq(rows, width),
        [whole(rows, span), per_seq(span, width)],
        scalars=1,
        flops=2 * seqs * span * rows * width,
    )


def head_masks(dims, axis):
    lane = lax.broadcasted_iota(jnp.int32, dims, axis) // HEAD_DIM
    return [lane == h for h in range(QUAD // HEAD_DIM)]


def stack_heads(value, masks, axis):
    wide = value.astype(F32)
    return jnp.concatenate([jnp.where(m, wide, 0.0).astype(LOW) for m in masks], axis=axis)


def own_heads(stacked, masks, rows):
    parts = [stacked[h * rows : (h + 1) * rows] for h in range(len(masks))]
    out = jnp.where(masks[0], parts[0], 0.0)
    for mask, part in zip(masks[1:], parts[1:]):
        out = jnp.where(mask, part, out)
    return out


def attend_body(
    tokens, queries, summary, key_w, value_w, out_w, gain, bias,
    keys, values, probs, mixed, attended, lifted, inverse_out,
):
    span, width = tokens.shape
    rows = summary.shape[0]
    key_all = nn(summary[...], key_w[...]).astype(LOW)
    value_all = nn(summary[...], value_w[...]).astype(LOW)
    keys[...] = key_all
    values[...] = value_all
    side = head_masks((rows, QUAD), 1)
    turned = head_masks((QUAD, rows), 0)
    quads = []
    for q in range(width // QUAD):
        cut = slice(q * QUAD, (q + 1) * QUAD)
        scores = nt(stack_heads(key_all[:, cut], side, 0), queries[:, cut])
        lows = []
        for h in range(len(side)):
            part = scores[h * rows : (h + 1) * rows]
            grown = jnp.exp(part - jnp.max(part, axis=0, keepdims=True))
            lows.append((grown / jnp.sum(grown, axis=0, keepdims=True)).astype(LOW))
        low = jnp.concatenate(lows, axis=0)
        probs[q * low.shape[0] : (q + 1) * low.shape[0], :] = low
        quads.append(nn(stack_heads(value_all[:, cut].astype(F32).T, turned, 1), low).T)
    mixed_low = jnp.concatenate(quads, axis=1).astype(LOW)
    mixed[...] = mixed_low
    total = tokens[...].astype(F32) + nn(mixed_low, out_w[...])
    attended[...] = total
    unit, inverse = centre(total)
    inverse_out[...] = jnp.broadcast_to(inverse, inverse_out.shape)
    lifted[...] = (unit * gain[...] + bias[...]).astype(LOW)


def attend(tokens, queries, summary, key_w, value_w, out_w, gain, bias):
    seqs, span, width = tokens.shape
    rows = summary.shape[1]
    tall = (width // HEAD_DIM) * rows
    weight = whole(width, width)
    return call(
        attend_body,
        (seqs,),
        (tokens, queries, summary, key_w, value_w, out_w, gain, bias),
        [
            shape((seqs, rows, width)),
            shape((seqs, rows, width)),
            shape((seqs, tall, span)),
            shape((seqs, span, width)),
            shape((seqs, span, width), F32),
            shape((seqs, span, width)),
            shape((seqs, span, 128), F32),
        ],
        [
            per_seq(rows, width),
            per_seq(rows, width),
            per_seq(tall, span),
            per_seq(span, width),
            per_seq(span, width),
            per_seq(span, width),
            per_seq(span, 128),
        ],
        [
            per_seq(span, width),
            per_seq(span, width),
            per_seq(rows, width),
            weight,
            weight,
            weight,
            whole(1, width),
            whole(1, width),
        ],
        flops=2 * seqs * (2 * rows + span) * width * width + 16 * seqs * tall * span * QUAD // 4,
    )


def feed_body(first, lifted, cotangent, up, down, base, *refs):
    if first:
        down_grad, up_grad, back, out, turned = refs
    else:
        back_in, down_grad, up_grad, back, out, turned = refs

    @pl.when(pl.program_id(0) == 0)
    def _():
        turned[...] = lifted[...].T
        out[...] = base[...]
        back[...] = jnp.zeros_like(back) if first else back_in[...]

    hidden = nn(lifted[...], up[...])
    grad_active = nt(cotangent[...], down[...])
    share = 0.5 * (1.0 + lax.erf(hidden * 0.5**0.5))
    slope = share + hidden * jnp.exp(-0.5 * hidden * hidden) * 0.3989422804014327
    active = (hidden * share).astype(LOW)
    grad_hidden = (grad_active * slope).astype(LOW)
    down_grad[...] = nn(active.T, cotangent[...]).astype(LOW)
    up_grad[...] = nn(turned[...], grad_hidden).astype(LOW)
    back[...] += nt(grad_hidden, up[...])
    out[...] += nn(active, down[...])


def feed(share, shares, lifted, cotangent, up, down, base, back=None):
    rows, width = lifted.shape
    hidden = up.shape[1] // shares
    steps = hidden // width
    start = share * steps
    first = back is None
    square = whole(rows, width)
    extra = () if first else (back,)
    return call(
        functools.partial(feed_body, first),
        (steps,),
        (lifted, cotangent, up, down, base, *extra),
        [
            shape((hidden, width)),
            shape((steps, width, width)),
            shape((rows, width), F32),
            shape((rows, width), F32),
        ],
        [
            pl.BlockSpec((width, width), lambda i: (i, 0)),
            pl.BlockSpec((None, width, width), lambda i: (i, 0, 0)),
            square,
            square,
        ],
        [
            square,
            square,
            pl.BlockSpec((width, width), lambda i: (0, start + i)),
            pl.BlockSpec((width, width), lambda i: (start + i, 0)),
            square,
            *([square] * len(extra)),
        ],
        [pltpu.VMEM((width, rows), LOW)],
        flops=12 * rows * width * hidden,
    )


def attend_back_body(
    back, cotangent, attended, inverse, gain, queries, keys, values, probs, out_w, key_w, value_w,
    grad_attended, grad_branch, grad_queries, grad_keys, grad_values, grad_summary, norm_grads,
):
    span, width = cotangent.shape
    rows = keys.shape[0]

    @pl.when(pl.program_id(0) == 0)
    def _():
        norm_grads[...] = jnp.zeros_like(norm_grads)

    total = attended[...]
    scale = inverse[:, :1]
    unit = (total - jnp.mean(total, axis=-1, keepdims=True)) * scale
    grad = back[...]
    norm_grads[0:1, :] += jnp.sum(grad * unit, axis=0, keepdims=True)
    norm_grads[1:2, :] += jnp.sum(grad, axis=0, keepdims=True)
    whole_grad = cotangent[...].astype(F32) + normalize_back(grad, unit, scale, gain[...])
    grad_attended[...] = whole_grad
    branch = whole_grad.astype(LOW)
    grad_branch[...] = branch
    grad_mixed = nt(branch, out_w[...]).astype(LOW)
    side = head_masks((rows, QUAD), 1)
    turned = head_masks((QUAD, rows), 0)
    for q in range(width // QUAD):
        cut = slice(q * QUAD, (q + 1) * QUAD)
        mixed_cut = grad_mixed[:, cut]
        tall = len(side) * rows
        low = probs[q * tall : (q + 1) * tall, :]
        grad_probs = nt(stack_heads(values[:, cut], side, 0), mixed_cut)
        lows = []
        for h in range(len(side)):
            part = low[h * rows : (h + 1) * rows].astype(F32)
            ours = grad_probs[h * rows : (h + 1) * rows]
            inner = jnp.sum(part * ours, axis=0, keepdims=True)
            lows.append((part * (ours - inner)).astype(LOW))
        grad_scores = jnp.concatenate(lows, axis=0)
        grad_values[:, cut] = own_heads(nn(low, mixed_cut), side, rows).astype(LOW)
        grad_keys[:, cut] = own_heads(nn(grad_scores, queries[:, cut]), side, rows).astype(LOW)
        keys_turned = stack_heads(keys[:, cut].astype(F32).T, turned, 1)
        grad_queries[:, cut] = (nn(keys_turned, grad_scores) * SCALE).T.astype(LOW)
    grad_summary[...] = (
        nt(grad_keys[...], key_w[...]) + nt(grad_values[...], value_w[...])
    ).astype(LOW)


def attend_back(
    back, cotangent, attended, inverse, gain, queries, keys, values, probs, out_w, key_w, value_w
):
    seqs, span, width = cotangent.shape
    rows = keys.shape[1]
    tall = probs.shape[1]
    weight = whole(width, width)
    block, rows_block = per_seq(span, width), per_seq(rows, width)
    return call(
        attend_back_body,
        (seqs,),
        (
            back, cotangent, attended, inverse, gain, queries, keys, values, probs, out_w, key_w,
            value_w,
        ),
        [
            shape((seqs, span, width), F32),
            shape((seqs, span, width)),
            shape((seqs, span, width)),
            shape((seqs, rows, width)),
            shape((seqs, rows, width)),
            shape((seqs, rows, width)),
            shape((8, width), F32),
        ],
        [block, block, block, rows_block, rows_block, rows_block, whole(8, width)],
        [
            block, block, block, per_seq(span, 128), whole(1, width), block, rows_block, rows_block,
            per_seq(tall, span), weight, weight, weight,
        ],
        flops=2 * seqs * (2 * rows + span) * width * width + 40 * seqs * tall * span * QUAD // 4,
    )


def squares_body(
    normed, summary, mixed, grad_queries, grad_keys, grad_values, grad_branch,
    first, second, normed_t, summary_t, mixed_t,
):
    @pl.when(pl.program_id(0) == 0)
    def _():
        normed_t[...] = normed[...].T
        summary_t[...] = summary[...].T
        mixed_t[...] = mixed[...].T

    first[0] = nn(normed_t[...], grad_queries[...]).astype(LOW)
    first[1] = nn(summary_t[...], grad_keys[...]).astype(LOW)
    second[0] = nn(summary_t[...], grad_values[...]).astype(LOW)
    second[1] = nn(mixed_t[...], grad_branch[...]).astype(LOW)


def squares(normed, summary, mixed, grad_queries, grad_keys, grad_values, grad_branch):
    rows, width = normed.shape
    tall = summary.shape[0]
    cut = QUAD
    return call(
        squares_body,
        (width // cut,),
        (normed, summary, mixed, grad_queries, grad_keys, grad_values, grad_branch),
        [shape((2, width, width))] * 2,
        [pl.BlockSpec((2, width, cut), lambda i: (0, 0, i))] * 2,
        [
            whole(rows, width),
            whole(tall, width),
            whole(rows, width),
            pl.BlockSpec((rows, cut), lambda i: (0, i)),
            pl.BlockSpec((tall, cut), lambda i: (0, i)),
            pl.BlockSpec((tall, cut), lambda i: (0, i)),
            pl.BlockSpec((rows, cut), lambda i: (0, i)),
        ],
        [pltpu.VMEM((width, rows), LOW), pltpu.VMEM((width, tall), LOW), pltpu.VMEM((width, rows), LOW)],
        flops=4 * (rows + tall) * width * width,
    )


def leave_body(
    meta, grad_summary, columns, normed, tokens, gain, grad_queries, query_w, grad_attended,
    tokens_grad, terms, norm_grads, columns_t, terms_sum,
):
    seq = pl.program_id(0)
    rows, span = columns.shape

    @pl.when(seq == 0)
    def _():
        columns_t[...] = columns[...].T
        terms_sum[...] = jnp.zeros_like(terms_sum)
        norm_grads[...] = jnp.zeros_like(norm_grads)

    length = meta[1 + seq] - meta[0]
    lane = lax.broadcasted_iota(jnp.int32, (rows, span), 1) < length
    line = lax.broadcasted_iota(jnp.int32, (span, 1), 0) < length
    summed = grad_summary[...]
    terms_sum[...] += jnp.where(lane, nt(summed, normed[...]), 0.0)
    grad = nt(grad_queries[...], query_w[...]) + jnp.where(line, nn(columns_t[...], summed), 0.0)
    unit, inverse = centre(tokens[...].astype(F32))
    norm_grads[0:1, :] += jnp.sum(grad * unit, axis=0, keepdims=True)
    norm_grads[1:2, :] += jnp.sum(grad, axis=0, keepdims=True)
    tokens_grad[...] = (
        grad_attended[...] + normalize_back(grad, unit, inverse, gain[...])
    ).astype(LOW)

    @pl.when(seq == pl.num_programs(0) - 1)
    def _():
        terms[...] = terms_sum[...].astype(LOW)


def leave(meta, grad_summary, columns, normed, tokens, gain, grad_queries, query_w, grad_attended):
    seqs, span, width = tokens.shape
    rows = columns.shape[0]
    block = per_seq(span, width)
    return call(
        leave_body,
        (seqs,),
        (
            meta, grad_summary, columns, normed, tokens, gain, grad_queries, query_w,
            grad_attended,
        ),
        [shape(tokens.shape), shape((rows, span)), shape((8, width), F32)],
        [block, whole(rows, span), whole(8, width)],
        [
            per_seq(rows, width), whole(rows, span), block, block, whole(1, width), block,
            whole(width, width), block,
        ],
        [pltpu.VMEM((span, rows), LOW), pltpu.VMEM((rows, span), F32)],
        scalars=1,
        flops=2 * seqs * span * width * (width + 2 * rows),
    )


def swap(value, axis, mask):
    size = lax.axis_size(axis)
    return lax.ppermute(value, axis, [(i, i ^ mask) for i in range(size)])


def pick(value, at):
    return lax.dynamic_index_in_dim(value, at, 0, keepdims=False)


def bits_of(axis):
    return (lax.axis_size(axis) - 1).bit_length()


def bit(axis, at):
    return (lax.axis_index(axis) >> at) & 1


def in_order(mine, other, at):
    return jnp.where(at == 0, jnp.stack([mine, other]), jnp.stack([other, mine]))


def fold(value, axis, at):
    mine = bit(axis, at)
    return pick(value, mine) + swap(pick(value, 1 - mine), axis, 1 << at)


def unfold(value, axis, at):
    return in_order(value, swap(value, axis, 1 << at), bit(axis, at))


def sum_everywhere(pair):
    count = bits_of("krow")
    orders = [list(range(1, count)), list(range(count - 1, 0, -1))]
    pieces = []
    for part, order in zip(pair, orders):
        columns = part.shape[-1]
        piece = part.reshape(-1, columns)
        for at in [0, *order]:
            piece = fold(piece.reshape(2, -1, columns), "krow", at)
        pieces.append(piece)
    both = jnp.stack(pieces)
    for at in range(bits_of("dp")):
        both = both + swap(both, "dp", 1 << at)
    out = []
    for piece, part, order in zip(both, pair, orders):
        for at in reversed([0, *order]):
            piece = unfold(piece, "krow", at).reshape(-1, part.shape[-1])
        out.append(piece.reshape(part.shape))
    return out


def sum_krow(part):
    size = lax.axis_size("krow")
    pairs = size // 2
    rows, columns = part.shape
    mine, place = bit("krow", 0), lax.axis_index("krow") >> 1
    parts = part.reshape(2, pairs, rows // size, columns)
    half = pick(parts, mine).astype(F32) + swap(pick(parts, 1 - mine), "krow", 1).astype(F32)
    total = pick(half, place)
    for other in range(1, pairs):
        total = total + swap(pick(half, place ^ other).astype(LOW), "krow", 2 * other).astype(F32)
    total = total.astype(LOW)
    everyone = jnp.stack([total] + [swap(total, "krow", 2 * other) for other in range(1, pairs)])
    half = jnp.stack([pick(everyone, place ^ at) for at in range(pairs)])
    return unfold(half, "krow", 0).reshape(rows, columns)


def sum_small(value):
    for axis in ("krow", "dp"):
        for at in range(bits_of(axis)):
            value = value + swap(value, axis, 1 << at)
    return value


def local(
    tokens,
    lengths,
    attn_gain,
    attn_bias,
    query_weight,
    key_weight,
    value_weight,
    out_weight,
    compress,
    ffn_gain,
    ffn_bias,
    up_weight,
    down_weight,
    cotangent,
):
    seqs, span, width = tokens.shape
    ring = lax.axis_size("krow")
    rows = compress.shape[0] * ring
    attn_gain, attn_bias, ffn_gain, ffn_bias = (
        v.reshape(1, width) for v in (attn_gain, attn_bias, ffn_gain, ffn_bias)
    )
    columns = lax.all_to_all(
        compress.reshape(compress.shape[0], ring, span), "krow", 1, 0, tiled=False
    ).reshape(rows, span)
    offset = lax.axis_index("krow") * span
    meta = jnp.concatenate([offset[None].astype(jnp.int32), lengths])
    normed, queries = enter(tokens, attn_gain, attn_bias, query_weight)
    part = summarize(meta, columns, normed)
    summary = sum_krow(part.reshape(seqs * rows, width)).reshape(seqs, rows, width)
    keys, values, probs, mixed, attended, lifted, inverse = attend(
        tokens, queries, summary, key_weight, value_weight, out_weight, ffn_gain, ffn_bias
    )
    flat = (seqs * span, width)
    lifted_flat, cotangent_flat = lifted.reshape(flat), cotangent.reshape(flat)
    down_1, up_1, back, out = feed(
        0, 2, lifted_flat, cotangent_flat, up_weight, down_weight, attended.reshape(flat)
    )
    down_2, up_2, back, out = feed(
        1, 2, lifted_flat, cotangent_flat, up_weight, down_weight, out, back
    )
    block_out = out.astype(LOW).reshape(tokens.shape)
    grad_attended, grad_branch, grad_queries, grad_keys, grad_values, grad_summary, ffn_norms = (
        attend_back(
            back.reshape(tokens.shape), cotangent, attended, inverse, ffn_gain, queries, keys,
            values, probs, out_weight, key_weight, value_weight,
        )
    )
    tall = (seqs * rows, width)
    first, second = squares(
        normed.reshape(flat), summary.reshape(tall), mixed.reshape(flat),
        grad_queries.reshape(flat), grad_keys.reshape(tall), grad_values.reshape(tall),
        grad_branch.reshape(flat),
    )
    grad_summary = sum_krow(grad_summary.reshape(tall)).reshape(seqs, rows, width)
    tokens_grad, terms, attn_norms = leave(
        meta, grad_summary, columns, normed, tokens, attn_gain, grad_queries, query_weight,
        grad_attended,
    )
    down_1, up_1 = sum_everywhere((down_1, up_1))
    down_2, up_2 = sum_everywhere((down_2, up_2))
    first, second = sum_everywhere((first, second))
    compress_grad = lax.all_to_all(
        terms.reshape(ring, rows // ring, span), "krow", 0, 1, tiled=False
    ).reshape(rows // ring, ring * span)
    for at in range(bits_of("dp")):
        compress_grad = compress_grad + swap(compress_grad, "dp", 1 << at)
    norms = sum_small(jnp.concatenate([attn_norms[:2], ffn_norms[:2]]))
    down_grad = jnp.concatenate([down_1, down_2]).astype(F32)
    up_grad = (
        jnp.concatenate([up_1, up_2]).astype(F32).transpose(1, 0, 2).reshape(up_weight.shape)
    )
    attn_grads = [g.astype(F32) for g in (*first, *second)]
    grad_norm = jnp.sqrt(
        sum(jnp.sum(member * member) for member in (down_grad, up_grad, *attn_grads, norms))
    )
    return (
        block_out,
        tokens_grad,
        norms[0],
        norms[1],
        *attn_grads,
        compress_grad.astype(F32),
        norms[2],
        norms[3],
        up_grad,
        down_grad,
        grad_norm,
    )


def solution(mesh):
    rows, held = P("dp", "krow", None), P("krow", None)
    in_specs = (rows, P("dp"), P(), P(), P(), P(), P(), P(), held, P(), P(), P(), P(), rows)
    out_specs = (rows, rows, P(), P(), P(), P(), P(), P(), held, P(), P(), P(), P(), P())
    return jax.shard_map(local, mesh=mesh, in_specs=in_specs, out_specs=out_specs, check_vma=False)
```

```python
import functools

import jax
import jax.numpy as jnp
from jax import lax
from jax.experimental import pallas as pl
from jax.experimental.pallas import tpu as pltpu
from jax.sharding import PartitionSpec as P

HEAD_DIM = 64
QUAD = 256
EPSILON = 1e-05
SCALE = HEAD_DIM ** (-0.5)
LOW = jnp.bfloat16
F32 = jnp.float32
COST = 10**9


def dot(left_side, right_side, contract):
    return lax.dot_general(
        left_side, right_side, (contract, ((), ())), preferred_element_type=F32
    )


def nn(left_side, right_side):
    return dot(left_side, right_side, ((1,), (0,)))


def nt(left_side, right_side):
    return dot(left_side, right_side, ((1,), (1,)))


def shape(dims, kind=LOW):
    return jax.ShapeDtypeStruct(dims, kind)


def far(dims, kind=LOW):
    return pltpu.HBM(dims, kind)


def kept_far(*values):
    return tuple(pltpu.with_memory_space_constraint(v, pltpu.HBM) for v in values)


def whole(*dims):
    return pl.BlockSpec(dims, lambda *_: (0,) * len(dims), pipeline_mode=pl.Buffered(1))


def result(*dims):
    return pl.BlockSpec(dims, lambda *_: (0,) * len(dims))


def vector(width):
    return pl.BlockSpec((width,), lambda *_: (0,))


def per_seq(*dims):
    return pl.BlockSpec((None, *dims), lambda s, *_: (s, *(0,) * len(dims)))


def call(body, grid, ins, outs, out_specs, in_specs, scratch=(), scalars=0, limit=24, cost=1):
    return pl.pallas_call(
        body,
        grid_spec=pltpu.PrefetchScalarGridSpec(
            num_scalar_prefetch=scalars,
            grid=grid,
            in_specs=in_specs,
            out_specs=out_specs,
            scratch_shapes=scratch,
        ),
        out_shape=outs,
        compiler_params=pltpu.CompilerParams(vmem_limit_bytes=limit << 20),
        cost_estimate=pl.CostEstimate(flops=cost * COST, bytes_accessed=1, transcendentals=0),
    )(*ins)


def row(ref):
    return ref[...].reshape(1, -1)


def centre(values):
    centred = values - jnp.mean(values, axis=-1, keepdims=True)
    spread = jnp.mean(centred * centred, axis=-1, keepdims=True)
    inverse = lax.rsqrt(spread + EPSILON)
    return centred * inverse, inverse


def normalize_back(grad, unit, inverse, gain):
    scaled = grad * gain
    return inverse * (
        scaled
        - jnp.mean(scaled, axis=-1, keepdims=True)
        - unit * jnp.mean(scaled * unit, axis=-1, keepdims=True)
    )


def enter_body(tokens, gain, bias, normed):
    unit, _ = centre(tokens[...].astype(F32))
    normed[...] = (unit * row(gain) + row(bias)).astype(LOW)


def enter(tokens, gain, bias):
    seqs, span, width = tokens.shape
    block = per_seq(span, width)
    return call(
        enter_body,
        (seqs,),
        (tokens, gain, bias),
        far(tokens.shape),
        block,
        [block, vector(width), vector(width)],
        limit=10,
        cost=1,
    )


def project_body(normed, weight, queries):
    queries[...] = (nn(normed[...], weight[...]) * SCALE).astype(LOW)


def project(normed, weight):
    seqs, span, width = normed.shape
    block = per_seq(span, width)
    return call(
        project_body,
        (seqs,),
        (normed, weight),
        far(normed.shape),
        block,
        [block, whole(width, width)],
        limit=10,
        cost=1,
    )


def grad_active_body(cotangent, down, out):
    out[...] = nt(cotangent[...], down[...]).astype(LOW)


def grad_active_of(cotangent, down):
    rows, width = cotangent.shape
    hidden = down.shape[0]
    cut = QUAD * 2
    return call(
        grad_active_body,
        (hidden // cut,),
        (cotangent, down),
        far((rows, hidden)),
        pl.BlockSpec((rows, cut), lambda i: (0, i)),
        [whole(rows, width), pl.BlockSpec((cut, width), lambda i: (i, 0))],
        limit=14,
        cost=5,
    )


def block_at(step, order):
    return step - step % 2 + (order[0] ^ 1 ^ (step % 2))


def block_out_body(order, down, attended, *refs):
    *actives, out = refs
    width = attended.shape[1]
    total = attended[...]
    for at, active in enumerate(actives):
        start = pl.multiple_of(block_at(at, order) * width, width)
        total += nn(active[...], down[pl.ds(start, width), :])
    out[...] = total.astype(LOW)


def block_out_of(order, down, attended, *actives):
    seqs, span, width = attended.shape
    lines = pl.BlockSpec((span, width), lambda s, m: (s, 0))
    return call(
        block_out_body,
        (seqs,),
        (order, down, *kept_far(attended, *actives)),
        shape(attended.shape),
        per_seq(span, width),
        [whole(*down.shape), per_seq(span, width), *([lines] * len(actives))],
        scalars=1,
        limit=24,
        cost=6,
    )


def send_by_distance(me, value, held, kept, sent):
    pieces = 2 * kept.shape[0]
    cut = value.shape[0] // pieces
    held[...] = value
    for pair in range(pieces // 2):
        for other, out in enumerate((kept, sent)):
            start = pl.multiple_of(((2 * pair + other) ^ me) * cut, cut)
            out[pair] = held[pl.ds(start, cut), :].astype(LOW)


def take_by_distance(me, own, other, out):
    pieces = 2 * own.shape[0]
    cut = own.shape[1]
    for pair in range(pieces // 2):
        for at, source in enumerate((own, other)):
            start = pl.multiple_of(((2 * pair + at) ^ me) * cut, cut)
            out[pl.ds(start, cut), :] = source[pair]


def distance_rows(pairs, seqs, rows, width):
    return shape((pairs, seqs, rows // pairs // 2, width))


def distance_spec(pairs, rows, width):
    return pl.BlockSpec((pairs, None, rows // pairs // 2, width), lambda s, *_: (0, s, 0, 0))


def summarize_body(meta, columns, normed, kept, sent, held):
    seq = pl.program_id(0)
    rows, span = columns.shape
    at = meta[0] * span + lax.broadcasted_iota(jnp.int32, (rows, span), 1)
    masked = jnp.where(at < meta[1 + seq], columns[...].astype(F32), 0.0).astype(LOW)
    send_by_distance(meta[0], nn(masked, normed[...]), held, kept, sent)


def summarize(pairs, meta, columns, normed):
    seqs, span, width = normed.shape
    rows = columns.shape[0]
    return call(
        summarize_body,
        (seqs,),
        (meta, columns, normed),
        [distance_rows(pairs, seqs, rows, width)] * 2,
        [distance_spec(pairs, rows, width)] * 2,
        [whole(rows, span), per_seq(span, width)],
        [pltpu.VMEM((rows, width), F32)],
        scalars=1,
        limit=12,
        cost=2,
    )


def head_masks(dims, axis):
    lane = lax.broadcasted_iota(jnp.int32, dims, axis) // HEAD_DIM
    return [lane == h for h in range(QUAD // HEAD_DIM)]


def stack_heads(value, masks, axis):
    wide = value.astype(F32)
    return jnp.concatenate([jnp.where(m, wide, 0.0).astype(LOW) for m in masks], axis=axis)


def own_heads(stacked, masks, rows):
    parts = [stacked[h * rows : (h + 1) * rows] for h in range(len(masks))]
    out = jnp.where(masks[0], parts[0], 0.0)
    for mask, part in zip(masks[1:], parts[1:]):
        out = jnp.where(mask, part, out)
    return out


def attend_body(
    meta, tokens, queries, own, other, key_w, value_w, out_w, gain, bias,
    summary, keys, values, probs, mixed, attended, lifted, inverse_out,
):
    span, width = tokens.shape
    rows = summary.shape[0]
    take_by_distance(meta[0], own, other, summary)
    key_all = nn(summary[...], key_w[...]).astype(LOW)
    value_all = nn(summary[...], value_w[...]).astype(LOW)
    keys[...] = key_all
    values[...] = value_all
    side = head_masks((rows, QUAD), 1)
    turned = head_masks((QUAD, rows), 0)
    quads = []
    for q in range(width // QUAD):
        cut = slice(q * QUAD, (q + 1) * QUAD)
        scores = nt(stack_heads(key_all[:, cut], side, 0), queries[:, cut])
        lows = []
        for h in range(len(side)):
            part = scores[h * rows : (h + 1) * rows]
            grown = jnp.exp(part - jnp.max(part, axis=0, keepdims=True))
            lows.append((grown / jnp.sum(grown, axis=0, keepdims=True)).astype(LOW))
        low = jnp.concatenate(lows, axis=0)
        probs[q * low.shape[0] : (q + 1) * low.shape[0], :] = low
        quads.append(nn(stack_heads(value_all[:, cut].astype(F32).T, turned, 1), low).T)
    mixed_low = jnp.concatenate(quads, axis=1).astype(LOW)
    mixed[...] = mixed_low
    total = tokens[...].astype(F32) + nn(mixed_low, out_w[...])
    attended[...] = total
    unit, inverse = centre(total)
    inverse_out[...] = jnp.broadcast_to(inverse, inverse_out.shape)
    lifted[...] = (unit * row(gain) + row(bias)).astype(LOW)


def attend(meta, tokens, queries, own, other, key_w, value_w, out_w, gain, bias):
    seqs, span, width = tokens.shape
    pairs = own.shape[0]
    rows = 2 * pairs * own.shape[2]
    tall = (width // HEAD_DIM) * rows
    weight = whole(width, width)
    return call(
        attend_body,
        (seqs,),
        (meta, *kept_far(tokens, queries), own, other, key_w, value_w, out_w, gain, bias),
        [
            far((seqs, rows, width)),
            far((seqs, rows, width)),
            far((seqs, rows, width)),
            far((seqs, tall, span)),
            far((seqs, span, width)),
            far((seqs, span, width), F32),
            shape((seqs, span, width)),
            far((seqs, span, 128), F32),
        ],
        [
            per_seq(rows, width),
            per_seq(rows, width),
            per_seq(rows, width),
            per_seq(tall, span),
            per_seq(span, width),
            per_seq(span, width),
            per_seq(span, width),
            per_seq(span, 128),
        ],
        [
            per_seq(span, width),
            per_seq(span, width),
            distance_spec(pairs, rows, width),
            distance_spec(pairs, rows, width),
            weight,
            weight,
            weight,
            vector(width),
            vector(width),
        ],
        scalars=1,
        limit=32,
        cost=10,
    )


def feed_step(order, lifted, cotangent, grad_active, up, turned, outs):
    active_out, grad_out, down_grad, up_grad = outs
    hidden = nn(lifted[...], up[...])
    share = 0.5 * (1.0 + lax.erf(hidden * 0.5**0.5))
    slope = share + hidden * jnp.exp(-0.5 * hidden * hidden) * 0.3989422804014327
    active = (hidden * share).astype(LOW)
    grad_hidden = (grad_active[...].astype(F32) * slope).astype(LOW)
    active_out[...] = active
    grad_out[...] = grad_hidden
    pieces, line = down_grad.shape[0], down_grad.shape[1]
    value = nn(active.T, cotangent[...])
    for piece in range(pieces):
        down_grad[piece ^ order[1]] = value[piece * line : (piece + 1) * line].astype(LOW)
    value = nn(turned[...], grad_hidden)
    line = up_grad.shape[1]
    for piece in range(pieces):
        up_grad[piece ^ order[2]] = value[piece * line : (piece + 1) * line].astype(LOW)


def feed_body(steps, order, lifted, cotangent, grad_active, up, *refs):
    *outs, turned = refs
    step = pl.program_id(0)

    @pl.when(step == 0)
    def _():
        turned[...] = lifted[...].T

    for at in range(len(outs) // 4):
        pl.when(step // steps == at)(
            functools.partial(
                feed_step, order, lifted, cotangent, grad_active, up, turned, outs[4 * at : 4 * at + 4]
            )
        )


def feed(first, blocks, pieces, order, lifted, cotangent, grad_active, up):
    rows, width = lifted.shape
    steps = width // QUAD

    def columns(i, m):
        return (0, block_at(first + i // steps, m) * steps + i % steps)

    def held(at, i):
        return jnp.clip(i - at * steps, 0, steps - 1)

    out_specs = []
    for at in range(blocks):
        out_specs += [
            pl.BlockSpec((rows, QUAD), lambda i, m, at=at: (0, held(at, i))),
            pl.BlockSpec((rows, QUAD), lambda i, m, at=at: (0, held(at, i))),
            pl.BlockSpec(
                (pieces, None, QUAD // pieces, width), lambda i, m, at=at: (0, held(at, i), 0, 0)
            ),
            pl.BlockSpec((pieces, width // pieces, QUAD), lambda i, m, at=at: (0, 0, held(at, i))),
        ]
    return call(
        functools.partial(feed_body, steps),
        (blocks * steps,),
        (order, lifted, cotangent, grad_active, up),
        [
            far((rows, width)),
            far((rows, width)),
            shape((pieces, steps, QUAD // pieces, width)),
            shape((pieces, width // pieces, width)),
        ]
        * blocks,
        out_specs,
        [
            whole(rows, width),
            whole(rows, width),
            pl.BlockSpec((rows, QUAD), columns),
            pl.BlockSpec((width, QUAD), columns),
        ],
        [pltpu.VMEM((width, rows), LOW)],
        scalars=1,
        limit=20,
        cost=6 * blocks,
    )


def feed_back_body(
    order, hidden_1, hidden_2, hidden_3, hidden_4, up, cotangent, attended, inverse, gain, out_w,
    grad_attended, grad_branch, grad_mixed, norm_grads,
):
    width = cotangent.shape[1]

    @pl.when(pl.program_id(0) == 0)
    def _():
        norm_grads[...] = jnp.zeros_like(norm_grads)

    total = attended[...]
    scale = inverse[:, :1]
    unit = (total - jnp.mean(total, axis=-1, keepdims=True)) * scale
    grad = 0.0
    for at, hidden in enumerate((hidden_1, hidden_2, hidden_3, hidden_4)):
        start = pl.multiple_of(block_at(at, order) * width, width)
        grad += nt(hidden[...], up[:, pl.ds(start, width)])
    norm_grads[0:1, :] += jnp.sum(grad * unit, axis=0, keepdims=True)
    norm_grads[1:2, :] += jnp.sum(grad, axis=0, keepdims=True)
    whole_grad = cotangent[...].astype(F32) + normalize_back(grad, unit, scale, row(gain))
    grad_attended[...] = whole_grad
    branch = whole_grad.astype(LOW)
    grad_branch[...] = branch
    grad_mixed[...] = nt(branch, out_w[...]).astype(LOW)


def feed_back(order, hiddens, up, cotangent, attended, inverse, gain, out_w):
    seqs, span, width = cotangent.shape
    block = per_seq(span, width)
    lines = pl.BlockSpec((span, width), lambda s, *_: (s, 0))
    return call(
        feed_back_body,
        (seqs,),
        (
            order, *kept_far(*hiddens), up, *kept_far(cotangent, attended, inverse), gain, out_w,
        ),
        [
            far((seqs, span, width), F32),
            far((seqs, span, width)),
            far((seqs, span, width)),
            shape((8, width), F32),
        ],
        [block, block, block, result(8, width)],
        [
            *([lines] * len(hiddens)), whole(*up.shape), block, block, per_seq(span, 128),
            vector(width), whole(width, width),
        ],
        scalars=1,
        limit=24,
        cost=8,
    )


def attend_back_body(
    meta, grad_mixed, queries, keys, values, probs, key_w, value_w,
    grad_queries, grad_keys, grad_values, kept, sent, held,
):
    span, width = grad_mixed.shape
    rows = keys.shape[0]
    side = head_masks((rows, QUAD), 1)
    turned = head_masks((QUAD, rows), 0)
    for q in range(width // QUAD):
        cut = slice(q * QUAD, (q + 1) * QUAD)
        mixed_cut = grad_mixed[:, cut]
        tall = len(side) * rows
        low = probs[q * tall : (q + 1) * tall, :]
        grad_probs = nt(stack_heads(values[:, cut], side, 0), mixed_cut)
        lows = []
        for h in range(len(side)):
            part = low[h * rows : (h + 1) * rows].astype(F32)
            ours = grad_probs[h * rows : (h + 1) * rows]
            inner = jnp.sum(part * ours, axis=0, keepdims=True)
            lows.append((part * (ours - inner)).astype(LOW))
        grad_scores = jnp.concatenate(lows, axis=0)
        grad_values[:, cut] = own_heads(nn(low, mixed_cut), side, rows).astype(LOW)
        grad_keys[:, cut] = own_heads(nn(grad_scores, queries[:, cut]), side, rows).astype(LOW)
        keys_turned = stack_heads(keys[:, cut].astype(F32).T, turned, 1)
        grad_queries[:, cut] = (nn(keys_turned, grad_scores) * SCALE).T.astype(LOW)
    grad_summary = nt(grad_keys[...], key_w[...]) + nt(grad_values[...], value_w[...])
    send_by_distance(meta[0], grad_summary, held, kept, sent)


def attend_back(pairs, meta, grad_mixed, queries, keys, values, probs, key_w, value_w):
    seqs, span, width = grad_mixed.shape
    rows = keys.shape[1]
    tall = probs.shape[1]
    weight = whole(width, width)
    block, rows_block = per_seq(span, width), per_seq(rows, width)
    distance = distance_spec(pairs, rows, width)
    return call(
        attend_back_body,
        (seqs,),
        (meta, *kept_far(grad_mixed, queries, keys, values, probs), key_w, value_w),
        [
            far((seqs, span, width)),
            far((seqs, rows, width)),
            far((seqs, rows, width)),
            distance_rows(pairs, seqs, rows, width),
            distance_rows(pairs, seqs, rows, width),
        ],
        [block, rows_block, rows_block, distance, distance],
        [block, block, rows_block, rows_block, per_seq(tall, span), weight, weight],
        [pltpu.VMEM((rows, width), F32)],
        scalars=1,
        limit=24,
        cost=14,
    )


def squares_body(
    order, normed, summary, mixed, grad_queries, grad_keys, grad_values, grad_branch,
    sent_1, sent_2, kept_1, kept_2, normed_t, summary_t, mixed_t,
):
    @pl.when(pl.program_id(0) == 0)
    def _():
        normed_t[...] = normed[...].T
        summary_t[...] = summary[...].T
        mixed_t[...] = mixed[...].T

    pieces = sent_1.shape[0]
    half = normed_t.shape[0] // 2
    members = (
        (normed_t, grad_queries, (sent_1, kept_1), 0, order[1]),
        (summary_t, grad_keys, (sent_1, kept_1), 1, order[1]),
        (summary_t, grad_values, (sent_2, kept_2), 0, order[2]),
        (mixed_t, grad_branch, (sent_2, kept_2), 1, order[2]),
    )
    for left, right, outs, at, mask in members:
        for out, side in zip(outs, (1 - order[0], order[0])):
            start = pl.multiple_of(side * half, half)
            value = nn(left[pl.ds(start, half), :], right[...])
            cut = half // pieces
            for piece in range(pieces):
                out[piece ^ mask, at] = value[piece * cut : (piece + 1) * cut].astype(LOW)


def squares(
    pieces, order, normed, summary, mixed, grad_queries, grad_keys, grad_values, grad_branch
):
    rows, width = normed.shape
    tall = summary.shape[0]
    cut = QUAD
    line = width // 2 // pieces
    return call(
        squares_body,
        (width // cut,),
        (
            order, normed, summary, mixed,
            *kept_far(grad_queries, grad_keys, grad_values, grad_branch),
        ),
        [shape((pieces, 2, line, width))] * 4,
        [pl.BlockSpec((pieces, 2, line, cut), lambda i, m: (0, 0, 0, i))] * 4,
        [
            whole(rows, width),
            whole(tall, width),
            whole(rows, width),
            pl.BlockSpec((rows, cut), lambda i, m: (0, i)),
            pl.BlockSpec((tall, cut), lambda i, m: (0, i)),
            pl.BlockSpec((tall, cut), lambda i, m: (0, i)),
            pl.BlockSpec((rows, cut), lambda i, m: (0, i)),
        ],
        [
            pltpu.VMEM((width, rows), LOW),
            pltpu.VMEM((width, tall), LOW),
            pltpu.VMEM((width, rows), LOW),
        ],
        scalars=1,
        limit=24,
        cost=7,
    )


def place_feed_body(order, *refs):
    inputs, (down, up, total) = refs[:8], refs[8:]
    share, side = pl.program_id(0), pl.program_id(1)
    ours = (side ^ order[0]) == 0

    @pl.when((share == 0) & (side == 0))
    def _():
        total[...] = jnp.zeros_like(total)

    def place(down_in, up_in):
        pieces, steps, line, _ = down_in.shape
        tall = up_in.shape[1]

        def one(piece, square):
            for step in range(steps):
                value = down_in[piece ^ order[1], step].astype(F32)
                start = pl.multiple_of(step * pieces * line + piece * line, line)
                down[pl.ds(start, line), :] = value
                square += jnp.sum(value * value, axis=0, keepdims=True)
            value = up_in[piece ^ order[2]].astype(F32)
            up[pl.ds(pl.multiple_of(piece * tall, tall), tall), :] = value
            return square + jnp.sum(value * value, axis=0, keepdims=True)

        total[0:1, :] += lax.fori_loop(0, pieces, one, jnp.zeros((1, down.shape[1]), F32))

    for at in range(4):
        chosen = (share == at // 2) & (ours if at % 2 == 0 else jnp.logical_not(ours))
        pl.when(chosen)(
            functools.partial(place, inputs[4 * (at // 2) + at % 2], inputs[4 * (at // 2) + 2 + at % 2])
        )


def place_feed(order, down_shape, up_shape, *arrays):
    width = down_shape[1]
    return call(
        place_feed_body,
        (2, 2),
        (order, *arrays),
        [shape(down_shape, F32), shape(up_shape, F32), shape((8, width), F32)],
        [
            pl.BlockSpec((width, width), lambda h, i, m: (2 * h + i, 0)),
            pl.BlockSpec((width, width), lambda h, i, m: (0, 2 * h + i)),
            result(8, width),
        ],
        [whole(*x.shape) for x in arrays],
        scalars=1,
        limit=28,
        cost=8,
    )


def place_squares_body(order, own_1, other_1, own_2, other_2, others, norms, *refs):
    *outs, norm, total = refs
    side = pl.program_id(0)
    ours = (side ^ order[0]) == 0

    @pl.when(side == 0)
    def _():
        total[...] = others[...]

    def place(first, second):
        pieces, _, line, _ = first.shape

        def one(piece, square):
            for source, mask, pair in ((first, order[1], outs[:2]), (second, order[2], outs[2:])):
                for at, out in enumerate(pair):
                    value = source[piece ^ mask, at].astype(F32)
                    out[pl.ds(pl.multiple_of(piece * line, line), line), :] = value
                    square += jnp.sum(value * value, axis=0, keepdims=True)
            return square

        total[0:1, :] += lax.fori_loop(0, pieces, one, jnp.zeros((1, outs[0].shape[1]), F32))

    pl.when(ours)(lambda: place(own_1, own_2))
    pl.when(jnp.logical_not(ours))(lambda: place(other_1, other_2))

    @pl.when(side == 1)
    def _():
        square = jnp.sum(total[0:1, :], keepdims=True) + jnp.sum(
            norms[...] * norms[...], keepdims=True
        )
        norm[...] = jnp.sqrt(square)


def place_squares(order, own_1, other_1, own_2, other_2, others, norms):
    pieces, _, line, width = own_1.shape
    arrays = (own_1, other_1, own_2, other_2, others, norms)
    return call(
        place_squares_body,
        (2,),
        (order, *arrays),
        [shape((2 * pieces * line, width), F32)] * 4 + [shape((1, 1), F32)],
        [pl.BlockSpec((pieces * line, width), lambda i, m: (i, 0))] * 4 + [result(1, 1)],
        [whole(*x.shape) for x in arrays],
        [pltpu.VMEM(others.shape, F32)],
        scalars=1,
        limit=24,
        cost=5,
    )


def leave_body(
    meta, own, other, columns, normed, tokens, gain, grad_queries, query_w, grad_attended,
    tokens_grad, terms, norm_grads, columns_t, terms_sum, grad_summary,
):
    seq = pl.program_id(0)
    rows, span = columns.shape

    @pl.when(seq == 0)
    def _():
        columns_t[...] = columns[...].T
        terms_sum[...] = jnp.zeros_like(terms_sum)
        norm_grads[...] = jnp.zeros_like(norm_grads)

    take_by_distance(meta[0], own, other, grad_summary)
    length = meta[1 + seq] - meta[0] * span
    lane = lax.broadcasted_iota(jnp.int32, (rows, span), 1) < length
    line = lax.broadcasted_iota(jnp.int32, (span, 1), 0) < length
    summed = grad_summary[...]
    terms_sum[...] += jnp.where(lane, nt(summed, normed[...]), 0.0)
    grad = nt(grad_queries[...], query_w[...]) + jnp.where(line, nn(columns_t[...], summed), 0.0)
    unit, inverse = centre(tokens[...].astype(F32))
    norm_grads[0:1, :] += jnp.sum(grad * unit, axis=0, keepdims=True)
    norm_grads[1:2, :] += jnp.sum(grad, axis=0, keepdims=True)
    tokens_grad[...] = (
        grad_attended[...] + normalize_back(grad, unit, inverse, row(gain))
    ).astype(LOW)

    @pl.when(seq == pl.num_programs(0) - 1)
    def _():
        terms[...] = terms_sum[...].astype(LOW)


def leave(
    meta, own, other, columns, normed, tokens, gain, grad_queries, query_w, grad_attended
):
    seqs, span, width = tokens.shape
    rows = columns.shape[0]
    distance = distance_spec(own.shape[0], rows, width)
    block = per_seq(span, width)
    return call(
        leave_body,
        (seqs,),
        (
            meta, own, other, columns, *kept_far(normed, tokens), gain, *kept_far(grad_queries), query_w,
            *kept_far(grad_attended),
        ),
        [shape(tokens.shape), shape((rows, span)), shape((8, width), F32)],
        [block, result(rows, span), result(8, width)],
        [
            distance, distance, whole(rows, span), block, block, vector(width), block,
            whole(width, width), block,
        ],
        [
            pltpu.VMEM((span, rows), LOW),
            pltpu.VMEM((rows, span), F32),
            pltpu.VMEM((rows, width), LOW),
        ],
        scalars=1,
        limit=20,
        cost=5,
    )


def swap(value, axis, mask):
    size = lax.axis_size(axis)
    return lax.ppermute(value, axis, [(i, i ^ mask) for i in range(size)])


def pick(value, at):
    return lax.dynamic_index_in_dim(value, at, 0, keepdims=False)


def bits_of(axis):
    return (lax.axis_size(axis) - 1).bit_length()


def bit(axis, at):
    return (lax.axis_index(axis) >> at) & 1


def after(values, ticket):
    return lax.optimization_barrier((values, ticket))[0]


def in_order(mine, other, at):
    return jnp.where(at == 0, jnp.stack([mine, other]), jnp.stack([other, mine]))


def krow_orders():
    count = bits_of("krow")
    return [list(range(1, count)), list(range(count - 1, 0, -1))]


def distance_masks():
    count = bits_of("krow")
    masks = [bit("krow", 0)]
    for order in krow_orders():
        masks.append(sum(bit("krow", at) << (count - 2 - d) for d, at in enumerate(order)))
    return jnp.stack(masks).astype(jnp.int32)


def sum_everywhere(sent, halved):
    orders = krow_orders()
    flight = [swap(x, "krow", 1) for x in sent]
    kept = yield sent
    ticket = yield kept
    for digit in range(len(orders[0])):
        flight, kept = after((flight, kept), ticket)
        half = kept[0].shape[0] // 2
        sent = [k[half:] + f[half:] for k, f in zip(kept, flight)]
        kept = [k[:half] + f[:half] for k, f in zip(kept, flight)]
        flight = [swap(x, "krow", 1 << o[digit]) for x, o in zip(sent, orders)]
        ticket = yield (sent, kept)
    flight, kept = after((flight, kept), ticket)
    value = jnp.concatenate([k + f for k, f in zip(kept, flight)])
    split = []
    for at in range(bits_of("dp")):
        if at < halved:
            half = value.reshape(2, -1, value.shape[-1])
            mine = bit("dp", at)
            sent, kept = pick(half, 1 - mine), pick(half, mine)
            split.append((at, mine))
        else:
            sent = kept = value
        flight = swap(sent, "dp", 1 << at)
        ticket = yield (sent, kept)
        flight, kept = after((flight, kept), ticket)
        value = kept + flight
    for at, mine in reversed(split):
        flight = swap(value, "dp", 1 << at)
        ticket = yield value
        flight, value = after((flight, value), ticket)
        value = in_order(value, flight, mine).reshape(-1, value.shape[-1])
    values = list(value.reshape(2, 1, -1, value.shape[-1]))
    for digit in reversed(range(len(orders[0]))):
        flight = [swap(v, "krow", 1 << o[digit]) for v, o in zip(values, orders)]
        ticket = yield values
        flight, values = after((flight, values), ticket)
        values = [jnp.concatenate([v, f]) for v, f in zip(values, flight)]
    flight = [swap(v, "krow", 1) for v in values]
    ticket = yield values
    yield after([x for pair in zip(values, flight) for x in pair], ticket)


def sum_krow(sent, kept):
    pairs = kept.shape[0]
    flight = swap(sent, "krow", 1)
    ticket = yield kept
    kept, flight = after((kept, flight), ticket)
    half = [k.astype(F32) + f.astype(F32) for k, f in zip(kept, flight)]
    sent = [h.astype(LOW) for h in half[1:]]
    flight = [swap(x, "krow", 2 * pair) for pair, x in enumerate(sent, 1)]
    kept = half[0]
    ticket = yield (kept, sent)
    kept, flight = after((kept, flight), ticket)
    total = sum([f.astype(F32) for f in flight], kept).astype(LOW)
    flight = [swap(total, "krow", 2 * pair) for pair in range(1, pairs)]
    ticket = yield total
    total, flight = after((total, flight), ticket)
    own = jnp.stack([total, *flight])
    flight = swap(own, "krow", 1)
    ticket = yield own
    yield after((own, flight), ticket)


def sum_small(value):
    for axis in ("krow", "dp"):
        for at in range(bits_of(axis)):
            flight = swap(value, axis, 1 << at)
            ticket = yield value
            flight, value = after((flight, value), ticket)
            value = value + flight
    yield value


def sum_terms(terms, ring):
    rows, span = terms.shape
    value = lax.all_to_all(
        terms.reshape(ring, rows // ring, span), "krow", 0, 1, tiled=False
    ).reshape(rows // ring, ring * span)
    ticket = yield terms
    value = after(value, ticket)
    for at in range(bits_of("dp")):
        flight = swap(value, "dp", 1 << at)
        ticket = yield value
        flight, value = after((flight, value), ticket)
        value = value + flight
    yield value


class Line:
    def __init__(self, ticket):
        self.ticket = ticket

    def step(self, *sums):
        for each in sums:
            self.ticket = each.send(self.ticket)

    def run(self, kernel, *values):
        self.ticket = kernel(*after(values, self.ticket))
        return self.ticket


    def start(self, steps, *first):
        self.ticket = (self.ticket, next(steps))
        for value in first:
            self.ticket = (self.ticket, steps.send(value))
        return steps


PLAN = "S1KF212A1Bg1Q3g12312g1O32g1gL2312c32c3n2n31c32n132nP3ncn3"
HALVED = {"1": 2, "2": 2, "3": 2}


def local(
    tokens,
    lengths,
    attn_gain,
    attn_bias,
    query_weight,
    key_weight,
    value_weight,
    out_weight,
    compress,
    ffn_gain,
    ffn_bias,
    up_weight,
    down_weight,
    cotangent,
):
    seqs, span, width = tokens.shape
    ring = lax.axis_size("krow")
    rows = compress.shape[0] * ring
    pairs = pieces = ring // 2
    flat, tall = (seqs * span, width), (seqs * rows, width)
    order = distance_masks()
    meta = jnp.concatenate([lax.axis_index("krow")[None].astype(jnp.int32), lengths])
    columns = lax.all_to_all(
        compress.reshape(compress.shape[0], ring, span), "krow", 1, 0, tiled=False
    ).reshape(rows, span)
    cotangent_flat = cotangent.reshape(flat)
    normed = enter(tokens, attn_gain, attn_bias)
    kept, sent = summarize(pairs, meta, columns, normed)
    line = Line((kept, sent))
    summing = line.start(sum_krow(sent, kept))
    line.step(summing)
    grad_active = line.run(grad_active_of, cotangent_flat, down_weight)
    line.step(summing)
    queries = line.run(project, normed, query_weight)
    line.step(summing, summing)
    summary, keys, values, probs, mixed, attended, lifted, inverse = attend(
        meta, tokens, queries, *line.ticket, key_weight, value_weight, out_weight, ffn_gain,
        ffn_bias,
    )
    line.ticket = lifted

    def as_pieces(arrays):
        return [x.reshape(pieces, -1, width) for x in arrays]

    known, sums, results = {}, {}, {}

    def feed_blocks(first, blocks):
        return line.run(
            lambda lifted: feed(
                first, blocks, pieces, order, lifted.reshape(flat), cotangent_flat, grad_active,
                up_weight,
            ),
            lifted,
        )

    def run_s():
        known["active_1"], known["hidden_1"], *known["sent_1"] = feed_blocks(0, 1)

    def run_k():
        known["active_2"], known["hidden_2"], *known["kept_1"] = feed_blocks(1, 1)

    def run_f():
        out = feed_blocks(2, 2)
        known["active_3"], known["hidden_3"], *known["sent_2"] = out[:4]
        known["active_4"], known["hidden_4"], *known["kept_2"] = out[4:]

    def run_a():
        known["grad_attended"], known["grad_branch"], known["grad_mixed"], known["ffn_norms"] = (
            line.run(
                lambda *hiddens: feed_back(
                    order, hiddens, up_weight, cotangent, attended, inverse, ffn_gain, out_weight
                ),
                *(known[f"hidden_{at}"] for at in range(1, 5)),
            )
        )

    def run_b():
        *known["grads"], known["kept_g"], known["sent_g"] = line.run(
            lambda grad_mixed: attend_back(
                pairs, meta, grad_mixed, queries, keys, values, probs, key_weight, value_weight
            ),
            known["grad_mixed"],
        )

    def run_q():
        out = line.run(
            lambda branch, grad_queries, grad_keys, grad_values: squares(
                pieces, order, normed.reshape(flat), summary.reshape(tall), mixed.reshape(flat),
                grad_queries.reshape(flat), grad_keys.reshape(tall), grad_values.reshape(tall),
                branch.reshape(flat),
            ),
            known["grad_branch"],
            *known["grads"],
        )
        known["sent_3"], known["kept_3"] = out[:2], out[2:]

    def run_o():
        known["block_out"] = line.run(
            lambda *actives: block_out_of(order, down_weight, attended, *actives),
            *(known[f"active_{at}"] for at in range(1, 5)),
        )

    def run_l():
        finish("g")
        known["tokens_grad"], known["terms"], attn_norms = line.run(
            lambda own, other: leave(
                meta, own, other, columns, normed, tokens, attn_gain, known["grads"][0],
                query_weight, known["grad_attended"],
            ),
            *results["g"],
        )
        known["norms"] = jnp.concatenate([attn_norms[:2], known["ffn_norms"][:2]])

    def run_p():
        finish("1")
        finish("2")
        form = (pieces, width // QUAD, QUAD // pieces, width)
        arrays = [
            x.reshape(form) if at % 4 < 2 else x
            for at, x in enumerate((*results["1"], *results["2"]))
        ]
        known["feed"] = line.run(
            lambda *arrays: place_feed(order, down_weight.shape, up_weight.shape, *arrays),
            *arrays,
        )

    def begin(name):
        if name == "g":
            return sum_krow(known["sent_g"], known["kept_g"])
        if name == "n":
            return sum_small(known["norms"])
        if name == "c":
            return sum_terms(known["terms"], ring)
        return sum_everywhere(as_pieces(known[f"sent_{name}"]), HALVED[name])

    def advance(name):
        if name not in sums:
            sums[name] = [begin(name), 0]
            line.start(sums[name][0])
        else:
            if sums[name][1] == 1 and name in HALVED:
                sums[name][0].send(as_pieces(known[f"kept_{name}"]))
            try:
                line.step(sums[name][0])
                results[name] = line.ticket
            except StopIteration:
                return False
        sums[name][1] += 1
        return True

    def finish(name):
        while advance(name):
            pass

    kernels = {
        "S": run_s, "K": run_k, "F": run_f, "A": run_a, "B": run_b, "Q": run_q, "O": run_o,
        "L": run_l, "P": run_p,
    }
    for name in PLAN:
        if name in kernels:
            kernels[name]()
        else:
            advance(name)
    for name in "nc3":
        finish(name)
    down_grad, up_grad, others = known["feed"]
    arrays = [x.reshape(pieces, 2, -1, width) for x in results["3"]]
    norms, compress_grad = results["n"], results["c"]
    *attn_grads, grad_norm = place_squares(order, *arrays, others, norms)
    block_out, tokens_grad = known["block_out"], known["tokens_grad"]
    return (
        block_out,
        tokens_grad,
        norms[0],
        norms[1],
        *attn_grads,
        compress_grad.astype(F32),
        norms[2],
        norms[3],
        up_grad,
        down_grad,
        grad_norm.reshape(()),
    )


def solution(mesh):
    rows, held = P("dp", "krow", None), P("krow", None)
    in_specs = (rows, P("dp"), P(), P(), P(), P(), P(), P(), held, P(), P(), P(), P(), rows)
    out_specs = (rows, rows, P(), P(), P(), P(), P(), P(), held, P(), P(), P(), P(), P())
    return jax.shard_map(local, mesh=mesh, in_specs=in_specs, out_specs=out_specs, check_vma=False)
```

```python
import functools

import jax
import jax.numpy as jnp
from jax import lax
from jax.experimental import pallas as pl
from jax.experimental.pallas import tpu as pltpu
from jax.sharding import PartitionSpec as P

HEAD_DIM = 64
QUAD = 256
EPSILON = 1e-05
SCALE = HEAD_DIM ** (-0.5)
LOW = jnp.bfloat16
F32 = jnp.float32
COST = 4 * 10**9


def dot(left_side, right_side, contract):
    return lax.dot_general(
        left_side, right_side, (contract, ((), ())), preferred_element_type=F32
    )


def nn(left_side, right_side):
    return dot(left_side, right_side, ((1,), (0,)))


def nt(left_side, right_side):
    return dot(left_side, right_side, ((1,), (1,)))


def shape(dims, kind=LOW):
    return jax.ShapeDtypeStruct(dims, kind)


def far(dims, kind=LOW):
    return pltpu.HBM(dims, kind)


def kept_far(*values):
    return tuple(pltpu.with_memory_space_constraint(v, pltpu.HBM) for v in values)


def whole(*dims):
    return pl.BlockSpec(dims, lambda *_: (0,) * len(dims), pipeline_mode=pl.Buffered(1))


def result(*dims):
    return pl.BlockSpec(dims, lambda *_: (0,) * len(dims))


def vector(width):
    return pl.BlockSpec((width,), lambda *_: (0,))


def per_seq(*dims):
    return pl.BlockSpec((None, *dims), lambda s, *_: (s, *(0,) * len(dims)))


def call(body, grid, ins, outs, out_specs, in_specs, scratch=(), scalars=0, limit=24, cost=1):
    return pl.pallas_call(
        body,
        grid_spec=pltpu.PrefetchScalarGridSpec(
            num_scalar_prefetch=scalars,
            grid=grid,
            in_specs=in_specs,
            out_specs=out_specs,
            scratch_shapes=scratch,
        ),
        out_shape=outs,
        compiler_params=pltpu.CompilerParams(vmem_limit_bytes=limit << 20),
        name=getattr(body, "__name__", None) or body.func.__name__,
        cost_estimate=pl.CostEstimate(flops=cost * COST, bytes_accessed=1, transcendentals=0),
    )(*ins)


def row(ref):
    return ref[...].reshape(1, -1)


def centre(values):
    centred = values - jnp.mean(values, axis=-1, keepdims=True)
    spread = jnp.mean(centred * centred, axis=-1, keepdims=True)
    inverse = lax.rsqrt(spread + EPSILON)
    return centred * inverse, inverse


def normalize_back(grad, unit, inverse, gain):
    scaled = grad * gain
    return inverse * (
        scaled
        - jnp.mean(scaled, axis=-1, keepdims=True)
        - unit * jnp.mean(scaled * unit, axis=-1, keepdims=True)
    )


def enter_body(tokens, gain, bias, normed):
    unit, _ = centre(tokens[...].astype(F32))
    normed[...] = (unit * row(gain) + row(bias)).astype(LOW)


def enter(tokens, gain, bias):
    seqs, span, width = tokens.shape
    block = per_seq(span, width)
    return call(
        enter_body,
        (seqs,),
        (tokens, gain, bias),
        far(tokens.shape),
        block,
        [block, vector(width), vector(width)],
        limit=10,
        cost=1,
    )


def project_body(normed, weight, queries):
    queries[...] = (nn(normed[...], weight[...]) * SCALE).astype(LOW)


def project(normed, weight):
    seqs, span, width = normed.shape
    block = per_seq(span, width)
    return call(
        project_body,
        (seqs,),
        (normed, weight),
        far(normed.shape),
        block,
        [block, whole(width, width)],
        limit=10,
        cost=1,
    )


def grad_active_body(cotangent, down, out):
    out[...] = nt(cotangent[...], down[...]).astype(LOW)


def grad_active_of(cotangent, down):
    rows, width = cotangent.shape
    hidden = down.shape[0]
    cut = QUAD * 2
    return call(
        grad_active_body,
        (hidden // cut,),
        (cotangent, down),
        far((rows, hidden)),
        pl.BlockSpec((rows, cut), lambda i: (0, i)),
        [whole(rows, width), pl.BlockSpec((cut, width), lambda i: (i, 0))],
        limit=14,
        cost=5,
    )


def block_at(pair, own, order):
    return 2 * pair + (order[0] ^ 1 ^ own)


def block_out_body(order, down, attended, sent, kept, out):
    width = attended.shape[1]
    total = attended[...]
    for own, actives in enumerate((sent, kept)):
        for pair in range(actives.shape[0]):
            start = pl.multiple_of(block_at(pair, own, order) * width, width)
            total += nn(actives[pair], down[pl.ds(start, width), :])
    out[...] = total.astype(LOW)


def block_out_of(order, down, attended, *actives):
    seqs, span, width = attended.shape
    lines = pl.BlockSpec((actives[0].shape[0], span, width), lambda s, m: (0, s, 0))
    return call(
        block_out_body,
        (seqs,),
        (order, down, *kept_far(attended, *actives)),
        shape(attended.shape),
        per_seq(span, width),
        [whole(*down.shape), per_seq(span, width), *([lines] * len(actives))],
        scalars=1,
        limit=24,
        cost=0,
    )


def send_by_distance(me, value, held, kept, sent):
    pieces = 2 * kept.shape[0]
    cut = value.shape[0] // pieces
    held[...] = value
    for pair in range(pieces // 2):
        for other, out in enumerate((kept, sent)):
            start = pl.multiple_of(((2 * pair + other) ^ me) * cut, cut)
            out[pair] = held[pl.ds(start, cut), :].astype(LOW)


def take_by_distance(me, own, other, out):
    pieces = 2 * own.shape[0]
    cut = own.shape[1]
    for pair in range(pieces // 2):
        for at, source in enumerate((own, other)):
            start = pl.multiple_of(((2 * pair + at) ^ me) * cut, cut)
            out[pl.ds(start, cut), :] = source[pair]


def distance_rows(pairs, seqs, rows, width):
    return shape((pairs, seqs, rows // pairs // 2, width))


def distance_spec(pairs, rows, width):
    return pl.BlockSpec((pairs, None, rows // pairs // 2, width), lambda s, *_: (0, s, 0, 0))


def summarize_body(meta, columns, normed, kept, sent, held):
    seq = pl.program_id(0)
    rows, span = columns.shape
    at = meta[0] * span + lax.broadcasted_iota(jnp.int32, (rows, span), 1)
    masked = jnp.where(at < meta[1 + seq], columns[...].astype(F32), 0.0).astype(LOW)
    send_by_distance(meta[0], nn(masked, normed[...]), held, kept, sent)


def summarize(pairs, meta, columns, normed):
    seqs, span, width = normed.shape
    rows = columns.shape[0]
    return call(
        summarize_body,
        (seqs,),
        (meta, columns, normed),
        [distance_rows(pairs, seqs, rows, width)] * 2,
        [distance_spec(pairs, rows, width)] * 2,
        [whole(rows, span), per_seq(span, width)],
        [pltpu.VMEM((rows, width), F32)],
        scalars=1,
        limit=12,
        cost=2,
    )


def head_masks(dims, axis):
    lane = lax.broadcasted_iota(jnp.int32, dims, axis) // HEAD_DIM
    return [lane == h for h in range(QUAD // HEAD_DIM)]


def stack_heads(value, masks, axis):
    wide = value.astype(F32)
    return jnp.concatenate([jnp.where(m, wide, 0.0).astype(LOW) for m in masks], axis=axis)


def own_heads(stacked, masks, rows):
    parts = [stacked[h * rows : (h + 1) * rows] for h in range(len(masks))]
    out = jnp.where(masks[0], parts[0], 0.0)
    for mask, part in zip(masks[1:], parts[1:]):
        out = jnp.where(mask, part, out)
    return out


def attend_body(
    meta, tokens, queries, own, other, key_w, value_w, out_w, gain, bias,
    summary, keys, values, probs, mixed, attended, lifted, inverse_out,
):
    span, width = tokens.shape
    rows = summary.shape[0]
    take_by_distance(meta[0], own, other, summary)
    key_all = nn(summary[...], key_w[...]).astype(LOW)
    value_all = nn(summary[...], value_w[...]).astype(LOW)
    keys[...] = key_all
    values[...] = value_all
    side = head_masks((rows, QUAD), 1)
    turned = head_masks((QUAD, rows), 0)
    quads = []
    for q in range(width // QUAD):
        cut = slice(q * QUAD, (q + 1) * QUAD)
        scores = nt(stack_heads(key_all[:, cut], side, 0), queries[:, cut])
        lows = []
        for h in range(len(side)):
            part = scores[h * rows : (h + 1) * rows]
            grown = jnp.exp(part - jnp.max(part, axis=0, keepdims=True))
            lows.append((grown / jnp.sum(grown, axis=0, keepdims=True)).astype(LOW))
        low = jnp.concatenate(lows, axis=0)
        probs[q * low.shape[0] : (q + 1) * low.shape[0], :] = low
        quads.append(nn(stack_heads(value_all[:, cut].astype(F32).T, turned, 1), low).T)
    mixed_low = jnp.concatenate(quads, axis=1).astype(LOW)
    mixed[...] = mixed_low
    total = tokens[...].astype(F32) + nn(mixed_low, out_w[...])
    attended[...] = total
    unit, inverse = centre(total)
    inverse_out[...] = jnp.broadcast_to(inverse, inverse_out.shape)
    lifted[...] = (unit * row(gain) + row(bias)).astype(LOW)


def attend(meta, tokens, queries, own, other, key_w, value_w, out_w, gain, bias):
    seqs, span, width = tokens.shape
    pairs = own.shape[0]
    rows = 2 * pairs * own.shape[2]
    tall = (width // HEAD_DIM) * rows
    weight = whole(width, width)
    return call(
        attend_body,
        (seqs,),
        (meta, *kept_far(tokens, queries), own, other, key_w, value_w, out_w, gain, bias),
        [
            far((seqs, rows, width)),
            far((seqs, rows, width)),
            far((seqs, rows, width)),
            far((seqs, tall, span)),
            far((seqs, span, width)),
            far((seqs, span, width), F32),
            shape((seqs, span, width)),
            far((seqs, span, 128), F32),
        ],
        [
            per_seq(rows, width),
            per_seq(rows, width),
            per_seq(rows, width),
            per_seq(tall, span),
            per_seq(span, width),
            per_seq(span, width),
            per_seq(span, width),
            per_seq(span, 128),
        ],
        [
            per_seq(span, width),
            per_seq(span, width),
            distance_spec(pairs, rows, width),
            distance_spec(pairs, rows, width),
            weight,
            weight,
            weight,
            vector(width),
            vector(width),
        ],
        scalars=1,
        limit=32,
        cost=10,
    )


def feed_body(
    order, lifted, cotangent, grad_active, up, active_out, grad_out, down_grad, up_grad, turned
):
    @pl.when(pl.program_id(0) == 0)
    def _():
        turned[...] = lifted[...].T

    hidden = nn(lifted[...], up[...])
    share = 0.5 * (1.0 + lax.erf(hidden * 0.5**0.5))
    slope = share + hidden * jnp.exp(-0.5 * hidden * hidden) * 0.3989422804014327
    active = (hidden * share).astype(LOW)
    grad_hidden = (grad_active[...].astype(F32) * slope).astype(LOW)
    active_out[...] = active
    grad_out[...] = grad_hidden
    pieces, line = down_grad.shape[0], down_grad.shape[1]
    value = nn(active.T, cotangent[...])
    for piece in range(pieces):
        down_grad[piece ^ order[1]] = value[piece * line : (piece + 1) * line].astype(LOW)
    value = nn(turned[...], grad_hidden)
    line = up_grad.shape[1]
    for piece in range(pieces):
        up_grad[piece ^ order[2]] = value[piece * line : (piece + 1) * line].astype(LOW)


def feed(own, pieces, order, lifted, cotangent, grad_active, up):
    rows, width = lifted.shape
    steps = width // QUAD
    pairs = up.shape[1] // width // 2

    def columns(i, m):
        return (0, block_at(i // steps, own, m) * steps + i % steps)

    def lines(i, m):
        return (i // steps, 0, i % steps)

    return call(
        feed_body,
        (pairs * steps,),
        (order, lifted, cotangent, grad_active, up),
        [
            far((pairs, rows, width)),
            far((pairs, rows, width)),
            shape((pieces, pairs, steps, QUAD // pieces, width)),
            shape((pieces, pairs, width // pieces, width)),
        ],
        [
            pl.BlockSpec((None, rows, QUAD), lines),
            pl.BlockSpec((None, rows, QUAD), lines),
            pl.BlockSpec(
                (pieces, None, None, QUAD // pieces, width),
                lambda i, m: (0, i // steps, i % steps, 0, 0),
            ),
            pl.BlockSpec(
                (pieces, None, width // pieces, QUAD), lambda i, m: (0, i // steps, 0, i % steps)
            ),
        ],
        [
            whole(rows, width),
            whole(rows, width),
            pl.BlockSpec((rows, QUAD), columns),
            pl.BlockSpec((width, QUAD), columns),
        ],
        [pltpu.VMEM((width, rows), LOW)],
        scalars=1,
        limit=20,
        cost=6 * pairs,
    )


def feed_back_body(
    order, sent, kept, up, cotangent, attended, inverse, gain, out_w,
    grad_attended, grad_branch, grad_mixed, norm_grads,
):
    width = cotangent.shape[1]

    @pl.when(pl.program_id(0) == 0)
    def _():
        norm_grads[...] = jnp.zeros_like(norm_grads)

    total = attended[...]
    scale = inverse[:, :1]
    unit = (total - jnp.mean(total, axis=-1, keepdims=True)) * scale
    grad = 0.0
    for own, hiddens in enumerate((sent, kept)):
        for pair in range(hiddens.shape[0]):
            start = pl.multiple_of(block_at(pair, own, order) * width, width)
            grad += nt(hiddens[pair], up[:, pl.ds(start, width)])
    norm_grads[0:1, :] += jnp.sum(grad * unit, axis=0, keepdims=True)
    norm_grads[1:2, :] += jnp.sum(grad, axis=0, keepdims=True)
    whole_grad = cotangent[...].astype(F32) + normalize_back(grad, unit, scale, row(gain))
    grad_attended[...] = whole_grad
    branch = whole_grad.astype(LOW)
    grad_branch[...] = branch
    grad_mixed[...] = nt(branch, out_w[...]).astype(LOW)


def feed_back(order, hiddens, up, cotangent, attended, inverse, gain, out_w):
    seqs, span, width = cotangent.shape
    block = per_seq(span, width)
    lines = pl.BlockSpec((hiddens[0].shape[0], span, width), lambda s, *_: (0, s, 0))
    return call(
        feed_back_body,
        (seqs,),
        (
            order, *kept_far(*hiddens), up, *kept_far(cotangent, attended, inverse), gain, out_w,
        ),
        [
            far((seqs, span, width), F32),
            far((seqs, span, width)),
            far((seqs, span, width)),
            shape((8, width), F32),
        ],
        [block, block, block, result(8, width)],
        [
            *([lines] * len(hiddens)), whole(*up.shape), block, block, per_seq(span, 128),
            vector(width), whole(width, width),
        ],
        scalars=1,
        limit=24,
        cost=8,
    )


def attend_back_body(
    meta, grad_mixed, queries, keys, values, probs, key_w, value_w,
    grad_queries, grad_keys, grad_values, kept, sent, held,
):
    span, width = grad_mixed.shape
    rows = keys.shape[0]
    side = head_masks((rows, QUAD), 1)
    turned = head_masks((QUAD, rows), 0)
    for q in range(width // QUAD):
        cut = slice(q * QUAD, (q + 1) * QUAD)
        mixed_cut = grad_mixed[:, cut]
        tall = len(side) * rows
        low = probs[q * tall : (q + 1) * tall, :]
        grad_probs = nt(stack_heads(values[:, cut], side, 0), mixed_cut)
        lows = []
        for h in range(len(side)):
            part = low[h * rows : (h + 1) * rows].astype(F32)
            ours = grad_probs[h * rows : (h + 1) * rows]
            inner = jnp.sum(part * ours, axis=0, keepdims=True)
            lows.append((part * (ours - inner)).astype(LOW))
        grad_scores = jnp.concatenate(lows, axis=0)
        grad_values[:, cut] = own_heads(nn(low, mixed_cut), side, rows).astype(LOW)
        grad_keys[:, cut] = own_heads(nn(grad_scores, queries[:, cut]), side, rows).astype(LOW)
        keys_turned = stack_heads(keys[:, cut].astype(F32).T, turned, 1)
        grad_queries[:, cut] = (nn(keys_turned, grad_scores) * SCALE).T.astype(LOW)
    grad_summary = nt(grad_keys[...], key_w[...]) + nt(grad_values[...], value_w[...])
    send_by_distance(meta[0], grad_summary, held, kept, sent)


def attend_back(pairs, meta, grad_mixed, queries, keys, values, probs, key_w, value_w):
    seqs, span, width = grad_mixed.shape
    rows = keys.shape[1]
    tall = probs.shape[1]
    weight = whole(width, width)
    block, rows_block = per_seq(span, width), per_seq(rows, width)
    distance = distance_spec(pairs, rows, width)
    return call(
        attend_back_body,
        (seqs,),
        (meta, *kept_far(grad_mixed, queries, keys, values, probs), key_w, value_w),
        [
            far((seqs, span, width)),
            far((seqs, rows, width)),
            far((seqs, rows, width)),
            distance_rows(pairs, seqs, rows, width),
            distance_rows(pairs, seqs, rows, width),
        ],
        [block, rows_block, rows_block, distance, distance],
        [block, block, rows_block, rows_block, per_seq(tall, span), weight, weight],
        [pltpu.VMEM((rows, width), F32)],
        scalars=1,
        limit=24,
        cost=14,
    )


def squares_body(
    order, normed, summary, mixed, grad_queries, grad_keys, grad_values, grad_branch,
    sent_1, sent_2, kept_1, kept_2, normed_t, summary_t, mixed_t,
):
    @pl.when(pl.program_id(0) == 0)
    def _():
        normed_t[...] = normed[...].T
        summary_t[...] = summary[...].T
        mixed_t[...] = mixed[...].T

    pieces = sent_1.shape[0]
    half = normed_t.shape[0] // 2
    members = (
        (normed_t, grad_queries, (sent_1, kept_1), 0, order[1]),
        (summary_t, grad_keys, (sent_1, kept_1), 1, order[1]),
        (summary_t, grad_values, (sent_2, kept_2), 0, order[2]),
        (mixed_t, grad_branch, (sent_2, kept_2), 1, order[2]),
    )
    for left, right, outs, at, mask in members:
        for out, side in zip(outs, (1 - order[0], order[0])):
            start = pl.multiple_of(side * half, half)
            value = nn(left[pl.ds(start, half), :], right[...])
            cut = half // pieces
            for piece in range(pieces):
                out[piece ^ mask, at] = value[piece * cut : (piece + 1) * cut].astype(LOW)


def squares(
    pieces, order, normed, summary, mixed, grad_queries, grad_keys, grad_values, grad_branch
):
    rows, width = normed.shape
    tall = summary.shape[0]
    cut = QUAD
    line = width // 2 // pieces
    return call(
        squares_body,
        (width // cut,),
        (
            order, normed, summary, mixed,
            *kept_far(grad_queries, grad_keys, grad_values, grad_branch),
        ),
        [shape((pieces, 2, line, width))] * 4,
        [pl.BlockSpec((pieces, 2, line, cut), lambda i, m: (0, 0, 0, i))] * 4,
        [
            whole(rows, width),
            whole(tall, width),
            whole(rows, width),
            pl.BlockSpec((rows, cut), lambda i, m: (0, i)),
            pl.BlockSpec((tall, cut), lambda i, m: (0, i)),
            pl.BlockSpec((tall, cut), lambda i, m: (0, i)),
            pl.BlockSpec((rows, cut), lambda i, m: (0, i)),
        ],
        [
            pltpu.VMEM((width, rows), LOW),
            pltpu.VMEM((width, tall), LOW),
            pltpu.VMEM((width, rows), LOW),
        ],
        scalars=1,
        limit=24,
        cost=7,
    )


def place_feed_body(order, own_down, other_down, own_up, other_up, down, up, total):
    pair, side = pl.program_id(0), pl.program_id(1)
    ours = (side ^ order[0]) == 0

    @pl.when((pair == 0) & (side == 0))
    def _():
        total[...] = jnp.zeros_like(total)

    def place(down_in, up_in):
        pieces, _, steps, line, _ = down_in.shape
        tall = up_in.shape[2]

        def one(piece, square):
            for step in range(steps):
                value = down_in[piece ^ order[1], pair, step].astype(F32)
                start = pl.multiple_of(step * pieces * line + piece * line, line)
                down[pl.ds(start, line), :] = value
                square += jnp.sum(value * value, axis=0, keepdims=True)
            value = up_in[piece ^ order[2], pair].astype(F32)
            up[pl.ds(pl.multiple_of(piece * tall, tall), tall), :] = value
            return square + jnp.sum(value * value, axis=0, keepdims=True)

        total[0:1, :] += lax.fori_loop(0, pieces, one, jnp.zeros((1, down.shape[1]), F32))

    pl.when(ours)(lambda: place(own_down, own_up))
    pl.when(jnp.logical_not(ours))(lambda: place(other_down, other_up))


def place_feed(order, down_shape, up_shape, *arrays):
    width = down_shape[1]
    return call(
        place_feed_body,
        (down_shape[0] // width // 2, 2),
        (order, *arrays),
        [shape(down_shape, F32), shape(up_shape, F32), shape((8, width), F32)],
        [
            pl.BlockSpec((width, width), lambda h, i, m: (2 * h + i, 0)),
            pl.BlockSpec((width, width), lambda h, i, m: (0, 2 * h + i)),
            result(8, width),
        ],
        [whole(*x.shape) for x in arrays],
        scalars=1,
        limit=28,
        cost=0,
    )


def place_squares_body(order, own_1, other_1, own_2, other_2, others, norms, *refs):
    *outs, attn_gain, attn_bias, ffn_gain, ffn_bias, norm, total = refs
    side = pl.program_id(0)
    ours = (side ^ order[0]) == 0

    @pl.when(side == 0)
    def _():
        total[...] = others[...]

    def place(first, second):
        pieces, _, line, _ = first.shape

        def one(piece, square):
            for source, mask, pair in ((first, order[1], outs[:2]), (second, order[2], outs[2:])):
                for at, out in enumerate(pair):
                    value = source[piece ^ mask, at].astype(F32)
                    out[pl.ds(pl.multiple_of(piece * line, line), line), :] = value
                    square += jnp.sum(value * value, axis=0, keepdims=True)
            return square

        total[0:1, :] += lax.fori_loop(0, pieces, one, jnp.zeros((1, outs[0].shape[1]), F32))

    pl.when(ours)(lambda: place(own_1, own_2))
    pl.when(jnp.logical_not(ours))(lambda: place(other_1, other_2))

    @pl.when(side == 1)
    def _():
        value = norms[...].astype(F32)
        square = jnp.sum(total[0:1, :], keepdims=True) + jnp.sum(value * value, keepdims=True)
        span = value.shape[1]
        cuts = attn_gain.shape[0] // span
        for at, out in enumerate((attn_gain, attn_bias, ffn_gain, ffn_bias)):
            for cut in range(cuts):
                line = value[at * cuts + cut : at * cuts + cut + 1]
                out[cut * span : (cut + 1) * span] = line.reshape(span)
        norm[...] = jnp.sqrt(square)


def place_squares(order, own_1, other_1, own_2, other_2, others, norms):
    pieces, _, line, width = own_1.shape
    arrays = (own_1, other_1, own_2, other_2, others, norms)
    return call(
        place_squares_body,
        (2,),
        (order, *arrays),
        [shape((2 * pieces * line, width), F32)] * 4
        + [shape((width,), F32)] * 4
        + [shape((1, 1), F32)],
        [pl.BlockSpec((pieces * line, width), lambda i, m: (i, 0))] * 4
        + [result(width)] * 4
        + [result(1, 1)],
        [whole(*x.shape) for x in arrays],
        [pltpu.VMEM(others.shape, F32)],
        scalars=1,
        limit=24,
        cost=5,
    )


def leave_body(
    meta, own, other, columns, normed, tokens, gain, grad_queries, query_w, grad_attended,
    ffn_norms, tokens_grad, packed, columns_t, terms_sum, norm_grads, grad_summary,
):
    seq = pl.program_id(0)
    rows, span = columns.shape

    @pl.when(seq == 0)
    def _():
        columns_t[...] = columns[...].T
        terms_sum[...] = jnp.zeros_like(terms_sum)
        norm_grads[...] = jnp.zeros_like(norm_grads)

    take_by_distance(meta[0], own, other, grad_summary)
    length = meta[1 + seq] - meta[0] * span
    lane = lax.broadcasted_iota(jnp.int32, (rows, span), 1) < length
    line = lax.broadcasted_iota(jnp.int32, (span, 1), 0) < length
    summed = grad_summary[...]
    terms_sum[...] += jnp.where(lane, nt(summed, normed[...]), 0.0)
    grad = nt(grad_queries[...], query_w[...]) + jnp.where(line, nn(columns_t[...], summed), 0.0)
    unit, inverse = centre(tokens[...].astype(F32))
    norm_grads[0:1, :] += jnp.sum(grad * unit, axis=0, keepdims=True)
    norm_grads[1:2, :] += jnp.sum(grad, axis=0, keepdims=True)
    tokens_grad[...] = (
        grad_attended[...] + normalize_back(grad, unit, inverse, row(gain))
    ).astype(LOW)

    @pl.when(seq == pl.num_programs(0) - 1)
    def _():
        total = terms_sum[...].astype(LOW)
        width = norm_grads.shape[1]
        lines = [
            source[at : at + 1, cut : cut + span]
            for source in (norm_grads, ffn_norms)
            for at in range(2)
            for cut in range(0, width, span)
        ]
        share, tall = rows // packed.shape[0], packed.shape[1]
        lines.append(jnp.zeros((tall - share - len(lines), span), F32))
        norms = jnp.concatenate(lines, axis=0).astype(LOW)
        for at in range(packed.shape[0]):
            packed[at, :share, :] = total[at * share : (at + 1) * share]
            packed[at, share:, :] = norms


def leave(
    ring, meta, own, other, columns, normed, tokens, gain, grad_queries, query_w, grad_attended,
    ffn_norms,
):
    seqs, span, width = tokens.shape
    rows = columns.shape[0]
    distance = distance_spec(own.shape[0], rows, width)
    tall = rows // ring + -(-4 * width // span // 16) * 16
    block = per_seq(span, width)
    return call(
        leave_body,
        (seqs,),
        (
            meta, own, other, columns, *kept_far(normed, tokens), gain, *kept_far(grad_queries), query_w,
            *kept_far(grad_attended), ffn_norms,
        ),
        [shape(tokens.shape), shape((ring, tall, span))],
        [block, result(ring, tall, span)],
        [
            distance, distance, whole(rows, span), block, block, vector(width), block,
            whole(width, width), block, whole(8, width),
        ],
        [
            pltpu.VMEM((span, rows), LOW),
            pltpu.VMEM((rows, span), F32),
            pltpu.VMEM((8, width), F32),
            pltpu.VMEM((rows, width), LOW),
        ],
        scalars=1,
        limit=20,
        cost=0,
    )


def swap(value, axis, mask):
    size = lax.axis_size(axis)
    return lax.ppermute(value, axis, [(i, i ^ mask) for i in range(size)])


def pick(value, at):
    return lax.dynamic_index_in_dim(value, at, 0, keepdims=False)


def bits_of(axis):
    return (lax.axis_size(axis) - 1).bit_length()


def bit(axis, at):
    return (lax.axis_index(axis) >> at) & 1


def after(values, ticket):
    return lax.optimization_barrier((values, ticket))[0]


def in_order(mine, other, at):
    return jnp.where(at == 0, jnp.stack([mine, other]), jnp.stack([other, mine]))


def krow_orders():
    count = bits_of("krow")
    return [list(range(1, count)), list(range(count - 1, 0, -1))]


def distance_masks():
    count = bits_of("krow")
    masks = [bit("krow", 0)]
    for order in krow_orders():
        masks.append(sum(bit("krow", at) << (count - 2 - d) for d, at in enumerate(order)))
    return jnp.stack(masks).astype(jnp.int32)


def sum_everywhere(sent, halved):
    orders = krow_orders()
    flight = [swap(x, "krow", 1) for x in sent]
    kept = yield sent
    ticket = yield kept
    for digit in range(len(orders[0])):
        flight, kept = after((flight, kept), ticket)
        half = kept[0].shape[0] // 2
        sent = [k[half:] + f[half:] for k, f in zip(kept, flight)]
        kept = [k[:half] + f[:half] for k, f in zip(kept, flight)]
        flight = [swap(x, "krow", 1 << o[digit]) for x, o in zip(sent, orders)]
        ticket = yield (sent, kept)
    flight, kept = after((flight, kept), ticket)
    values = [(k + f)[0] for k, f in zip(kept, flight)]
    count = bits_of("dp")
    strides = [list(range(count)), list(range(count - 1, -1, -1))]
    sides = [bit("dp", stride[0]) for stride in strides]
    for stage in range(count):
        sent = kept = values
        if stage < halved:
            halves = [v.reshape(2, -1, v.shape[-1]) for v in values]
            sent = [pick(h, 1 - side) for h, side in zip(halves, sides)]
            kept = [pick(h, side) for h, side in zip(halves, sides)]
        flight = [swap(x, "dp", 1 << o[stage]) for x, o in zip(sent, strides)]
        ticket = yield (sent, kept)
        flight, kept = after((flight, kept), ticket)
        values = [k + f for k, f in zip(kept, flight)]
    if halved:
        flight = [swap(x, "dp", 1 << o[0]) for x, o in zip(values, strides)]
        ticket = yield values
        flight, values = after((flight, values), ticket)
        values = [
            in_order(v, f, side).reshape(-1, v.shape[-1])
            for v, f, side in zip(values, flight, sides)
        ]
    values = [v[None] for v in values]
    for digit in reversed(range(len(orders[0]))):
        flight = [swap(v, "krow", 1 << o[digit]) for v, o in zip(values, orders)]
        ticket = yield values
        flight, values = after((flight, values), ticket)
        values = [jnp.concatenate([v, f]) for v, f in zip(values, flight)]
    flight = [swap(v, "krow", 1) for v in values]
    ticket = yield values
    yield after([x for pair in zip(values, flight) for x in pair], ticket)


def sum_krow(sent, kept):
    pairs = kept.shape[0]
    flight = swap(sent, "krow", 1)
    ticket = yield kept
    kept, flight = after((kept, flight), ticket)
    half = [k.astype(F32) + f.astype(F32) for k, f in zip(kept, flight)]
    sent = [h.astype(LOW) for h in half[1:]]
    flight = [swap(x, "krow", 2 * pair) for pair, x in enumerate(sent, 1)]
    kept = half[0]
    ticket = yield (kept, sent)
    kept, flight = after((kept, flight), ticket)
    total = sum([f.astype(F32) for f in flight], kept).astype(LOW)
    flight = [swap(total, "krow", 2 * pair) for pair in range(1, pairs)]
    ticket = yield total
    total, flight = after((total, flight), ticket)
    own = jnp.stack([total, *flight])
    flight = swap(own, "krow", 1)
    ticket = yield own
    yield after((own, flight), ticket)


def sum_terms(packed, share):
    span = packed.shape[2]
    flight = lax.all_to_all(packed, "krow", 0, 0, tiled=True)
    ticket = yield packed
    flight = after(flight, ticket)
    norms = jnp.sum(flight[:, share:].astype(F32), axis=0).astype(LOW)
    value = jnp.concatenate([flight[:, :share].reshape(-1, span), norms])
    for at in range(bits_of("dp")):
        flight = swap(value, "dp", 1 << at)
        ticket = yield value
        flight, value = after((flight, value), ticket)
        value = value + flight
    norms, value = value[packed.shape[0] * share :], value.astype(F32)
    ring = packed.shape[0]
    rows = ring * share
    compress = value[:rows].reshape(ring, share, span).transpose(1, 0, 2).reshape(share, -1)
    yield (compress, norms)


class Line:
    def __init__(self, ticket):
        self.ticket = ticket

    def step(self, *sums):
        for each in sums:
            self.ticket = each.send(self.ticket)

    def run(self, kernel, *values):
        self.ticket = kernel(*after(values, self.ticket))
        return self.ticket


    def start(self, steps, *first):
        self.ticket = (self.ticket, next(steps))
        for value in first:
            self.ticket = (self.ticket, steps.send(value))
        return steps


PLAN = "S1K1AB1gQ1g3g13ggL31313c31c3Oc3c11P33"
HALVED = {"1": 1, "3": 1}


def local(
    tokens,
    lengths,
    attn_gain,
    attn_bias,
    query_weight,
    key_weight,
    value_weight,
    out_weight,
    compress,
    ffn_gain,
    ffn_bias,
    up_weight,
    down_weight,
    cotangent,
):
    seqs, span, width = tokens.shape
    ring = lax.axis_size("krow")
    rows = compress.shape[0] * ring
    pairs = pieces = ring // 2
    flat, tall = (seqs * span, width), (seqs * rows, width)
    order = distance_masks()
    meta = jnp.concatenate([lax.axis_index("krow")[None].astype(jnp.int32), lengths])
    columns = lax.all_to_all(
        compress.reshape(compress.shape[0], ring, span), "krow", 1, 0, tiled=False
    ).reshape(rows, span)
    cotangent_flat = cotangent.reshape(flat)
    normed = enter(tokens, attn_gain, attn_bias)
    kept, sent = summarize(pairs, meta, columns, normed)
    line = Line((kept, sent))
    summing = line.start(sum_krow(sent, kept))
    line.step(summing)
    grad_active = line.run(grad_active_of, cotangent_flat, down_weight)
    line.step(summing)
    queries = line.run(project, normed, query_weight)
    line.step(summing, summing)
    summary, keys, values, probs, mixed, attended, lifted, inverse = attend(
        meta, tokens, queries, *line.ticket, key_weight, value_weight, out_weight, ffn_gain,
        ffn_bias,
    )
    line.ticket = lifted

    def as_pieces(arrays):
        return [x.reshape(pieces, -1, width) for x in arrays]

    known, sums, results = {}, {}, {}

    def run_feed(own):
        name = ("sent", "kept")[own]
        known[f"active_{name}"], known[f"hidden_{name}"], *known[f"{name}_1"] = line.run(
            lambda lifted: feed(
                own, pieces, order, lifted.reshape(flat), cotangent_flat, grad_active, up_weight
            ),
            lifted,
        )

    def run_a():
        known["grad_attended"], known["grad_branch"], known["grad_mixed"], known["ffn_norms"] = (
            line.run(
                lambda *hiddens: feed_back(
                    order, hiddens, up_weight, cotangent, attended, inverse, ffn_gain, out_weight
                ),
                known["hidden_sent"],
                known["hidden_kept"],
            )
        )

    def run_b():
        *known["grads"], known["kept_g"], known["sent_g"] = line.run(
            lambda grad_mixed: attend_back(
                pairs, meta, grad_mixed, queries, keys, values, probs, key_weight, value_weight
            ),
            known["grad_mixed"],
        )

    def run_q():
        out = line.run(
            lambda branch, grad_queries, grad_keys, grad_values: squares(
                pieces, order, normed.reshape(flat), summary.reshape(tall), mixed.reshape(flat),
                grad_queries.reshape(flat), grad_keys.reshape(tall), grad_values.reshape(tall),
                branch.reshape(flat),
            ),
            known["grad_branch"],
            *known["grads"],
        )
        known["sent_3"], known["kept_3"] = out[:2], out[2:]

    def run_o():
        known["block_out"] = line.run(
            lambda *actives: block_out_of(order, down_weight, attended, *actives),
            known["active_sent"],
            known["active_kept"],
        )

    def run_l():
        finish("g")
        known["tokens_grad"], known["terms"] = line.run(
            lambda own, other: leave(
                ring, meta, own, other, columns, normed, tokens, attn_gain, known["grads"][0],
                query_weight, known["grad_attended"], known["ffn_norms"],
            ),
            *results["g"],
        )

    def run_p():
        finish("1")
        pairs_held = down_weight.shape[0] // width // 2
        steps = width // QUAD
        forms = ((pieces, pairs_held, steps, QUAD // pieces, width), (pieces, pairs_held, -1, width))
        arrays = [x.reshape(forms[at // 2]) for at, x in enumerate(results["1"])]
        known["feed"] = line.run(
            lambda *arrays: place_feed(order, down_weight.shape, up_weight.shape, *arrays),
            *arrays,
        )

    def begin(name):
        if name == "g":
            return sum_krow(known["sent_g"], known["kept_g"])
        if name == "c":
            return sum_terms(known["terms"], rows // ring)
        return sum_everywhere(as_pieces(known[f"sent_{name}"]), HALVED[name])

    def advance(name):
        if name not in sums:
            sums[name] = [begin(name), 0]
            with jax.named_scope(f"sum_{name}_0"):
                line.start(sums[name][0])
        else:
            if sums[name][1] == 1 and name in HALVED:
                sums[name][0].send(as_pieces(known[f"kept_{name}"]))
            try:
                with jax.named_scope(f"sum_{name}_{sums[name][1]}"):
                    line.step(sums[name][0])
                results[name] = line.ticket
            except StopIteration:
                return False
        sums[name][1] += 1
        return True

    def finish(name):
        while advance(name):
            pass

    kernels = {
        "S": lambda: run_feed(0), "K": lambda: run_feed(1), "A": run_a, "B": run_b, "Q": run_q,
        "O": run_o, "L": run_l, "P": run_p,
    }
    for name in PLAN:
        if name in kernels:
            kernels[name]()
        else:
            advance(name)
    for name in "c3":
        finish(name)
    down_grad, up_grad, others = known["feed"]
    arrays = [x.reshape(pieces, 2, -1, width) for x in results["3"]]
    compress_grad, norms = results["c"]
    *attn_grads, gain_1, bias_1, gain_2, bias_2, grad_norm = place_squares(order, *arrays, others, norms)
    block_out, tokens_grad = known["block_out"], known["tokens_grad"]
    return (
        block_out,
        tokens_grad,
        gain_1,
        bias_1,
        *attn_grads,
        compress_grad,
        gain_2,
        bias_2,
        up_grad,
        down_grad,
        grad_norm.reshape(()),
    )


def solution(mesh):
    rows, held = P("dp", "krow", None), P("krow", None)
    in_specs = (rows, P("dp"), P(), P(), P(), P(), P(), P(), held, P(), P(), P(), P(), rows)
    out_specs = (rows, rows, P(), P(), P(), P(), P(), P(), held, P(), P(), P(), P(), P())
    return jax.shard_map(local, mesh=mesh, in_specs=in_specs, out_specs=out_specs, check_vma=False)
```

```python
import functools

import jax
import jax.numpy as jnp
from jax import lax
from jax.experimental import pallas as pl
from jax.experimental.pallas import tpu as pltpu
from jax.sharding import PartitionSpec as P

HEAD_DIM = 64
QUAD = 256
EPSILON = 1e-05
SCALE = HEAD_DIM ** (-0.5)
LOW = jnp.bfloat16
F32 = jnp.float32
COST = 3 * 10**9


def dot(left_side, right_side, contract):
    return lax.dot_general(
        left_side, right_side, (contract, ((), ())), preferred_element_type=F32
    )


def nn(left_side, right_side):
    return dot(left_side, right_side, ((1,), (0,)))


def nt(left_side, right_side):
    return dot(left_side, right_side, ((1,), (1,)))


def shape(dims, kind=LOW):
    return jax.ShapeDtypeStruct(dims, kind)


def far(dims, kind=LOW):
    return pltpu.HBM(dims, kind)


def kept_far(*values):
    return tuple(pltpu.with_memory_space_constraint(v, pltpu.HBM) for v in values)


def whole(*dims):
    return pl.BlockSpec(dims, lambda *_: (0,) * len(dims), pipeline_mode=pl.Buffered(1))


def result(*dims):
    return pl.BlockSpec(dims, lambda *_: (0,) * len(dims))


def vector(width):
    return pl.BlockSpec((width,), lambda *_: (0,))


def per_seq(*dims):
    return pl.BlockSpec((None, *dims), lambda s, *_: (s, *(0,) * len(dims)))


def call(body, grid, ins, outs, out_specs, in_specs, scratch=(), scalars=0, limit=24, cost=1):
    return pl.pallas_call(
        body,
        grid_spec=pltpu.PrefetchScalarGridSpec(
            num_scalar_prefetch=scalars,
            grid=grid,
            in_specs=in_specs,
            out_specs=out_specs,
            scratch_shapes=scratch,
        ),
        out_shape=outs,
        compiler_params=pltpu.CompilerParams(vmem_limit_bytes=limit << 20),
        name=getattr(body, "__name__", None) or body.func.__name__,
        cost_estimate=pl.CostEstimate(flops=cost * COST, bytes_accessed=1, transcendentals=0),
    )(*ins)


def row(ref):
    return ref[...].reshape(1, -1)


def centre(values):
    centred = values - jnp.mean(values, axis=-1, keepdims=True)
    spread = jnp.mean(centred * centred, axis=-1, keepdims=True)
    inverse = lax.rsqrt(spread + EPSILON)
    return centred * inverse, inverse


def normalize_back(grad, unit, inverse, gain):
    scaled = grad * gain
    return inverse * (
        scaled
        - jnp.mean(scaled, axis=-1, keepdims=True)
        - unit * jnp.mean(scaled * unit, axis=-1, keepdims=True)
    )


def enter_body(tokens, gain, bias, normed):
    unit, _ = centre(tokens[...].astype(F32))
    normed[...] = (unit * row(gain) + row(bias)).astype(LOW)


def enter(tokens, gain, bias):
    seqs, span, width = tokens.shape
    block = per_seq(span, width)
    return call(
        enter_body,
        (seqs,),
        (tokens, gain, bias),
        far(tokens.shape),
        block,
        [block, vector(width), vector(width)],
        limit=10,
        cost=1,
    )


def project_body(normed, weight, queries):
    queries[...] = (nn(normed[...], weight[...]) * SCALE).astype(LOW)


def project(normed, weight):
    seqs, span, width = normed.shape
    block = per_seq(span, width)
    return call(
        project_body,
        (seqs,),
        (normed, weight),
        far(normed.shape),
        block,
        [block, whole(width, width)],
        limit=10,
        cost=1,
    )


def grad_active_body(cotangent, down, out):
    out[...] = nt(cotangent[...], down[...]).astype(LOW)


def grad_active_of(cotangent, down):
    rows, width = cotangent.shape
    hidden = down.shape[0]
    cut = QUAD * 2
    return call(
        grad_active_body,
        (hidden // cut,),
        (cotangent, down),
        far((rows, hidden)),
        pl.BlockSpec((rows, cut), lambda i: (0, i)),
        [whole(rows, width), pl.BlockSpec((cut, width), lambda i: (i, 0))],
        limit=14,
        cost=5,
    )


def block_at(pair, own, order):
    return 2 * pair + (order[0] ^ 1 ^ own)


def block_out_body(order, down, attended, sent, kept, out):
    width = attended.shape[1]
    total = attended[...]
    for own, actives in enumerate((sent, kept)):
        for pair in range(actives.shape[0]):
            start = pl.multiple_of(block_at(pair, own, order) * width, width)
            total += nn(actives[pair], down[pl.ds(start, width), :])
    out[...] = total.astype(LOW)


def block_out_of(order, down, attended, *actives):
    seqs, span, width = attended.shape
    lines = pl.BlockSpec((actives[0].shape[0], span, width), lambda s, m: (0, s, 0))
    return call(
        block_out_body,
        (seqs,),
        (order, down, *kept_far(attended, *actives)),
        shape(attended.shape),
        per_seq(span, width),
        [whole(*down.shape), per_seq(span, width), *([lines] * len(actives))],
        scalars=1,
        limit=24,
        cost=6,
    )


def send_by_distance(me, value, held, kept, sent):
    pieces = 2 * kept.shape[0]
    cut = value.shape[0] // pieces
    held[...] = value
    for pair in range(pieces // 2):
        for other, out in enumerate((kept, sent)):
            start = pl.multiple_of(((2 * pair + other) ^ me) * cut, cut)
            out[pair] = held[pl.ds(start, cut), :].astype(LOW)


def take_by_distance(me, own, other, out):
    pieces = 2 * own.shape[0]
    cut = own.shape[1]
    for pair in range(pieces // 2):
        for at, source in enumerate((own, other)):
            start = pl.multiple_of(((2 * pair + at) ^ me) * cut, cut)
            out[pl.ds(start, cut), :] = source[pair]


def distance_rows(pairs, seqs, rows, width):
    return shape((pairs, seqs, rows // pairs // 2, width))


def distance_spec(pairs, rows, width):
    return pl.BlockSpec((pairs, None, rows // pairs // 2, width), lambda s, *_: (0, s, 0, 0))


def summarize_body(meta, columns, normed, kept, sent, held):
    seq = pl.program_id(0)
    rows, span = columns.shape
    at = meta[0] * span + lax.broadcasted_iota(jnp.int32, (rows, span), 1)
    masked = jnp.where(at < meta[1 + seq], columns[...].astype(F32), 0.0).astype(LOW)
    send_by_distance(meta[0], nn(masked, normed[...]), held, kept, sent)


def summarize(pairs, meta, columns, normed):
    seqs, span, width = normed.shape
    rows = columns.shape[0]
    return call(
        summarize_body,
        (seqs,),
        (meta, columns, normed),
        [distance_rows(pairs, seqs, rows, width)] * 2,
        [distance_spec(pairs, rows, width)] * 2,
        [whole(rows, span), per_seq(span, width)],
        [pltpu.VMEM((rows, width), F32)],
        scalars=1,
        limit=12,
        cost=2,
    )


def head_masks(dims, axis):
    lane = lax.broadcasted_iota(jnp.int32, dims, axis) // HEAD_DIM
    return [lane == h for h in range(QUAD // HEAD_DIM)]


def stack_heads(value, masks, axis):
    wide = value.astype(F32)
    return jnp.concatenate([jnp.where(m, wide, 0.0).astype(LOW) for m in masks], axis=axis)


def own_heads(stacked, masks, rows):
    parts = [stacked[h * rows : (h + 1) * rows] for h in range(len(masks))]
    out = jnp.where(masks[0], parts[0], 0.0)
    for mask, part in zip(masks[1:], parts[1:]):
        out = jnp.where(mask, part, out)
    return out


def attend_body(
    meta, tokens, queries, own, other, key_w, value_w, out_w, gain, bias,
    summary, keys, values, probs, mixed, attended, lifted, inverse_out,
):
    span, width = tokens.shape
    rows = summary.shape[0]
    take_by_distance(meta[0], own, other, summary)
    key_all = nn(summary[...], key_w[...]).astype(LOW)
    value_all = nn(summary[...], value_w[...]).astype(LOW)
    keys[...] = key_all
    values[...] = value_all
    side = head_masks((rows, QUAD), 1)
    turned = head_masks((QUAD, rows), 0)
    quads = []
    for q in range(width // QUAD):
        cut = slice(q * QUAD, (q + 1) * QUAD)
        scores = nt(stack_heads(key_all[:, cut], side, 0), queries[:, cut])
        lows = []
        for h in range(len(side)):
            part = scores[h * rows : (h + 1) * rows]
            grown = jnp.exp(part - jnp.max(part, axis=0, keepdims=True))
            lows.append((grown / jnp.sum(grown, axis=0, keepdims=True)).astype(LOW))
        low = jnp.concatenate(lows, axis=0)
        probs[q * low.shape[0] : (q + 1) * low.shape[0], :] = low
        quads.append(nn(stack_heads(value_all[:, cut].astype(F32).T, turned, 1), low).T)
    mixed_low = jnp.concatenate(quads, axis=1).astype(LOW)
    mixed[...] = mixed_low
    total = tokens[...].astype(F32) + nn(mixed_low, out_w[...])
    attended[...] = total
    unit, inverse = centre(total)
    inverse_out[...] = jnp.broadcast_to(inverse, inverse_out.shape)
    lifted[...] = (unit * row(gain) + row(bias)).astype(LOW)


def attend(meta, tokens, queries, own, other, key_w, value_w, out_w, gain, bias):
    seqs, span, width = tokens.shape
    pairs = own.shape[0]
    rows = 2 * pairs * own.shape[2]
    tall = (width // HEAD_DIM) * rows
    weight = whole(width, width)
    return call(
        attend_body,
        (seqs,),
        (meta, *kept_far(tokens, queries), own, other, key_w, value_w, out_w, gain, bias),
        [
            far((seqs, rows, width)),
            far((seqs, rows, width)),
            far((seqs, rows, width)),
            far((seqs, tall, span)),
            far((seqs, span, width)),
            far((seqs, span, width), F32),
            shape((seqs, span, width)),
            far((seqs, span, 128), F32),
        ],
        [
            per_seq(rows, width),
            per_seq(rows, width),
            per_seq(rows, width),
            per_seq(tall, span),
            per_seq(span, width),
            per_seq(span, width),
            per_seq(span, width),
            per_seq(span, 128),
        ],
        [
            per_seq(span, width),
            per_seq(span, width),
            distance_spec(pairs, rows, width),
            distance_spec(pairs, rows, width),
            weight,
            weight,
            weight,
            vector(width),
            vector(width),
        ],
        scalars=1,
        limit=32,
        cost=10,
    )


def feed_body(
    order, lifted, cotangent, grad_active, up, active_out, grad_out, down_grad, up_grad, turned
):
    @pl.when(pl.program_id(0) == 0)
    def _():
        turned[...] = lifted[...].T

    hidden = nn(lifted[...], up[...])
    share = 0.5 * (1.0 + lax.erf(hidden * 0.5**0.5))
    slope = share + hidden * jnp.exp(-0.5 * hidden * hidden) * 0.3989422804014327
    active = (hidden * share).astype(LOW)
    grad_hidden = (grad_active[...].astype(F32) * slope).astype(LOW)
    active_out[...] = active
    grad_out[...] = grad_hidden
    pieces, line = down_grad.shape[0], down_grad.shape[1]
    value = nn(active.T, cotangent[...])
    for piece in range(pieces):
        down_grad[piece ^ order[1]] = value[piece * line : (piece + 1) * line].astype(LOW)
    value = nn(turned[...], grad_hidden)
    line = up_grad.shape[1]
    for piece in range(pieces):
        up_grad[piece ^ order[2]] = value[piece * line : (piece + 1) * line].astype(LOW)


def feed(own, pieces, order, lifted, cotangent, grad_active, up):
    rows, width = lifted.shape
    steps = width // QUAD
    pairs = up.shape[1] // width // 2

    def columns(i, m):
        return (0, block_at(i // steps, own, m) * steps + i % steps)

    def lines(i, m):
        return (i // steps, 0, i % steps)

    return call(
        feed_body,
        (pairs * steps,),
        (order, lifted, cotangent, grad_active, up),
        [
            far((pairs, rows, width)),
            far((pairs, rows, width)),
            shape((pieces, pairs, steps, QUAD // pieces, width)),
            shape((pieces, pairs, width // pieces, width)),
        ],
        [
            pl.BlockSpec((None, rows, QUAD), lines),
            pl.BlockSpec((None, rows, QUAD), lines),
            pl.BlockSpec(
                (pieces, None, None, QUAD // pieces, width),
                lambda i, m: (0, i // steps, i % steps, 0, 0),
            ),
            pl.BlockSpec(
                (pieces, None, width // pieces, QUAD), lambda i, m: (0, i // steps, 0, i % steps)
            ),
        ],
        [
            whole(rows, width),
            whole(rows, width),
            pl.BlockSpec((rows, QUAD), columns),
            pl.BlockSpec((width, QUAD), columns),
        ],
        [pltpu.VMEM((width, rows), LOW)],
        scalars=1,
        limit=20,
        cost=6 * pairs,
    )


def feed_back_body(
    order, sent, kept, up, cotangent, attended, inverse, gain, out_w,
    grad_attended, grad_branch, grad_mixed, norm_grads,
):
    width = cotangent.shape[1]

    @pl.when(pl.program_id(0) == 0)
    def _():
        norm_grads[...] = jnp.zeros_like(norm_grads)

    total = attended[...]
    scale = inverse[:, :1]
    unit = (total - jnp.mean(total, axis=-1, keepdims=True)) * scale
    grad = 0.0
    for own, hiddens in enumerate((sent, kept)):
        for pair in range(hiddens.shape[0]):
            start = pl.multiple_of(block_at(pair, own, order) * width, width)
            grad += nt(hiddens[pair], up[:, pl.ds(start, width)])
    norm_grads[0:1, :] += jnp.sum(grad * unit, axis=0, keepdims=True)
    norm_grads[1:2, :] += jnp.sum(grad, axis=0, keepdims=True)
    whole_grad = cotangent[...].astype(F32) + normalize_back(grad, unit, scale, row(gain))
    grad_attended[...] = whole_grad
    branch = whole_grad.astype(LOW)
    grad_branch[...] = branch
    grad_mixed[...] = nt(branch, out_w[...]).astype(LOW)


def feed_back(order, hiddens, up, cotangent, attended, inverse, gain, out_w):
    seqs, span, width = cotangent.shape
    block = per_seq(span, width)
    lines = pl.BlockSpec((hiddens[0].shape[0], span, width), lambda s, *_: (0, s, 0))
    return call(
        feed_back_body,
        (seqs,),
        (
            order, *kept_far(*hiddens), up, *kept_far(cotangent, attended, inverse), gain, out_w,
        ),
        [
            far((seqs, span, width), F32),
            far((seqs, span, width)),
            far((seqs, span, width)),
            shape((8, width), F32),
        ],
        [block, block, block, result(8, width)],
        [
            *([lines] * len(hiddens)), whole(*up.shape), block, block, per_seq(span, 128),
            vector(width), whole(width, width),
        ],
        scalars=1,
        limit=24,
        cost=8,
    )


def attend_back_body(
    meta, grad_mixed, queries, keys, values, probs, key_w, value_w,
    grad_queries, grad_keys, grad_values, kept, sent, held,
):
    span, width = grad_mixed.shape
    rows = keys.shape[0]
    side = head_masks((rows, QUAD), 1)
    turned = head_masks((QUAD, rows), 0)
    for q in range(width // QUAD):
        cut = slice(q * QUAD, (q + 1) * QUAD)
        mixed_cut = grad_mixed[:, cut]
        tall = len(side) * rows
        low = probs[q * tall : (q + 1) * tall, :]
        grad_probs = nt(stack_heads(values[:, cut], side, 0), mixed_cut)
        lows = []
        for h in range(len(side)):
            part = low[h * rows : (h + 1) * rows].astype(F32)
            ours = grad_probs[h * rows : (h + 1) * rows]
            inner = jnp.sum(part * ours, axis=0, keepdims=True)
            lows.append((part * (ours - inner)).astype(LOW))
        grad_scores = jnp.concatenate(lows, axis=0)
        grad_values[:, cut] = own_heads(nn(low, mixed_cut), side, rows).astype(LOW)
        grad_keys[:, cut] = own_heads(nn(grad_scores, queries[:, cut]), side, rows).astype(LOW)
        keys_turned = stack_heads(keys[:, cut].astype(F32).T, turned, 1)
        grad_queries[:, cut] = (nn(keys_turned, grad_scores) * SCALE).T.astype(LOW)
    grad_summary = nt(grad_keys[...], key_w[...]) + nt(grad_values[...], value_w[...])
    send_by_distance(meta[0], grad_summary, held, kept, sent)


def attend_back(pairs, meta, grad_mixed, queries, keys, values, probs, key_w, value_w):
    seqs, span, width = grad_mixed.shape
    rows = keys.shape[1]
    tall = probs.shape[1]
    weight = whole(width, width)
    block, rows_block = per_seq(span, width), per_seq(rows, width)
    distance = distance_spec(pairs, rows, width)
    return call(
        attend_back_body,
        (seqs,),
        (meta, *kept_far(grad_mixed, queries, keys, values, probs), key_w, value_w),
        [
            far((seqs, span, width)),
            far((seqs, rows, width)),
            far((seqs, rows, width)),
            distance_rows(pairs, seqs, rows, width),
            distance_rows(pairs, seqs, rows, width),
        ],
        [block, rows_block, rows_block, distance, distance],
        [block, block, rows_block, rows_block, per_seq(tall, span), weight, weight],
        [pltpu.VMEM((rows, width), F32)],
        scalars=1,
        limit=24,
        cost=14,
    )


def squares_body(
    order, normed, summary, mixed, grad_queries, grad_keys, grad_values, grad_branch,
    sent_1, sent_2, kept_1, kept_2, normed_t, summary_t, mixed_t,
):
    @pl.when(pl.program_id(0) == 0)
    def _():
        normed_t[...] = normed[...].T
        summary_t[...] = summary[...].T
        mixed_t[...] = mixed[...].T

    pieces = sent_1.shape[0]
    half = normed_t.shape[0] // 2
    members = (
        (normed_t, grad_queries, (sent_1, kept_1), 0, order[1]),
        (summary_t, grad_keys, (sent_1, kept_1), 1, order[1]),
        (summary_t, grad_values, (sent_2, kept_2), 0, order[2]),
        (mixed_t, grad_branch, (sent_2, kept_2), 1, order[2]),
    )
    for left, right, outs, at, mask in members:
        for out, side in zip(outs, (1 - order[0], order[0])):
            start = pl.multiple_of(side * half, half)
            value = nn(left[pl.ds(start, half), :], right[...])
            cut = half // pieces
            for piece in range(pieces):
                out[piece ^ mask, at] = value[piece * cut : (piece + 1) * cut].astype(LOW)


def squares(
    pieces, order, normed, summary, mixed, grad_queries, grad_keys, grad_values, grad_branch
):
    rows, width = normed.shape
    tall = summary.shape[0]
    cut = QUAD
    line = width // 2 // pieces
    return call(
        squares_body,
        (width // cut,),
        (
            order, normed, summary, mixed,
            *kept_far(grad_queries, grad_keys, grad_values, grad_branch),
        ),
        [shape((pieces, 2, line, width))] * 4,
        [pl.BlockSpec((pieces, 2, line, cut), lambda i, m: (0, 0, 0, i))] * 4,
        [
            whole(rows, width),
            whole(tall, width),
            whole(rows, width),
            pl.BlockSpec((rows, cut), lambda i, m: (0, i)),
            pl.BlockSpec((tall, cut), lambda i, m: (0, i)),
            pl.BlockSpec((tall, cut), lambda i, m: (0, i)),
            pl.BlockSpec((rows, cut), lambda i, m: (0, i)),
        ],
        [
            pltpu.VMEM((width, rows), LOW),
            pltpu.VMEM((width, tall), LOW),
            pltpu.VMEM((width, rows), LOW),
        ],
        scalars=1,
        limit=24,
        cost=7,
    )


def place_feed_body(order, own_down, other_down, own_up, other_up, down, up, total):
    pair, side = pl.program_id(0), pl.program_id(1)
    ours = (side ^ order[0]) == 0

    @pl.when((pair == 0) & (side == 0))
    def _():
        total[...] = jnp.zeros_like(total)

    def place(down_in, up_in):
        pieces, _, steps, line, _ = down_in.shape
        tall = up_in.shape[2]

        def one(piece, square):
            for step in range(steps):
                value = down_in[piece ^ order[1], pair, step].astype(F32)
                start = pl.multiple_of(step * pieces * line + piece * line, line)
                down[pl.ds(start, line), :] = value
                square += jnp.sum(value * value, axis=0, keepdims=True)
            value = up_in[piece ^ order[2], pair].astype(F32)
            up[pl.ds(pl.multiple_of(piece * tall, tall), tall), :] = value
            return square + jnp.sum(value * value, axis=0, keepdims=True)

        total[0:1, :] += lax.fori_loop(0, pieces, one, jnp.zeros((1, down.shape[1]), F32))

    pl.when(ours)(lambda: place(own_down, own_up))
    pl.when(jnp.logical_not(ours))(lambda: place(other_down, other_up))


def place_feed(order, down_shape, up_shape, *arrays):
    width = down_shape[1]
    return call(
        place_feed_body,
        (down_shape[0] // width // 2, 2),
        (order, *arrays),
        [shape(down_shape, F32), shape(up_shape, F32), shape((8, width), F32)],
        [
            pl.BlockSpec((width, width), lambda h, i, m: (2 * h + i, 0)),
            pl.BlockSpec((width, width), lambda h, i, m: (0, 2 * h + i)),
            result(8, width),
        ],
        [whole(*x.shape) for x in arrays],
        scalars=1,
        limit=28,
        cost=8,
    )


def place_squares_body(order, *refs):
    inputs, (others, norms, *outs), total = refs[:8], refs[8:-1], refs[-1]
    *outs, attn_gain, attn_bias, ffn_gain, ffn_bias, norm = outs
    side = pl.program_id(0)
    ours = (side ^ order[0]) == 0

    @pl.when(side == 0)
    def _():
        total[...] = others[...]

    def place(first, second):
        count, _, line, width = first[0].shape
        square = jnp.zeros((1, width), F32)
        for at in range(2 * count):
            for source, mask, pair in ((first, order[1], outs[:2]), (second, order[2], outs[2:])):
                start = pl.multiple_of((at ^ mask) * line, line)
                for member, out in enumerate(pair):
                    value = source[at // count][at % count, member].astype(F32)
                    out[pl.ds(start, line), :] = value
                    square += jnp.sum(value * value, axis=0, keepdims=True)
        total[0:1, :] += square

    pl.when(ours)(lambda: place(inputs[:2], inputs[4:6]))
    pl.when(jnp.logical_not(ours))(lambda: place(inputs[2:4], inputs[6:]))

    @pl.when(side == 1)
    def _():
        value = norms[...].astype(F32)
        square = jnp.sum(total[0:1, :], keepdims=True) + jnp.sum(value * value, keepdims=True)
        span = value.shape[1]
        cuts = attn_gain.shape[0] // span
        for at, out in enumerate((attn_gain, attn_bias, ffn_gain, ffn_bias)):
            for cut in range(cuts):
                line = value[at * cuts + cut : at * cuts + cut + 1]
                out[cut * span : (cut + 1) * span] = line.reshape(span)
        norm[...] = jnp.sqrt(square)


def place_squares(order, others, norms, *arrays):
    count, _, line, width = arrays[0].shape
    return call(
        place_squares_body,
        (2,),
        (order, *arrays, others, norms),
        [shape((4 * count * line, width), F32)] * 4
        + [shape((width,), F32)] * 4
        + [shape((1, 1), F32)],
        [pl.BlockSpec((2 * count * line, width), lambda i, m: (i, 0))] * 4
        + [result(width)] * 4
        + [result(1, 1)],
        [whole(*x.shape) for x in (*arrays, others, norms)],
        [pltpu.VMEM(others.shape, F32)],
        scalars=1,
        limit=24,
        cost=5,
    )


def leave_body(
    meta, own, other, columns, normed, tokens, gain, grad_queries, query_w, grad_attended,
    ffn_norms, tokens_grad, packed, columns_t, terms_sum, norm_grads, grad_summary,
):
    seq = pl.program_id(0)
    rows, span = columns.shape

    @pl.when(seq == 0)
    def _():
        columns_t[...] = columns[...].T
        terms_sum[...] = jnp.zeros_like(terms_sum)
        norm_grads[...] = jnp.zeros_like(norm_grads)

    take_by_distance(meta[0], own, other, grad_summary)
    length = meta[1 + seq] - meta[0] * span
    lane = lax.broadcasted_iota(jnp.int32, (rows, span), 1) < length
    line = lax.broadcasted_iota(jnp.int32, (span, 1), 0) < length
    summed = grad_summary[...]
    terms_sum[...] += jnp.where(lane, nt(summed, normed[...]), 0.0)
    grad = nt(grad_queries[...], query_w[...]) + jnp.where(line, nn(columns_t[...], summed), 0.0)
    unit, inverse = centre(tokens[...].astype(F32))
    norm_grads[0:1, :] += jnp.sum(grad * unit, axis=0, keepdims=True)
    norm_grads[1:2, :] += jnp.sum(grad, axis=0, keepdims=True)
    tokens_grad[...] = (
        grad_attended[...] + normalize_back(grad, unit, inverse, row(gain))
    ).astype(LOW)

    @pl.when(seq == pl.num_programs(0) - 1)
    def _():
        total = terms_sum[...].astype(LOW)
        width = norm_grads.shape[1]
        lines = [
            source[at : at + 1, cut : cut + span]
            for source in (norm_grads, ffn_norms)
            for at in range(2)
            for cut in range(0, width, span)
        ]
        share, tall = rows // packed.shape[0], packed.shape[1]
        lines.append(jnp.zeros((tall - share - len(lines), span), F32))
        norms = jnp.concatenate(lines, axis=0).astype(LOW)
        for at in range(packed.shape[0]):
            packed[at, :share, :] = total[at * share : (at + 1) * share]
            packed[at, share:, :] = norms


def leave(
    ring, meta, own, other, columns, normed, tokens, gain, grad_queries, query_w, grad_attended,
    ffn_norms,
):
    seqs, span, width = tokens.shape
    rows = columns.shape[0]
    distance = distance_spec(own.shape[0], rows, width)
    tall = rows // ring + -(-4 * width // span // 16) * 16
    block = per_seq(span, width)
    return call(
        leave_body,
        (seqs,),
        (
            meta, own, other, columns, *kept_far(normed, tokens), gain, *kept_far(grad_queries), query_w,
            *kept_far(grad_attended), ffn_norms,
        ),
        [shape(tokens.shape), shape((ring, tall, span))],
        [block, result(ring, tall, span)],
        [
            distance, distance, whole(rows, span), block, block, vector(width), block,
            whole(width, width), block, whole(8, width),
        ],
        [
            pltpu.VMEM((span, rows), LOW),
            pltpu.VMEM((rows, span), F32),
            pltpu.VMEM((8, width), F32),
            pltpu.VMEM((rows, width), LOW),
        ],
        scalars=1,
        limit=20,
        cost=5,
    )


def swap(value, axis, mask):
    size = lax.axis_size(axis)
    return lax.ppermute(value, axis, [(i, i ^ mask) for i in range(size)])


def pick(value, at):
    return lax.dynamic_index_in_dim(value, at, 0, keepdims=False)


def bits_of(axis):
    return (lax.axis_size(axis) - 1).bit_length()


def bit(axis, at):
    return (lax.axis_index(axis) >> at) & 1


def after(values, ticket):
    return lax.optimization_barrier((values, ticket))[0]


def in_order(mine, other, at):
    return jnp.where(at == 0, jnp.stack([mine, other]), jnp.stack([other, mine]))


def krow_orders():
    count = bits_of("krow")
    return [list(range(1, count)), list(range(count - 1, 0, -1))]


def distance_masks():
    count = bits_of("krow")
    masks = [bit("krow", 0)]
    for order in krow_orders():
        masks.append(sum(bit("krow", at) << (count - 2 - d) for d, at in enumerate(order)))
    return jnp.stack(masks).astype(jnp.int32)


def sum_everywhere(sent, halved, parted):
    orders = krow_orders()
    flight = [swap(x, "krow", 1) for x in sent]
    kept = yield sent
    ticket = yield kept
    for digit in range(len(orders[0])):
        flight, kept = after((flight, kept), ticket)
        half = kept[0].shape[0] // 2
        sent = [k[half:] + f[half:] for k, f in zip(kept, flight)]
        kept = [k[:half] + f[:half] for k, f in zip(kept, flight)]
        flight = [swap(x, "krow", 1 << o[digit]) for x, o in zip(sent, orders)]
        ticket = yield (sent, kept)
    flight, kept = after((flight, kept), ticket)
    values = [(k + f)[0] for k, f in zip(kept, flight)]
    count = bits_of("dp")
    strides = [list(range(count)), list(range(count - 1, -1, -1))]
    sides = [bit("dp", stride[0]) for stride in strides]
    for stage in range(count):
        sent = kept = values
        if stage < halved:
            halves = [v.reshape(2, -1, v.shape[-1]) for v in values]
            sent = [pick(h, 1 - side) for h, side in zip(halves, sides)]
            kept = [pick(h, side) for h, side in zip(halves, sides)]
        flight = [swap(x, "dp", 1 << o[stage]) for x, o in zip(sent, strides)]
        ticket = yield (sent, kept)
        flight, kept = after((flight, kept), ticket)
        values = [k + f for k, f in zip(kept, flight)]
    if halved:
        flight = [swap(x, "dp", 1 << o[0]) for x, o in zip(values, strides)]
        ticket = yield values
        flight, values = after((flight, values), ticket)
        values = [
            in_order(v, f, side).reshape(-1, v.shape[-1])
            for v, f, side in zip(values, flight, sides)
        ]
    values = [v[None] for v in values]
    for digit in reversed(range(1, len(orders[0]))):
        flight = [swap(v, "krow", 1 << o[digit]) for v, o in zip(values, orders)]
        ticket = yield values
        flight, values = after((flight, values), ticket)
        values = [jnp.concatenate([v, f]) for v, f in zip(values, flight)]
    early = [swap(v, "krow", 1) for v in values] if parted else []
    flight = [swap(v, "krow", 1 << o[0]) for v, o in zip(values, orders)]
    ticket = yield values
    flight, values, early = after((flight, values, early), ticket)
    if parted:
        late = [swap(f, "krow", 1) for f in flight]
        ticket = yield (flight, values, early)
        yield after([x for color in zip(values, flight, early, late) for x in color], ticket)
    else:
        values = [jnp.concatenate([v, f]) for v, f in zip(values, flight)]
        flight = [swap(v, "krow", 1) for v in values]
        ticket = yield values
        yield after([x for color in zip(values, flight) for x in color], ticket)


def sum_krow(sent, kept):
    pairs = kept.shape[0]
    flight = swap(sent, "krow", 1)
    ticket = yield kept
    kept, flight = after((kept, flight), ticket)
    half = [k.astype(F32) + f.astype(F32) for k, f in zip(kept, flight)]
    sent = [h.astype(LOW) for h in half[1:]]
    flight = [swap(x, "krow", 2 * pair) for pair, x in enumerate(sent, 1)]
    kept = half[0]
    ticket = yield (kept, sent)
    kept, flight = after((kept, flight), ticket)
    total = sum([f.astype(F32) for f in flight], kept).astype(LOW)
    flight = [swap(total, "krow", 2 * pair) for pair in range(1, pairs)]
    ticket = yield total
    total, flight = after((total, flight), ticket)
    own = jnp.stack([total, *flight])
    flight = swap(own, "krow", 1)
    ticket = yield own
    yield after((own, flight), ticket)


def sum_terms(packed, share):
    span = packed.shape[2]
    flight = lax.all_to_all(packed, "krow", 0, 0, tiled=True)
    ticket = yield packed
    flight = after(flight, ticket)
    norms = jnp.sum(flight[:, share:].astype(F32), axis=0).astype(LOW)
    value = jnp.concatenate([flight[:, :share].reshape(-1, span), norms])
    for at in range(bits_of("dp")):
        flight = swap(value, "dp", 1 << at)
        ticket = yield value
        flight, value = after((flight, value), ticket)
        value = value + flight
    norms, value = value[packed.shape[0] * share :], value.astype(F32)
    ring = packed.shape[0]
    rows = ring * share
    compress = value[:rows].reshape(ring, share, span).transpose(1, 0, 2).reshape(share, -1)
    yield (compress, norms)


class Line:
    def __init__(self, ticket):
        self.ticket = ticket

    def step(self, *sums):
        for each in sums:
            self.ticket = each.send(self.ticket)

    def run(self, kernel, *values):
        self.ticket = kernel(*after(values, self.ticket))
        return self.ticket


    def start(self, steps, *first):
        self.ticket = (self.ticket, next(steps))
        for value in first:
            self.ticket = (self.ticket, steps.send(value))
        return steps


PLAN = "S1K1AB1gQ1gg31O13gL313c31c3c3c311P33"
HALVED = {"1": 1, "3": 1}


def local(
    tokens,
    lengths,
    attn_gain,
    attn_bias,
    query_weight,
    key_weight,
    value_weight,
    out_weight,
    compress,
    ffn_gain,
    ffn_bias,
    up_weight,
    down_weight,
    cotangent,
):
    seqs, span, width = tokens.shape
    ring = lax.axis_size("krow")
    rows = compress.shape[0] * ring
    pairs = pieces = ring // 2
    flat, tall = (seqs * span, width), (seqs * rows, width)
    order = distance_masks()
    meta = jnp.concatenate([lax.axis_index("krow")[None].astype(jnp.int32), lengths])
    columns = lax.all_to_all(
        compress.reshape(compress.shape[0], ring, span), "krow", 1, 0, tiled=False
    ).reshape(rows, span)
    cotangent_flat = cotangent.reshape(flat)
    normed = enter(tokens, attn_gain, attn_bias)
    kept, sent = summarize(pairs, meta, columns, normed)
    line = Line((kept, sent))
    summing = line.start(sum_krow(sent, kept))
    line.step(summing)
    grad_active = line.run(grad_active_of, cotangent_flat, down_weight)
    line.step(summing)
    queries = line.run(project, normed, query_weight)
    line.step(summing, summing)
    summary, keys, values, probs, mixed, attended, lifted, inverse = attend(
        meta, tokens, queries, *line.ticket, key_weight, value_weight, out_weight, ffn_gain,
        ffn_bias,
    )
    line.ticket = lifted

    def as_pieces(arrays):
        return [x.reshape(pieces, -1, width) for x in arrays]

    known, sums, results = {}, {}, {}

    def run_feed(own):
        name = ("sent", "kept")[own]
        known[f"active_{name}"], known[f"hidden_{name}"], *known[f"{name}_1"] = line.run(
            lambda lifted: feed(
                own, pieces, order, lifted.reshape(flat), cotangent_flat, grad_active, up_weight
            ),
            lifted,
        )

    def run_a():
        known["grad_attended"], known["grad_branch"], known["grad_mixed"], known["ffn_norms"] = (
            line.run(
                lambda *hiddens: feed_back(
                    order, hiddens, up_weight, cotangent, attended, inverse, ffn_gain, out_weight
                ),
                known["hidden_sent"],
                known["hidden_kept"],
            )
        )

    def run_b():
        *known["grads"], known["kept_g"], known["sent_g"] = line.run(
            lambda grad_mixed: attend_back(
                pairs, meta, grad_mixed, queries, keys, values, probs, key_weight, value_weight
            ),
            known["grad_mixed"],
        )

    def run_q():
        out = line.run(
            lambda branch, grad_queries, grad_keys, grad_values: squares(
                pieces, order, normed.reshape(flat), summary.reshape(tall), mixed.reshape(flat),
                grad_queries.reshape(flat), grad_keys.reshape(tall), grad_values.reshape(tall),
                branch.reshape(flat),
            ),
            known["grad_branch"],
            *known["grads"],
        )
        known["sent_3"], known["kept_3"] = out[:2], out[2:]

    def run_o():
        known["block_out"] = line.run(
            lambda *actives: block_out_of(order, down_weight, attended, *actives),
            known["active_sent"],
            known["active_kept"],
        )

    def run_l():
        finish("g")
        known["tokens_grad"], known["terms"] = line.run(
            lambda own, other: leave(
                ring, meta, own, other, columns, normed, tokens, attn_gain, known["grads"][0],
                query_weight, known["grad_attended"], known["ffn_norms"],
            ),
            *results["g"],
        )

    def run_p():
        finish("1")
        pairs_held = down_weight.shape[0] // width // 2
        steps = width // QUAD
        forms = ((pieces, pairs_held, steps, QUAD // pieces, width), (pieces, pairs_held, -1, width))
        arrays = [x.reshape(forms[at // 2]) for at, x in enumerate(results["1"])]
        known["feed"] = line.run(
            lambda *arrays: place_feed(order, down_weight.shape, up_weight.shape, *arrays),
            *arrays,
        )

    def begin(name):
        if name == "g":
            return sum_krow(known["sent_g"], known["kept_g"])
        if name == "c":
            return sum_terms(known["terms"], rows // ring)
        return sum_everywhere(as_pieces(known[f"sent_{name}"]), HALVED[name], name == "3")

    def advance(name):
        if name not in sums:
            sums[name] = [begin(name), 0]
            with jax.named_scope(f"sum_{name}_0"):
                line.start(sums[name][0])
        else:
            if sums[name][1] == 1 and name in HALVED:
                sums[name][0].send(as_pieces(known[f"kept_{name}"]))
            try:
                with jax.named_scope(f"sum_{name}_{sums[name][1]}"):
                    line.step(sums[name][0])
                results[name] = line.ticket
            except StopIteration:
                return False
        sums[name][1] += 1
        return True

    def finish(name):
        while advance(name):
            pass

    kernels = {
        "S": lambda: run_feed(0), "K": lambda: run_feed(1), "A": run_a, "B": run_b, "Q": run_q,
        "O": run_o, "L": run_l, "P": run_p,
    }
    for name in PLAN:
        if name in kernels:
            kernels[name]()
        else:
            advance(name)
    for name in "c3":
        finish(name)
    down_grad, up_grad, others = known["feed"]
    arrays = [x.reshape(pieces // 2, 2, -1, width) for x in results["3"]]
    compress_grad, norms = results["c"]
    *attn_grads, gain_1, bias_1, gain_2, bias_2, grad_norm = place_squares(
        order, others, norms, *arrays
    )
    block_out, tokens_grad = known["block_out"], known["tokens_grad"]
    return (
        block_out,
        tokens_grad,
        gain_1,
        bias_1,
        *attn_grads,
        compress_grad,
        gain_2,
        bias_2,
        up_grad,
        down_grad,
        grad_norm.reshape(()),
    )


def solution(mesh):
    rows, held = P("dp", "krow", None), P("krow", None)
    in_specs = (rows, P("dp"), P(), P(), P(), P(), P(), P(), held, P(), P(), P(), P(), rows)
    out_specs = (rows, rows, P(), P(), P(), P(), P(), P(), held, P(), P(), P(), P(), P())
    return jax.shard_map(local, mesh=mesh, in_specs=in_specs, out_specs=out_specs, check_vma=False)
```

```python
import functools

import jax
import jax.numpy as jnp
from jax import lax
from jax.experimental import pallas as pl
from jax.experimental.pallas import tpu as pltpu
from jax.sharding import PartitionSpec as P

HEAD_DIM = 64
QUAD = 256
EPSILON = 1e-05
SCALE = HEAD_DIM ** (-0.5)
LOW = jnp.bfloat16
F32 = jnp.float32
COST = 3 * 10**9


def dot(left_side, right_side, contract):
    return lax.dot_general(
        left_side, right_side, (contract, ((), ())), preferred_element_type=F32
    )


def nn(left_side, right_side):
    return dot(left_side, right_side, ((1,), (0,)))


def nt(left_side, right_side):
    return dot(left_side, right_side, ((1,), (1,)))


def shape(dims, kind=LOW):
    return jax.ShapeDtypeStruct(dims, kind)


def far(dims, kind=LOW):
    return pltpu.HBM(dims, kind)


def kept_far(*values):
    return tuple(pltpu.with_memory_space_constraint(v, pltpu.HBM) for v in values)


def whole(*dims):
    return pl.BlockSpec(dims, lambda *_: (0,) * len(dims), pipeline_mode=pl.Buffered(1))


def result(*dims):
    return pl.BlockSpec(dims, lambda *_: (0,) * len(dims))


def vector(width):
    return pl.BlockSpec((width,), lambda *_: (0,))


def per_seq(*dims):
    return pl.BlockSpec((None, *dims), lambda s, *_: (s, *(0,) * len(dims)))


def call(body, grid, ins, outs, out_specs, in_specs, scratch=(), scalars=0, limit=24, cost=1):
    return pl.pallas_call(
        body,
        grid_spec=pltpu.PrefetchScalarGridSpec(
            num_scalar_prefetch=scalars,
            grid=grid,
            in_specs=in_specs,
            out_specs=out_specs,
            scratch_shapes=scratch,
        ),
        out_shape=outs,
        compiler_params=pltpu.CompilerParams(vmem_limit_bytes=limit << 20),
        name=getattr(body, "__name__", None) or body.func.__name__,
        cost_estimate=pl.CostEstimate(flops=cost * COST, bytes_accessed=1, transcendentals=0),
    )(*ins)


def row(ref):
    return ref[...].reshape(1, -1)


def centre(values):
    centred = values - jnp.mean(values, axis=-1, keepdims=True)
    spread = jnp.mean(centred * centred, axis=-1, keepdims=True)
    inverse = lax.rsqrt(spread + EPSILON)
    return centred * inverse, inverse


def normalize_back(grad, unit, inverse, gain):
    scaled = grad * gain
    return inverse * (
        scaled
        - jnp.mean(scaled, axis=-1, keepdims=True)
        - unit * jnp.mean(scaled * unit, axis=-1, keepdims=True)
    )


def enter_body(tokens, gain, bias, normed):
    unit, _ = centre(tokens[...].astype(F32))
    normed[...] = (unit * row(gain) + row(bias)).astype(LOW)


def enter(tokens, gain, bias):
    seqs, span, width = tokens.shape
    block = per_seq(span, width)
    return call(
        enter_body,
        (seqs,),
        (tokens, gain, bias),
        shape(tokens.shape),
        block,
        [block, vector(width), vector(width)],
        limit=10,
        cost=1,
    )


def project_body(normed, weight, queries):
    queries[...] = (nn(normed[...], weight[...]) * SCALE).astype(LOW)


def project(normed, weight):
    seqs, span, width = normed.shape
    block = per_seq(span, width)
    return call(
        project_body,
        (seqs,),
        (normed, weight),
        shape(normed.shape),
        block,
        [block, whole(width, width)],
        limit=10,
        cost=1,
    )


def grad_active_body(cotangent, down, out):
    out[...] = nt(cotangent[...], down[...]).astype(LOW)


def grad_active_of(cotangent, down):
    rows, width = cotangent.shape
    hidden = down.shape[0]
    cut = QUAD * 2
    return call(
        grad_active_body,
        (hidden // cut,),
        (cotangent, down),
        far((rows, hidden)),
        pl.BlockSpec((rows, cut), lambda i: (0, i)),
        [whole(rows, width), pl.BlockSpec((cut, width), lambda i: (i, 0))],
        limit=14,
        cost=5,
    )


def block_at(pair, own, order):
    return 2 * pair + (order[0] ^ 1 ^ own)


def block_out_body(order, down, attended, sent, kept, out):
    width = attended.shape[1]
    total = attended[...]
    for own, actives in enumerate((sent, kept)):
        for pair in range(actives.shape[0]):
            start = pl.multiple_of(block_at(pair, own, order) * width, width)
            total += nn(actives[pair], down[pl.ds(start, width), :])
    out[...] = total.astype(LOW)


def block_out_of(order, down, attended, *actives):
    seqs, span, width = attended.shape
    lines = pl.BlockSpec((actives[0].shape[0], span, width), lambda s, m: (0, s, 0))
    return call(
        block_out_body,
        (seqs,),
        (order, down, *kept_far(attended, *actives)),
        shape(attended.shape),
        per_seq(span, width),
        [whole(*down.shape), per_seq(span, width), *([lines] * len(actives))],
        scalars=1,
        limit=24,
        cost=6,
    )


def send_by_distance(me, value, held, kept, sent):
    pieces = 2 * kept.shape[0]
    cut = value.shape[0] // pieces
    held[...] = value
    for pair in range(pieces // 2):
        for other, out in enumerate((kept, sent)):
            start = pl.multiple_of(((2 * pair + other) ^ me) * cut, cut)
            out[pair] = held[pl.ds(start, cut), :].astype(LOW)


def take_by_distance(me, own, other, out):
    pieces = 2 * own.shape[0]
    cut = own.shape[1]
    for pair in range(pieces // 2):
        for at, source in enumerate((own, other)):
            start = pl.multiple_of(((2 * pair + at) ^ me) * cut, cut)
            out[pl.ds(start, cut), :] = source[pair]


def distance_rows(pairs, seqs, rows, width):
    return shape((pairs, seqs, rows // pairs // 2, width))


def distance_spec(pairs, rows, width):
    return pl.BlockSpec((pairs, None, rows // pairs // 2, width), lambda s, *_: (0, s, 0, 0))


def summarize_body(meta, columns, normed, kept, sent, held):
    seq = pl.program_id(0)
    rows, span = columns.shape
    at = meta[0] * span + lax.broadcasted_iota(jnp.int32, (rows, span), 1)
    masked = jnp.where(at < meta[1 + seq], columns[...].astype(F32), 0.0).astype(LOW)
    send_by_distance(meta[0], nn(masked, normed[...]), held, kept, sent)


def summarize(pairs, meta, columns, normed):
    seqs, span, width = normed.shape
    rows = columns.shape[0]
    return call(
        summarize_body,
        (seqs,),
        (meta, columns, normed),
        [distance_rows(pairs, seqs, rows, width)] * 2,
        [distance_spec(pairs, rows, width)] * 2,
        [whole(rows, span), per_seq(span, width)],
        [pltpu.VMEM((rows, width), F32)],
        scalars=1,
        limit=12,
        cost=2,
    )


def head_masks(dims, axis):
    lane = lax.broadcasted_iota(jnp.int32, dims, axis) // HEAD_DIM
    return [lane == h for h in range(QUAD // HEAD_DIM)]


def stack_heads(value, masks, axis):
    wide = value.astype(F32)
    return jnp.concatenate([jnp.where(m, wide, 0.0).astype(LOW) for m in masks], axis=axis)


def own_heads(stacked, masks, rows):
    parts = [stacked[h * rows : (h + 1) * rows] for h in range(len(masks))]
    out = jnp.where(masks[0], parts[0], 0.0)
    for mask, part in zip(masks[1:], parts[1:]):
        out = jnp.where(mask, part, out)
    return out


def attend_body(
    meta, tokens, queries, own, other, key_w, value_w, out_w, gain, bias,
    summary, keys, values, probs, mixed, attended, lifted, inverse_out,
):
    span, width = tokens.shape
    rows = summary.shape[0]
    take_by_distance(meta[0], own, other, summary)
    key_all = nn(summary[...], key_w[...]).astype(LOW)
    value_all = nn(summary[...], value_w[...]).astype(LOW)
    keys[...] = key_all
    values[...] = value_all
    side = head_masks((rows, QUAD), 1)
    turned = head_masks((QUAD, rows), 0)
    quads = []
    for q in range(width // QUAD):
        cut = slice(q * QUAD, (q + 1) * QUAD)
        scores = nt(stack_heads(key_all[:, cut], side, 0), queries[:, cut])
        lows = []
        for h in range(len(side)):
            part = scores[h * rows : (h + 1) * rows]
            grown = jnp.exp(part - jnp.max(part, axis=0, keepdims=True))
            lows.append((grown / jnp.sum(grown, axis=0, keepdims=True)).astype(LOW))
        low = jnp.concatenate(lows, axis=0)
        probs[q * low.shape[0] : (q + 1) * low.shape[0], :] = low
        quads.append(nn(stack_heads(value_all[:, cut].astype(F32).T, turned, 1), low).T)
    mixed_low = jnp.concatenate(quads, axis=1).astype(LOW)
    mixed[...] = mixed_low
    total = tokens[...].astype(F32) + nn(mixed_low, out_w[...])
    attended[...] = total
    unit, inverse = centre(total)
    inverse_out[...] = jnp.broadcast_to(inverse, inverse_out.shape)
    lifted[...] = (unit * row(gain) + row(bias)).astype(LOW)


def attend(meta, tokens, queries, own, other, key_w, value_w, out_w, gain, bias):
    seqs, span, width = tokens.shape
    pairs = own.shape[0]
    rows = 2 * pairs * own.shape[2]
    tall = (width // HEAD_DIM) * rows
    weight = whole(width, width)
    return call(
        attend_body,
        (seqs,),
        (meta, *kept_far(tokens, queries), own, other, key_w, value_w, out_w, gain, bias),
        [
            far((seqs, rows, width)),
            far((seqs, rows, width)),
            far((seqs, rows, width)),
            far((seqs, tall, span)),
            far((seqs, span, width)),
            far((seqs, span, width), F32),
            shape((seqs, span, width)),
            far((seqs, span, 128), F32),
        ],
        [
            per_seq(rows, width),
            per_seq(rows, width),
            per_seq(rows, width),
            per_seq(tall, span),
            per_seq(span, width),
            per_seq(span, width),
            per_seq(span, width),
            per_seq(span, 128),
        ],
        [
            per_seq(span, width),
            per_seq(span, width),
            distance_spec(pairs, rows, width),
            distance_spec(pairs, rows, width),
            weight,
            weight,
            weight,
            vector(width),
            vector(width),
        ],
        scalars=1,
        limit=32,
        cost=10,
    )


def feed_body(
    order, lifted, cotangent, grad_active, up, active_out, grad_out, down_grad, up_grad, turned
):
    @pl.when(pl.program_id(0) == 0)
    def _():
        turned[...] = lifted[...].T

    hidden = nn(lifted[...], up[...])
    share = 0.5 * (1.0 + lax.erf(hidden * 0.5**0.5))
    slope = share + hidden * jnp.exp(-0.5 * hidden * hidden) * 0.3989422804014327
    active = (hidden * share).astype(LOW)
    grad_hidden = (grad_active[...].astype(F32) * slope).astype(LOW)
    active_out[...] = active
    grad_out[...] = grad_hidden
    pieces, line = down_grad.shape[0], down_grad.shape[1]
    value = nn(active.T, cotangent[...])
    for piece in range(pieces):
        down_grad[piece ^ order[1]] = value[piece * line : (piece + 1) * line].astype(LOW)
    value = nn(turned[...], grad_hidden)
    line = up_grad.shape[1]
    for piece in range(pieces):
        up_grad[piece ^ order[2]] = value[piece * line : (piece + 1) * line].astype(LOW)


def feed(own, pieces, order, lifted, cotangent, grad_active, up):
    rows, width = lifted.shape
    steps = width // QUAD
    pairs = up.shape[1] // width // 2

    def columns(i, m):
        return (0, block_at(i // steps, own, m) * steps + i % steps)

    def lines(i, m):
        return (i // steps, 0, i % steps)

    return call(
        feed_body,
        (pairs * steps,),
        (order, lifted, cotangent, grad_active, up),
        [
            far((pairs, rows, width)),
            far((pairs, rows, width)),
            shape((pieces, pairs, steps, QUAD // pieces, width)),
            shape((pieces, pairs, width // pieces, width)),
        ],
        [
            pl.BlockSpec((None, rows, QUAD), lines),
            pl.BlockSpec((None, rows, QUAD), lines),
            pl.BlockSpec(
                (pieces, None, None, QUAD // pieces, width),
                lambda i, m: (0, i // steps, i % steps, 0, 0),
            ),
            pl.BlockSpec(
                (pieces, None, width // pieces, QUAD), lambda i, m: (0, i // steps, 0, i % steps)
            ),
        ],
        [
            whole(rows, width),
            whole(rows, width),
            pl.BlockSpec((rows, QUAD), columns),
            pl.BlockSpec((width, QUAD), columns),
        ],
        [pltpu.VMEM((width, rows), LOW)],
        scalars=1,
        limit=20,
        cost=6 * pairs,
    )


def feed_back_body(
    order, sent, kept, up, cotangent, attended, inverse, gain, out_w,
    grad_attended, grad_branch, grad_mixed, norm_grads,
):
    width = cotangent.shape[1]

    @pl.when(pl.program_id(0) == 0)
    def _():
        norm_grads[...] = jnp.zeros_like(norm_grads)

    total = attended[...]
    scale = inverse[:, :1]
    unit = (total - jnp.mean(total, axis=-1, keepdims=True)) * scale
    grad = 0.0
    for own, hiddens in enumerate((sent, kept)):
        for pair in range(hiddens.shape[0]):
            start = pl.multiple_of(block_at(pair, own, order) * width, width)
            grad += nt(hiddens[pair], up[:, pl.ds(start, width)])
    norm_grads[0:1, :] += jnp.sum(grad * unit, axis=0, keepdims=True)
    norm_grads[1:2, :] += jnp.sum(grad, axis=0, keepdims=True)
    whole_grad = cotangent[...].astype(F32) + normalize_back(grad, unit, scale, row(gain))
    grad_attended[...] = whole_grad
    branch = whole_grad.astype(LOW)
    grad_branch[...] = branch
    grad_mixed[...] = nt(branch, out_w[...]).astype(LOW)


def feed_back(order, hiddens, up, cotangent, attended, inverse, gain, out_w):
    seqs, span, width = cotangent.shape
    block = per_seq(span, width)
    lines = pl.BlockSpec((hiddens[0].shape[0], span, width), lambda s, *_: (0, s, 0))
    return call(
        feed_back_body,
        (seqs,),
        (
            order, *kept_far(*hiddens), up, *kept_far(cotangent, attended, inverse), gain, out_w,
        ),
        [
            far((seqs, span, width), F32),
            far((seqs, span, width)),
            far((seqs, span, width)),
            shape((8, width), F32),
        ],
        [block, block, block, result(8, width)],
        [
            *([lines] * len(hiddens)), whole(*up.shape), block, block, per_seq(span, 128),
            vector(width), whole(width, width),
        ],
        scalars=1,
        limit=24,
        cost=8,
    )


def attend_back_body(
    meta, grad_mixed, queries, keys, values, probs, key_w, value_w,
    grad_queries, grad_keys, grad_values, kept, sent, held,
):
    span, width = grad_mixed.shape
    rows = keys.shape[0]
    side = head_masks((rows, QUAD), 1)
    turned = head_masks((QUAD, rows), 0)
    for q in range(width // QUAD):
        cut = slice(q * QUAD, (q + 1) * QUAD)
        mixed_cut = grad_mixed[:, cut]
        tall = len(side) * rows
        low = probs[q * tall : (q + 1) * tall, :]
        grad_probs = nt(stack_heads(values[:, cut], side, 0), mixed_cut)
        lows = []
        for h in range(len(side)):
            part = low[h * rows : (h + 1) * rows].astype(F32)
            ours = grad_probs[h * rows : (h + 1) * rows]
            inner = jnp.sum(part * ours, axis=0, keepdims=True)
            lows.append((part * (ours - inner)).astype(LOW))
        grad_scores = jnp.concatenate(lows, axis=0)
        grad_values[:, cut] = own_heads(nn(low, mixed_cut), side, rows).astype(LOW)
        grad_keys[:, cut] = own_heads(nn(grad_scores, queries[:, cut]), side, rows).astype(LOW)
        keys_turned = stack_heads(keys[:, cut].astype(F32).T, turned, 1)
        grad_queries[:, cut] = (nn(keys_turned, grad_scores) * SCALE).T.astype(LOW)
    grad_summary = nt(grad_keys[...], key_w[...]) + nt(grad_values[...], value_w[...])
    send_by_distance(meta[0], grad_summary, held, kept, sent)


def attend_back(pairs, meta, grad_mixed, queries, keys, values, probs, key_w, value_w):
    seqs, span, width = grad_mixed.shape
    rows = keys.shape[1]
    tall = probs.shape[1]
    weight = whole(width, width)
    block, rows_block = per_seq(span, width), per_seq(rows, width)
    distance = distance_spec(pairs, rows, width)
    return call(
        attend_back_body,
        (seqs,),
        (meta, *kept_far(grad_mixed, queries, keys, values, probs), key_w, value_w),
        [
            far((seqs, span, width)),
            far((seqs, rows, width)),
            far((seqs, rows, width)),
            distance_rows(pairs, seqs, rows, width),
            distance_rows(pairs, seqs, rows, width),
        ],
        [block, rows_block, rows_block, distance, distance],
        [block, block, rows_block, rows_block, per_seq(tall, span), weight, weight],
        [pltpu.VMEM((rows, width), F32)],
        scalars=1,
        limit=24,
        cost=14,
    )


def squares_body(
    order, normed, summary, mixed, grad_queries, grad_keys, grad_values, grad_branch,
    sent_1, sent_2, kept_1, kept_2, normed_t, summary_t, mixed_t,
):
    @pl.when(pl.program_id(0) == 0)
    def _():
        normed_t[...] = normed[...].T
        summary_t[...] = summary[...].T
        mixed_t[...] = mixed[...].T

    pieces = sent_1.shape[0]
    half = normed_t.shape[0] // 2
    members = (
        (normed_t, grad_queries, (sent_1, kept_1), 0, order[1]),
        (summary_t, grad_keys, (sent_1, kept_1), 1, order[1]),
        (summary_t, grad_values, (sent_2, kept_2), 0, order[2]),
        (mixed_t, grad_branch, (sent_2, kept_2), 1, order[2]),
    )
    for left, right, outs, at, mask in members:
        for out, side in zip(outs, (1 - order[0], order[0])):
            start = pl.multiple_of(side * half, half)
            value = nn(left[pl.ds(start, half), :], right[...])
            cut = half // pieces
            for piece in range(pieces):
                out[piece ^ mask, at] = value[piece * cut : (piece + 1) * cut].astype(LOW)


def squares(
    pieces, order, normed, summary, mixed, grad_queries, grad_keys, grad_values, grad_branch
):
    rows, width = normed.shape
    tall = summary.shape[0]
    cut = QUAD
    line = width // 2 // pieces
    return call(
        squares_body,
        (width // cut,),
        (
            order, normed, summary, mixed,
            *kept_far(grad_queries, grad_keys, grad_values, grad_branch),
        ),
        [shape((pieces, 2, line, width))] * 4,
        [pl.BlockSpec((pieces, 2, line, cut), lambda i, m: (0, 0, 0, i))] * 4,
        [
            whole(rows, width),
            whole(tall, width),
            whole(rows, width),
            pl.BlockSpec((rows, cut), lambda i, m: (0, i)),
            pl.BlockSpec((tall, cut), lambda i, m: (0, i)),
            pl.BlockSpec((tall, cut), lambda i, m: (0, i)),
            pl.BlockSpec((rows, cut), lambda i, m: (0, i)),
        ],
        [
            pltpu.VMEM((width, rows), LOW),
            pltpu.VMEM((width, tall), LOW),
            pltpu.VMEM((width, rows), LOW),
        ],
        scalars=1,
        limit=24,
        cost=7,
    )


def place_feed_body(order, own_down, other_down, own_up, other_up, down, up, total):
    pair, side = pl.program_id(0), pl.program_id(1)
    ours = (side ^ order[0]) == 0

    @pl.when((pair == 0) & (side == 0))
    def _():
        total[...] = jnp.zeros_like(total)

    def place(down_in, up_in):
        pieces, _, steps, line, _ = down_in.shape
        tall = up_in.shape[2]

        def one(piece, square):
            for step in range(steps):
                value = down_in[piece ^ order[1], pair, step].astype(F32)
                start = pl.multiple_of(step * pieces * line + piece * line, line)
                down[pl.ds(start, line), :] = value
                square += jnp.sum(value * value, axis=0, keepdims=True)
            value = up_in[piece ^ order[2], pair].astype(F32)
            up[pl.ds(pl.multiple_of(piece * tall, tall), tall), :] = value
            return square + jnp.sum(value * value, axis=0, keepdims=True)

        total[0:1, :] += lax.fori_loop(0, pieces, one, jnp.zeros((1, down.shape[1]), F32))

    pl.when(ours)(lambda: place(own_down, own_up))
    pl.when(jnp.logical_not(ours))(lambda: place(other_down, other_up))


def place_feed(order, down_shape, up_shape, *arrays):
    width = down_shape[1]
    return call(
        place_feed_body,
        (down_shape[0] // width // 2, 2),
        (order, *arrays),
        [shape(down_shape, F32), shape(up_shape, F32), shape((8, width), F32)],
        [
            pl.BlockSpec((width, width), lambda h, i, m: (2 * h + i, 0)),
            pl.BlockSpec((width, width), lambda h, i, m: (0, 2 * h + i)),
            result(8, width),
        ],
        [whole(*x.shape) for x in arrays],
        scalars=1,
        limit=28,
        cost=8,
    )


def place_squares_body(order, *refs):
    inputs, (others, norms, *outs), total = refs[:8], refs[8:-1], refs[-1]
    *outs, attn_gain, attn_bias, ffn_gain, ffn_bias, norm = outs
    side = pl.program_id(0)
    ours = (side ^ order[0]) == 0

    @pl.when(side == 0)
    def _():
        total[...] = others[...]

    def place(first, second):
        count, _, line, width = first[0].shape
        square = jnp.zeros((1, width), F32)
        for at in range(2 * count):
            for source, mask, pair in ((first, order[1], outs[:2]), (second, order[2], outs[2:])):
                start = pl.multiple_of((at ^ mask) * line, line)
                for member, out in enumerate(pair):
                    value = source[at // count][at % count, member].astype(F32)
                    out[pl.ds(start, line), :] = value
                    square += jnp.sum(value * value, axis=0, keepdims=True)
        total[0:1, :] += square

    pl.when(ours)(lambda: place(inputs[:2], inputs[4:6]))
    pl.when(jnp.logical_not(ours))(lambda: place(inputs[2:4], inputs[6:]))

    @pl.when(side == 1)
    def _():
        value = norms[...].astype(F32)
        square = jnp.sum(total[0:1, :], keepdims=True) + jnp.sum(value * value, keepdims=True)
        span = value.shape[1]
        cuts = attn_gain.shape[0] // span
        for at, out in enumerate((attn_gain, attn_bias, ffn_gain, ffn_bias)):
            for cut in range(cuts):
                line = value[at * cuts + cut : at * cuts + cut + 1]
                out[cut * span : (cut + 1) * span] = line.reshape(span)
        norm[...] = jnp.sqrt(square)


def place_squares(order, others, norms, *arrays):
    count, _, line, width = arrays[0].shape
    return call(
        place_squares_body,
        (2,),
        (order, *arrays, others, norms),
        [shape((4 * count * line, width), F32)] * 4
        + [shape((width,), F32)] * 4
        + [shape((1, 1), F32)],
        [pl.BlockSpec((2 * count * line, width), lambda i, m: (i, 0))] * 4
        + [result(width)] * 4
        + [result(1, 1)],
        [whole(*x.shape) for x in (*arrays, others, norms)],
        [pltpu.VMEM(others.shape, F32)],
        scalars=1,
        limit=24,
        cost=5,
    )


def leave_body(
    meta, own, other, columns, normed, tokens, gain, grad_queries, query_w, grad_attended,
    ffn_norms, tokens_grad, packed, columns_t, terms_sum, norm_grads, grad_summary,
):
    seq = pl.program_id(0)
    rows, span = columns.shape

    @pl.when(seq == 0)
    def _():
        columns_t[...] = columns[...].T
        terms_sum[...] = jnp.zeros_like(terms_sum)
        norm_grads[...] = jnp.zeros_like(norm_grads)

    take_by_distance(meta[0], own, other, grad_summary)
    length = meta[1 + seq] - meta[0] * span
    lane = lax.broadcasted_iota(jnp.int32, (rows, span), 1) < length
    line = lax.broadcasted_iota(jnp.int32, (span, 1), 0) < length
    summed = grad_summary[...]
    terms_sum[...] += jnp.where(lane, nt(summed, normed[...]), 0.0)
    grad = nt(grad_queries[...], query_w[...]) + jnp.where(line, nn(columns_t[...], summed), 0.0)
    unit, inverse = centre(tokens[...].astype(F32))
    norm_grads[0:1, :] += jnp.sum(grad * unit, axis=0, keepdims=True)
    norm_grads[1:2, :] += jnp.sum(grad, axis=0, keepdims=True)
    tokens_grad[...] = (
        grad_attended[...] + normalize_back(grad, unit, inverse, row(gain))
    ).astype(LOW)

    @pl.when(seq == pl.num_programs(0) - 1)
    def _():
        total = terms_sum[...].astype(LOW)
        width = norm_grads.shape[1]
        lines = [
            source[at : at + 1, cut : cut + span]
            for source in (norm_grads, ffn_norms)
            for at in range(2)
            for cut in range(0, width, span)
        ]
        share, tall = rows // packed.shape[0], packed.shape[1]
        lines.append(jnp.zeros((tall - share - len(lines), span), F32))
        norms = jnp.concatenate(lines, axis=0).astype(LOW)
        for at in range(packed.shape[0]):
            packed[at, :share, :] = total[at * share : (at + 1) * share]
            packed[at, share:, :] = norms


def leave(
    ring, meta, own, other, columns, normed, tokens, gain, grad_queries, query_w, grad_attended,
    ffn_norms,
):
    seqs, span, width = tokens.shape
    rows = columns.shape[0]
    distance = distance_spec(own.shape[0], rows, width)
    tall = rows // ring + -(-4 * width // span // 16) * 16
    block = per_seq(span, width)
    return call(
        leave_body,
        (seqs,),
        (
            meta, own, other, columns, *kept_far(normed, tokens), gain, *kept_far(grad_queries), query_w,
            *kept_far(grad_attended), ffn_norms,
        ),
        [shape(tokens.shape), shape((ring, tall, span))],
        [block, result(ring, tall, span)],
        [
            distance, distance, whole(rows, span), block, block, vector(width), block,
            whole(width, width), block, whole(8, width),
        ],
        [
            pltpu.VMEM((span, rows), LOW),
            pltpu.VMEM((rows, span), F32),
            pltpu.VMEM((8, width), F32),
            pltpu.VMEM((rows, width), LOW),
        ],
        scalars=1,
        limit=20,
        cost=5,
    )


def swap(value, axis, mask):
    size = lax.axis_size(axis)
    return lax.ppermute(value, axis, [(i, i ^ mask) for i in range(size)])


def pick(value, at):
    return lax.dynamic_index_in_dim(value, at, 0, keepdims=False)


def bits_of(axis):
    return (lax.axis_size(axis) - 1).bit_length()


def bit(axis, at):
    return (lax.axis_index(axis) >> at) & 1


def after(values, ticket):
    return lax.optimization_barrier((values, ticket))[0]


def in_order(mine, other, at):
    return jnp.where(at == 0, jnp.stack([mine, other]), jnp.stack([other, mine]))


def krow_orders():
    count = bits_of("krow")
    return [list(range(1, count)), list(range(count - 1, 0, -1))]


def distance_masks():
    count = bits_of("krow")
    masks = [bit("krow", 0)]
    for order in krow_orders():
        masks.append(sum(bit("krow", at) << (count - 2 - d) for d, at in enumerate(order)))
    return jnp.stack(masks).astype(jnp.int32)


def sum_everywhere(sent, halved, parted):
    orders = krow_orders()
    flight = [swap(x, "krow", 1) for x in sent]
    kept = yield sent
    ticket = yield kept
    for digit in range(len(orders[0])):
        flight, kept = after((flight, kept), ticket)
        half = kept[0].shape[0] // 2
        sent = [k[half:] + f[half:] for k, f in zip(kept, flight)]
        kept = [k[:half] + f[:half] for k, f in zip(kept, flight)]
        flight = [swap(x, "krow", 1 << o[digit]) for x, o in zip(sent, orders)]
        ticket = yield (sent, kept)
    flight, kept = after((flight, kept), ticket)
    values = [(k + f)[0] for k, f in zip(kept, flight)]
    count = bits_of("dp")
    strides = [list(range(count)), list(range(count - 1, -1, -1))]
    sides = [bit("dp", stride[0]) for stride in strides]
    for stage in range(count):
        sent = kept = values
        if stage < halved:
            halves = [v.reshape(2, -1, v.shape[-1]) for v in values]
            sent = [pick(h, 1 - side) for h, side in zip(halves, sides)]
            kept = [pick(h, side) for h, side in zip(halves, sides)]
        flight = [swap(x, "dp", 1 << o[stage]) for x, o in zip(sent, strides)]
        ticket = yield (sent, kept)
        flight, kept = after((flight, kept), ticket)
        values = [k + f for k, f in zip(kept, flight)]
    if halved:
        flight = [swap(x, "dp", 1 << o[0]) for x, o in zip(values, strides)]
        ticket = yield values
        flight, values = after((flight, values), ticket)
        values = [
            in_order(v, f, side).reshape(-1, v.shape[-1])
            for v, f, side in zip(values, flight, sides)
        ]
    values = [v[None] for v in values]
    for digit in reversed(range(1, len(orders[0]))):
        flight = [swap(v, "krow", 1 << o[digit]) for v, o in zip(values, orders)]
        ticket = yield values
        flight, values = after((flight, values), ticket)
        values = [jnp.concatenate([v, f]) for v, f in zip(values, flight)]
    early = [swap(v, "krow", 1) for v in values] if parted else []
    flight = [swap(v, "krow", 1 << o[0]) for v, o in zip(values, orders)]
    ticket = yield values
    flight, values, early = after((flight, values, early), ticket)
    if parted:
        late = [swap(f, "krow", 1) for f in flight]
        ticket = yield (flight, values, early)
        yield after([x for color in zip(values, flight, early, late) for x in color], ticket)
    else:
        values = [jnp.concatenate([v, f]) for v, f in zip(values, flight)]
        flight = [swap(v, "krow", 1) for v in values]
        ticket = yield values
        yield after([x for color in zip(values, flight) for x in color], ticket)


def sum_krow(sent, kept):
    pairs = kept.shape[0]
    flight = swap(sent, "krow", 1)
    ticket = yield kept
    kept, flight = after((kept, flight), ticket)
    half = [k.astype(F32) + f.astype(F32) for k, f in zip(kept, flight)]
    sent = [h.astype(LOW) for h in half[1:]]
    flight = [swap(x, "krow", 2 * pair) for pair, x in enumerate(sent, 1)]
    kept = half[0]
    ticket = yield (kept, sent)
    kept, flight = after((kept, flight), ticket)
    total = sum([f.astype(F32) for f in flight], kept).astype(LOW)
    flight = [swap(total, "krow", 2 * pair) for pair in range(1, pairs)]
    ticket = yield total
    total, flight = after((total, flight), ticket)
    own = jnp.stack([total, *flight])
    flight = swap(own, "krow", 1)
    ticket = yield own
    yield after((own, flight), ticket)


def sum_terms(packed, share):
    span = packed.shape[2]
    flight = lax.all_to_all(packed, "krow", 0, 0, tiled=True)
    ticket = yield packed
    flight = after(flight, ticket)
    norms = jnp.sum(flight[:, share:].astype(F32), axis=0).astype(LOW)
    value = jnp.concatenate([flight[:, :share].reshape(-1, span), norms])
    for at in range(bits_of("dp")):
        flight = swap(value, "dp", 1 << at)
        ticket = yield value
        flight, value = after((flight, value), ticket)
        value = value + flight
    norms, value = value[packed.shape[0] * share :], value.astype(F32)
    ring = packed.shape[0]
    rows = ring * share
    compress = value[:rows].reshape(ring, share, span).transpose(1, 0, 2).reshape(share, -1)
    yield (compress, norms)


class Line:
    def __init__(self, ticket):
        self.ticket = ticket

    def step(self, *sums):
        for each in sums:
            self.ticket = each.send(self.ticket)

    def run(self, kernel, *values):
        self.ticket = kernel(*after(values, self.ticket))
        return self.ticket


    def start(self, steps, *first):
        self.ticket = (self.ticket, next(steps))
        for value in first:
            self.ticket = (self.ticket, steps.send(value))
        return steps


PLAN = "S1K1AB1gQ1gg31O13gL313c31c3c3c311P33"
HALVED = {"1": 1, "3": 1}


def local(
    tokens,
    lengths,
    attn_gain,
    attn_bias,
    query_weight,
    key_weight,
    value_weight,
    out_weight,
    compress,
    ffn_gain,
    ffn_bias,
    up_weight,
    down_weight,
    cotangent,
):
    seqs, span, width = tokens.shape
    ring = lax.axis_size("krow")
    rows = compress.shape[0] * ring
    pairs = pieces = ring // 2
    flat, tall = (seqs * span, width), (seqs * rows, width)
    order = distance_masks()
    meta = jnp.concatenate([lax.axis_index("krow")[None].astype(jnp.int32), lengths])
    columns = lax.all_to_all(
        compress.reshape(compress.shape[0], ring, span), "krow", 1, 0, tiled=False
    ).reshape(rows, span)
    cotangent_flat = cotangent.reshape(flat)
    normed = enter(tokens, attn_gain, attn_bias)
    kept, sent = summarize(pairs, meta, columns, normed)
    line = Line((kept, sent))
    summing = line.start(sum_krow(sent, kept))
    line.step(summing)
    grad_active = line.run(grad_active_of, cotangent_flat, down_weight)
    line.step(summing)
    queries = line.run(project, normed, query_weight)
    line.step(summing, summing)
    summary, keys, values, probs, mixed, attended, lifted, inverse = attend(
        meta, tokens, queries, *line.ticket, key_weight, value_weight, out_weight, ffn_gain,
        ffn_bias,
    )
    line.ticket = lifted

    def as_pieces(arrays):
        return [x.reshape(pieces, -1, width) for x in arrays]

    known, sums, results = {}, {}, {}

    def run_feed(own):
        name = ("sent", "kept")[own]
        known[f"active_{name}"], known[f"hidden_{name}"], *known[f"{name}_1"] = line.run(
            lambda lifted: feed(
                own, pieces, order, lifted.reshape(flat), cotangent_flat, grad_active, up_weight
            ),
            lifted,
        )

    def run_a():
        known["grad_attended"], known["grad_branch"], known["grad_mixed"], known["ffn_norms"] = (
            line.run(
                lambda *hiddens: feed_back(
                    order, hiddens, up_weight, cotangent, attended, inverse, ffn_gain, out_weight
                ),
                known["hidden_sent"],
                known["hidden_kept"],
            )
        )

    def run_b():
        *known["grads"], known["kept_g"], known["sent_g"] = line.run(
            lambda grad_mixed: attend_back(
                pairs, meta, grad_mixed, queries, keys, values, probs, key_weight, value_weight
            ),
            known["grad_mixed"],
        )

    def run_q():
        out = line.run(
            lambda branch, grad_queries, grad_keys, grad_values: squares(
                pieces, order, normed.reshape(flat), summary.reshape(tall), mixed.reshape(flat),
                grad_queries.reshape(flat), grad_keys.reshape(tall), grad_values.reshape(tall),
                branch.reshape(flat),
            ),
            known["grad_branch"],
            *known["grads"],
        )
        known["sent_3"], known["kept_3"] = out[:2], out[2:]

    def run_o():
        known["block_out"] = line.run(
            lambda *actives: block_out_of(order, down_weight, attended, *actives),
            known["active_sent"],
            known["active_kept"],
        )

    def run_l():
        finish("g")
        known["tokens_grad"], known["terms"] = line.run(
            lambda own, other: leave(
                ring, meta, own, other, columns, normed, tokens, attn_gain, known["grads"][0],
                query_weight, known["grad_attended"], known["ffn_norms"],
            ),
            *results["g"],
        )

    def run_p():
        finish("1")
        pairs_held = down_weight.shape[0] // width // 2
        steps = width // QUAD
        forms = ((pieces, pairs_held, steps, QUAD // pieces, width), (pieces, pairs_held, -1, width))
        arrays = [x.reshape(forms[at // 2]) for at, x in enumerate(results["1"])]
        known["feed"] = line.run(
            lambda *arrays: place_feed(order, down_weight.shape, up_weight.shape, *arrays),
            *arrays,
        )

    def begin(name):
        if name == "g":
            return sum_krow(known["sent_g"], known["kept_g"])
        if name == "c":
            return sum_terms(known["terms"], rows // ring)
        return sum_everywhere(as_pieces(known[f"sent_{name}"]), HALVED[name], name == "3")

    def advance(name):
        if name not in sums:
            sums[name] = [begin(name), 0]
            with jax.named_scope(f"sum_{name}_0"):
                line.start(sums[name][0])
        else:
            if sums[name][1] == 1 and name in HALVED:
                sums[name][0].send(as_pieces(known[f"kept_{name}"]))
            try:
                with jax.named_scope(f"sum_{name}_{sums[name][1]}"):
                    line.step(sums[name][0])
                results[name] = line.ticket
            except StopIteration:
                return False
        sums[name][1] += 1
        return True

    def finish(name):
        while advance(name):
            pass

    kernels = {
        "S": lambda: run_feed(0), "K": lambda: run_feed(1), "A": run_a, "B": run_b, "Q": run_q,
        "O": run_o, "L": run_l, "P": run_p,
    }
    for name in PLAN:
        if name in kernels:
            kernels[name]()
        else:
            advance(name)
    for name in "c3":
        finish(name)
    down_grad, up_grad, others = known["feed"]
    arrays = [x.reshape(pieces // 2, 2, -1, width) for x in results["3"]]
    compress_grad, norms = results["c"]
    *attn_grads, gain_1, bias_1, gain_2, bias_2, grad_norm = place_squares(
        order, others, norms, *arrays
    )
    block_out, tokens_grad = known["block_out"], known["tokens_grad"]
    return (
        block_out,
        tokens_grad,
        gain_1,
        bias_1,
        *attn_grads,
        compress_grad,
        gain_2,
        bias_2,
        up_grad,
        down_grad,
        grad_norm.reshape(()),
    )


def solution(mesh):
    rows, held = P("dp", "krow", None), P("krow", None)
    in_specs = (rows, P("dp"), P(), P(), P(), P(), P(), P(), held, P(), P(), P(), P(), rows)
    out_specs = (rows, rows, P(), P(), P(), P(), P(), P(), held, P(), P(), P(), P(), P())
    return jax.shard_map(local, mesh=mesh, in_specs=in_specs, out_specs=out_specs, check_vma=False)
```

```python
import functools

import jax
import jax.numpy as jnp
from jax import lax
from jax.experimental import pallas as pl
from jax.experimental.pallas import tpu as pltpu
from jax.sharding import PartitionSpec as P

HEAD_DIM = 64
QUAD = 256
EPSILON = 1e-05
SCALE = HEAD_DIM ** (-0.5)
LOW = jnp.bfloat16
F32 = jnp.float32
COST = 3 * 10**9


def dot(left_side, right_side, contract):
    return lax.dot_general(
        left_side, right_side, (contract, ((), ())), preferred_element_type=F32
    )


def nn(left_side, right_side):
    return dot(left_side, right_side, ((1,), (0,)))


def nt(left_side, right_side):
    return dot(left_side, right_side, ((1,), (1,)))


def shape(dims, kind=LOW):
    return jax.ShapeDtypeStruct(dims, kind)


def far(dims, kind=LOW):
    return pltpu.HBM(dims, kind)


def kept_far(*values):
    return tuple(pltpu.with_memory_space_constraint(v, pltpu.HBM) for v in values)


def whole(*dims):
    return pl.BlockSpec(dims, lambda *_: (0,) * len(dims), pipeline_mode=pl.Buffered(1))


def result(*dims):
    return pl.BlockSpec(dims, lambda *_: (0,) * len(dims))


def vector(width):
    return pl.BlockSpec((width,), lambda *_: (0,))


def per_seq(*dims):
    return pl.BlockSpec((None, *dims), lambda s, *_: (s, *(0,) * len(dims)))


def call(body, grid, ins, outs, out_specs, in_specs, scratch=(), scalars=0, limit=24, cost=1):
    return pl.pallas_call(
        body,
        grid_spec=pltpu.PrefetchScalarGridSpec(
            num_scalar_prefetch=scalars,
            grid=grid,
            in_specs=in_specs,
            out_specs=out_specs,
            scratch_shapes=scratch,
        ),
        out_shape=outs,
        compiler_params=pltpu.CompilerParams(vmem_limit_bytes=limit << 20),
        name=getattr(body, "__name__", None) or body.func.__name__,
        cost_estimate=pl.CostEstimate(flops=cost * COST, bytes_accessed=1, transcendentals=0),
    )(*ins)


def row(ref):
    return ref[...].reshape(1, -1)


def centre(values):
    centred = values - jnp.mean(values, axis=-1, keepdims=True)
    spread = jnp.mean(centred * centred, axis=-1, keepdims=True)
    inverse = lax.rsqrt(spread + EPSILON)
    return centred * inverse, inverse


def normalize_back(grad, unit, inverse, gain):
    scaled = grad * gain
    return inverse * (
        scaled
        - jnp.mean(scaled, axis=-1, keepdims=True)
        - unit * jnp.mean(scaled * unit, axis=-1, keepdims=True)
    )


def enter_body(tokens, gain, bias, normed):
    unit, _ = centre(tokens[...].astype(F32))
    normed[...] = (unit * row(gain) + row(bias)).astype(LOW)


def enter(tokens, gain, bias):
    seqs, span, width = tokens.shape
    block = per_seq(span, width)
    return call(
        enter_body,
        (seqs,),
        (tokens, gain, bias),
        shape(tokens.shape),
        block,
        [block, vector(width), vector(width)],
        limit=10,
        cost=1,
    )


def project_body(normed, weight, queries):
    queries[...] = (nn(normed[...], weight[...]) * SCALE).astype(LOW)


def project(normed, weight):
    seqs, span, width = normed.shape
    block = per_seq(span, width)
    return call(
        project_body,
        (seqs,),
        (normed, weight),
        shape(normed.shape),
        block,
        [block, whole(width, width)],
        limit=10,
        cost=1,
    )


def grad_active_body(cotangent, down, out):
    out[...] = nt(cotangent[...], down[...]).astype(LOW)


def grad_active_of(cotangent, down):
    rows, width = cotangent.shape
    hidden = down.shape[0]
    cut = QUAD * 2
    return call(
        grad_active_body,
        (hidden // cut,),
        (cotangent, down),
        far((rows, hidden)),
        pl.BlockSpec((rows, cut), lambda i: (0, i)),
        [whole(rows, width), pl.BlockSpec((cut, width), lambda i: (i, 0))],
        limit=14,
        cost=5,
    )


def block_at(pair, own, order):
    return 2 * pair + (order[0] ^ 1 ^ own)


def block_out_body(order, down, attended, sent, kept, out):
    width = attended.shape[1]
    total = attended[...]
    for own, actives in enumerate((sent, kept)):
        for pair in range(actives.shape[0]):
            start = pl.multiple_of(block_at(pair, own, order) * width, width)
            total += nn(actives[pair], down[pl.ds(start, width), :])
    out[...] = total.astype(LOW)


def block_out_of(order, down, attended, *actives):
    seqs, span, width = attended.shape
    lines = pl.BlockSpec((actives[0].shape[0], span, width), lambda s, m: (0, s, 0))
    return call(
        block_out_body,
        (seqs,),
        (order, down, *kept_far(attended, *actives)),
        shape(attended.shape),
        per_seq(span, width),
        [whole(*down.shape), per_seq(span, width), *([lines] * len(actives))],
        scalars=1,
        limit=24,
        cost=6,
    )


def send_by_distance(me, value, held, kept, sent):
    pieces = 2 * kept.shape[0]
    cut = value.shape[0] // pieces
    held[...] = value
    for pair in range(pieces // 2):
        for other, out in enumerate((kept, sent)):
            start = pl.multiple_of(((2 * pair + other) ^ me) * cut, cut)
            out[pair] = held[pl.ds(start, cut), :].astype(LOW)


def take_by_distance(me, own, other, out):
    pieces = 2 * own.shape[0]
    cut = own.shape[1]
    for pair in range(pieces // 2):
        for at, source in enumerate((own, other)):
            start = pl.multiple_of(((2 * pair + at) ^ me) * cut, cut)
            out[pl.ds(start, cut), :] = source[pair]


def distance_rows(pairs, seqs, rows, width):
    return shape((pairs, seqs, rows // pairs // 2, width))


def distance_spec(pairs, rows, width):
    return pl.BlockSpec((pairs, None, rows // pairs // 2, width), lambda s, *_: (0, s, 0, 0))


def summarize_body(meta, columns, normed, kept, sent, held):
    seq = pl.program_id(0)
    rows, span = columns.shape
    at = meta[0] * span + lax.broadcasted_iota(jnp.int32, (rows, span), 1)
    masked = jnp.where(at < meta[1 + seq], columns[...].astype(F32), 0.0).astype(LOW)
    send_by_distance(meta[0], nn(masked, normed[...]), held, kept, sent)


def summarize(pairs, meta, columns, normed):
    seqs, span, width = normed.shape
    rows = columns.shape[0]
    return call(
        summarize_body,
        (seqs,),
        (meta, columns, normed),
        [distance_rows(pairs, seqs, rows, width)] * 2,
        [distance_spec(pairs, rows, width)] * 2,
        [whole(rows, span), per_seq(span, width)],
        [pltpu.VMEM((rows, width), F32)],
        scalars=1,
        limit=12,
        cost=2,
    )


def head_masks(dims, axis):
    lane = lax.broadcasted_iota(jnp.int32, dims, axis) // HEAD_DIM
    return [lane == h for h in range(QUAD // HEAD_DIM)]


def stack_heads(value, masks, axis):
    wide = value.astype(F32)
    return jnp.concatenate([jnp.where(m, wide, 0.0).astype(LOW) for m in masks], axis=axis)


def own_heads(stacked, masks, rows):
    parts = [stacked[h * rows : (h + 1) * rows] for h in range(len(masks))]
    out = jnp.where(masks[0], parts[0], 0.0)
    for mask, part in zip(masks[1:], parts[1:]):
        out = jnp.where(mask, part, out)
    return out


def attend_body(
    meta, tokens, queries, own, other, key_w, value_w, out_w, gain, bias,
    summary, keys, values, probs, mixed, attended, lifted, inverse_out,
):
    span, width = tokens.shape
    rows = summary.shape[0]
    take_by_distance(meta[0], own, other, summary)
    key_all = nn(summary[...], key_w[...]).astype(LOW)
    value_all = nn(summary[...], value_w[...]).astype(LOW)
    keys[...] = key_all
    values[...] = value_all
    side = head_masks((rows, QUAD), 1)
    turned = head_masks((QUAD, rows), 0)
    quads = []
    for q in range(width // QUAD):
        cut = slice(q * QUAD, (q + 1) * QUAD)
        scores = nt(stack_heads(key_all[:, cut], side, 0), queries[:, cut])
        lows = []
        for h in range(len(side)):
            part = scores[h * rows : (h + 1) * rows]
            grown = jnp.exp(part - jnp.max(part, axis=0, keepdims=True))
            lows.append((grown / jnp.sum(grown, axis=0, keepdims=True)).astype(LOW))
        low = jnp.concatenate(lows, axis=0)
        probs[q * low.shape[0] : (q + 1) * low.shape[0], :] = low
        quads.append(nn(stack_heads(value_all[:, cut].astype(F32).T, turned, 1), low).T)
    mixed_low = jnp.concatenate(quads, axis=1).astype(LOW)
    mixed[...] = mixed_low
    total = tokens[...].astype(F32) + nn(mixed_low, out_w[...])
    attended[...] = total
    unit, inverse = centre(total)
    inverse_out[...] = jnp.broadcast_to(inverse, inverse_out.shape)
    lifted[...] = (unit * row(gain) + row(bias)).astype(LOW)


def attend(meta, tokens, queries, own, other, key_w, value_w, out_w, gain, bias):
    seqs, span, width = tokens.shape
    pairs = own.shape[0]
    rows = 2 * pairs * own.shape[2]
    tall = (width // HEAD_DIM) * rows
    weight = whole(width, width)
    return call(
        attend_body,
        (seqs,),
        (meta, *kept_far(tokens, queries), own, other, key_w, value_w, out_w, gain, bias),
        [
            far((seqs, rows, width)),
            far((seqs, rows, width)),
            far((seqs, rows, width)),
            far((seqs, tall, span)),
            far((seqs, span, width)),
            far((seqs, span, width), F32),
            shape((seqs, span, width)),
            far((seqs, span, 128), F32),
        ],
        [
            per_seq(rows, width),
            per_seq(rows, width),
            per_seq(rows, width),
            per_seq(tall, span),
            per_seq(span, width),
            per_seq(span, width),
            per_seq(span, width),
            per_seq(span, 128),
        ],
        [
            per_seq(span, width),
            per_seq(span, width),
            distance_spec(pairs, rows, width),
            distance_spec(pairs, rows, width),
            weight,
            weight,
            weight,
            vector(width),
            vector(width),
        ],
        scalars=1,
        limit=32,
        cost=10,
    )


def feed_body(
    order, lifted, cotangent, grad_active, up, active_out, grad_out, down_grad, up_grad, turned
):
    @pl.when(pl.program_id(0) == 0)
    def _():
        turned[...] = lifted[...].T

    hidden = nn(lifted[...], up[...])
    share = 0.5 * (1.0 + lax.erf(hidden * 0.5**0.5))
    slope = share + hidden * jnp.exp(-0.5 * hidden * hidden) * 0.3989422804014327
    active = (hidden * share).astype(LOW)
    grad_hidden = (grad_active[...].astype(F32) * slope).astype(LOW)
    active_out[...] = active
    grad_out[...] = grad_hidden
    pieces, line = down_grad.shape[0], down_grad.shape[1]
    value = nn(active.T, cotangent[...])
    for piece in range(pieces):
        down_grad[piece ^ order[1]] = value[piece * line : (piece + 1) * line].astype(LOW)
    value = nn(turned[...], grad_hidden)
    line = up_grad.shape[1]
    for piece in range(pieces):
        up_grad[piece ^ order[2]] = value[piece * line : (piece + 1) * line].astype(LOW)


def feed(own, pieces, order, lifted, cotangent, grad_active, up):
    rows, width = lifted.shape
    steps = width // QUAD
    pairs = up.shape[1] // width // 2

    def columns(i, m):
        return (0, block_at(i // steps, own, m) * steps + i % steps)

    def lines(i, m):
        return (i // steps, 0, i % steps)

    return call(
        feed_body,
        (pairs * steps,),
        (order, lifted, cotangent, grad_active, up),
        [
            far((pairs, rows, width)),
            far((pairs, rows, width)),
            shape((pieces, pairs, steps, QUAD // pieces, width)),
            shape((pieces, pairs, width // pieces, width)),
        ],
        [
            pl.BlockSpec((None, rows, QUAD), lines),
            pl.BlockSpec((None, rows, QUAD), lines),
            pl.BlockSpec(
                (pieces, None, None, QUAD // pieces, width),
                lambda i, m: (0, i // steps, i % steps, 0, 0),
            ),
            pl.BlockSpec(
                (pieces, None, width // pieces, QUAD), lambda i, m: (0, i // steps, 0, i % steps)
            ),
        ],
        [
            whole(rows, width),
            whole(rows, width),
            pl.BlockSpec((rows, QUAD), columns),
            pl.BlockSpec((width, QUAD), columns),
        ],
        [pltpu.VMEM((width, rows), LOW)],
        scalars=1,
        limit=20,
        cost=6 * pairs,
    )


def feed_back_body(
    order, sent, kept, up, cotangent, attended, inverse, gain, out_w,
    grad_attended, grad_branch, grad_mixed, norm_grads,
):
    width = cotangent.shape[1]

    @pl.when(pl.program_id(0) == 0)
    def _():
        norm_grads[...] = jnp.zeros_like(norm_grads)

    total = attended[...]
    scale = inverse[:, :1]
    unit = (total - jnp.mean(total, axis=-1, keepdims=True)) * scale
    grad = 0.0
    for own, hiddens in enumerate((sent, kept)):
        for pair in range(hiddens.shape[0]):
            start = pl.multiple_of(block_at(pair, own, order) * width, width)
            grad += nt(hiddens[pair], up[:, pl.ds(start, width)])
    norm_grads[0:1, :] += jnp.sum(grad * unit, axis=0, keepdims=True)
    norm_grads[1:2, :] += jnp.sum(grad, axis=0, keepdims=True)
    whole_grad = cotangent[...].astype(F32) + normalize_back(grad, unit, scale, row(gain))
    grad_attended[...] = whole_grad
    branch = whole_grad.astype(LOW)
    grad_branch[...] = branch
    grad_mixed[...] = nt(branch, out_w[...]).astype(LOW)


def feed_back(order, hiddens, up, cotangent, attended, inverse, gain, out_w):
    seqs, span, width = cotangent.shape
    block = per_seq(span, width)
    lines = pl.BlockSpec((hiddens[0].shape[0], span, width), lambda s, *_: (0, s, 0))
    return call(
        feed_back_body,
        (seqs,),
        (
            order, *kept_far(*hiddens), up, *kept_far(cotangent, attended, inverse), gain, out_w,
        ),
        [
            far((seqs, span, width), F32),
            far((seqs, span, width)),
            shape((seqs, span, width)),
            shape((8, width), F32),
        ],
        [block, block, block, result(8, width)],
        [
            *([lines] * len(hiddens)), whole(*up.shape), block, block, per_seq(span, 128),
            vector(width), whole(width, width),
        ],
        scalars=1,
        limit=24,
        cost=8,
    )


def attend_back_body(
    meta, grad_mixed, queries, keys, values, probs, key_w, value_w,
    grad_queries, grad_keys, grad_values, kept, sent, held,
):
    span, width = grad_mixed.shape
    rows = keys.shape[0]
    side = head_masks((rows, QUAD), 1)
    turned = head_masks((QUAD, rows), 0)
    for q in range(width // QUAD):
        cut = slice(q * QUAD, (q + 1) * QUAD)
        mixed_cut = grad_mixed[:, cut]
        tall = len(side) * rows
        low = probs[q * tall : (q + 1) * tall, :]
        grad_probs = nt(stack_heads(values[:, cut], side, 0), mixed_cut)
        lows = []
        for h in range(len(side)):
            part = low[h * rows : (h + 1) * rows].astype(F32)
            ours = grad_probs[h * rows : (h + 1) * rows]
            inner = jnp.sum(part * ours, axis=0, keepdims=True)
            lows.append((part * (ours - inner)).astype(LOW))
        grad_scores = jnp.concatenate(lows, axis=0)
        grad_values[:, cut] = own_heads(nn(low, mixed_cut), side, rows).astype(LOW)
        grad_keys[:, cut] = own_heads(nn(grad_scores, queries[:, cut]), side, rows).astype(LOW)
        keys_turned = stack_heads(keys[:, cut].astype(F32).T, turned, 1)
        grad_queries[:, cut] = (nn(keys_turned, grad_scores) * SCALE).T.astype(LOW)
    grad_summary = nt(grad_keys[...], key_w[...]) + nt(grad_values[...], value_w[...])
    send_by_distance(meta[0], grad_summary, held, kept, sent)


def attend_back(pairs, meta, grad_mixed, queries, keys, values, probs, key_w, value_w):
    seqs, span, width = grad_mixed.shape
    rows = keys.shape[1]
    tall = probs.shape[1]
    weight = whole(width, width)
    block, rows_block = per_seq(span, width), per_seq(rows, width)
    distance = distance_spec(pairs, rows, width)
    return call(
        attend_back_body,
        (seqs,),
        (meta, grad_mixed, *kept_far(queries, keys, values, probs), key_w, value_w),
        [
            far((seqs, span, width)),
            far((seqs, rows, width)),
            far((seqs, rows, width)),
            distance_rows(pairs, seqs, rows, width),
            distance_rows(pairs, seqs, rows, width),
        ],
        [block, rows_block, rows_block, distance, distance],
        [block, block, rows_block, rows_block, per_seq(tall, span), weight, weight],
        [pltpu.VMEM((rows, width), F32)],
        scalars=1,
        limit=24,
        cost=14,
    )


def squares_body(
    order, normed, summary, mixed, grad_queries, grad_keys, grad_values, grad_branch,
    sent_1, sent_2, kept_1, kept_2, normed_t, summary_t, mixed_t,
):
    @pl.when(pl.program_id(0) == 0)
    def _():
        normed_t[...] = normed[...].T
        summary_t[...] = summary[...].T
        mixed_t[...] = mixed[...].T

    pieces = sent_1.shape[0]
    half = normed_t.shape[0] // 2
    members = (
        (normed_t, grad_queries, (sent_1, kept_1), 0, order[1]),
        (summary_t, grad_keys, (sent_1, kept_1), 1, order[1]),
        (summary_t, grad_values, (sent_2, kept_2), 0, order[2]),
        (mixed_t, grad_branch, (sent_2, kept_2), 1, order[2]),
    )
    for left, right, outs, at, mask in members:
        for out, side in zip(outs, (1 - order[0], order[0])):
            start = pl.multiple_of(side * half, half)
            value = nn(left[pl.ds(start, half), :], right[...])
            cut = half // pieces
            for piece in range(pieces):
                out[piece ^ mask, at] = value[piece * cut : (piece + 1) * cut].astype(LOW)


def squares(
    pieces, order, normed, summary, mixed, grad_queries, grad_keys, grad_values, grad_branch
):
    rows, width = normed.shape
    tall = summary.shape[0]
    cut = QUAD
    line = width // 2 // pieces
    return call(
        squares_body,
        (width // cut,),
        (
            order, normed, summary, mixed,
            *kept_far(grad_queries, grad_keys, grad_values, grad_branch),
        ),
        [shape((pieces, 2, line, width))] * 4,
        [pl.BlockSpec((pieces, 2, line, cut), lambda i, m: (0, 0, 0, i))] * 4,
        [
            whole(rows, width),
            whole(tall, width),
            whole(rows, width),
            pl.BlockSpec((rows, cut), lambda i, m: (0, i)),
            pl.BlockSpec((tall, cut), lambda i, m: (0, i)),
            pl.BlockSpec((tall, cut), lambda i, m: (0, i)),
            pl.BlockSpec((rows, cut), lambda i, m: (0, i)),
        ],
        [
            pltpu.VMEM((width, rows), LOW),
            pltpu.VMEM((width, tall), LOW),
            pltpu.VMEM((width, rows), LOW),
        ],
        scalars=1,
        limit=24,
        cost=7,
    )


def place_feed_body(order, own_down, other_down, own_up, other_up, down, up, total):
    pair, side = pl.program_id(0), pl.program_id(1)
    ours = (side ^ order[0]) == 0

    @pl.when((pair == 0) & (side == 0))
    def _():
        total[...] = jnp.zeros_like(total)

    def place(down_in, up_in):
        pieces, _, steps, line, _ = down_in.shape
        tall = up_in.shape[2]

        def one(piece, square):
            for step in range(steps):
                value = down_in[piece ^ order[1], pair, step].astype(F32)
                start = pl.multiple_of(step * pieces * line + piece * line, line)
                down[pl.ds(start, line), :] = value
                square += jnp.sum(value * value, axis=0, keepdims=True)
            value = up_in[piece ^ order[2], pair].astype(F32)
            up[pl.ds(pl.multiple_of(piece * tall, tall), tall), :] = value
            return square + jnp.sum(value * value, axis=0, keepdims=True)

        total[0:1, :] += lax.fori_loop(0, pieces, one, jnp.zeros((1, down.shape[1]), F32))

    pl.when(ours)(lambda: place(own_down, own_up))
    pl.when(jnp.logical_not(ours))(lambda: place(other_down, other_up))


def place_feed(order, down_shape, up_shape, *arrays):
    width = down_shape[1]
    return call(
        place_feed_body,
        (down_shape[0] // width // 2, 2),
        (order, *arrays),
        [shape(down_shape, F32), shape(up_shape, F32), shape((8, width), F32)],
        [
            pl.BlockSpec((width, width), lambda h, i, m: (2 * h + i, 0)),
            pl.BlockSpec((width, width), lambda h, i, m: (0, 2 * h + i)),
            result(8, width),
        ],
        [whole(*x.shape) for x in arrays],
        scalars=1,
        limit=28,
        cost=8,
    )


def place_squares_body(order, *refs):
    inputs, (others, norms, *outs), total = refs[:8], refs[8:-1], refs[-1]
    *outs, attn_gain, attn_bias, ffn_gain, ffn_bias, norm = outs
    side = pl.program_id(0)
    ours = (side ^ order[0]) == 0

    @pl.when(side == 0)
    def _():
        total[...] = others[...]

    def place(first, second):
        count, _, line, width = first[0].shape
        square = jnp.zeros((1, width), F32)
        for at in range(2 * count):
            for source, mask, pair in ((first, order[1], outs[:2]), (second, order[2], outs[2:])):
                start = pl.multiple_of((at ^ mask) * line, line)
                for member, out in enumerate(pair):
                    value = source[at // count][at % count, member].astype(F32)
                    out[pl.ds(start, line), :] = value
                    square += jnp.sum(value * value, axis=0, keepdims=True)
        total[0:1, :] += square

    pl.when(ours)(lambda: place(inputs[:2], inputs[4:6]))
    pl.when(jnp.logical_not(ours))(lambda: place(inputs[2:4], inputs[6:]))

    @pl.when(side == 1)
    def _():
        value = norms[...].astype(F32)
        square = jnp.sum(total[0:1, :], keepdims=True) + jnp.sum(value * value, keepdims=True)
        span = value.shape[1]
        cuts = attn_gain.shape[0] // span
        for at, out in enumerate((attn_gain, attn_bias, ffn_gain, ffn_bias)):
            for cut in range(cuts):
                line = value[at * cuts + cut : at * cuts + cut + 1]
                out[cut * span : (cut + 1) * span] = line.reshape(span)
        norm[...] = jnp.sqrt(square)


def place_squares(order, others, norms, *arrays):
    count, _, line, width = arrays[0].shape
    return call(
        place_squares_body,
        (2,),
        (order, *arrays, others, norms),
        [shape((4 * count * line, width), F32)] * 4
        + [shape((width,), F32)] * 4
        + [shape((1, 1), F32)],
        [pl.BlockSpec((2 * count * line, width), lambda i, m: (i, 0))] * 4
        + [result(width)] * 4
        + [result(1, 1)],
        [whole(*x.shape) for x in (*arrays, others, norms)],
        [pltpu.VMEM(others.shape, F32)],
        scalars=1,
        limit=24,
        cost=5,
    )


def leave_body(
    meta, own, other, columns, normed, tokens, gain, grad_queries, query_w, grad_attended,
    ffn_norms, tokens_grad, packed, columns_t, terms_sum, norm_grads, grad_summary,
):
    seq = pl.program_id(0)
    rows, span = columns.shape

    @pl.when(seq == 0)
    def _():
        columns_t[...] = columns[...].T
        terms_sum[...] = jnp.zeros_like(terms_sum)
        norm_grads[...] = jnp.zeros_like(norm_grads)

    take_by_distance(meta[0], own, other, grad_summary)
    length = meta[1 + seq] - meta[0] * span
    lane = lax.broadcasted_iota(jnp.int32, (rows, span), 1) < length
    line = lax.broadcasted_iota(jnp.int32, (span, 1), 0) < length
    summed = grad_summary[...]
    terms_sum[...] += jnp.where(lane, nt(summed, normed[...]), 0.0)
    grad = nt(grad_queries[...], query_w[...]) + jnp.where(line, nn(columns_t[...], summed), 0.0)
    unit, inverse = centre(tokens[...].astype(F32))
    norm_grads[0:1, :] += jnp.sum(grad * unit, axis=0, keepdims=True)
    norm_grads[1:2, :] += jnp.sum(grad, axis=0, keepdims=True)
    tokens_grad[...] = (
        grad_attended[...] + normalize_back(grad, unit, inverse, row(gain))
    ).astype(LOW)

    @pl.when(seq == pl.num_programs(0) - 1)
    def _():
        total = terms_sum[...].astype(LOW)
        width = norm_grads.shape[1]
        lines = [
            source[at : at + 1, cut : cut + span]
            for source in (norm_grads, ffn_norms)
            for at in range(2)
            for cut in range(0, width, span)
        ]
        share, tall = rows // packed.shape[0], packed.shape[1]
        lines.append(jnp.zeros((tall - share - len(lines), span), F32))
        norms = jnp.concatenate(lines, axis=0).astype(LOW)
        for at in range(packed.shape[0]):
            packed[at, :share, :] = total[at * share : (at + 1) * share]
            packed[at, share:, :] = norms


def leave(
    ring, meta, own, other, columns, normed, tokens, gain, grad_queries, query_w, grad_attended,
    ffn_norms,
):
    seqs, span, width = tokens.shape
    rows = columns.shape[0]
    distance = distance_spec(own.shape[0], rows, width)
    tall = rows // ring + -(-4 * width // span // 16) * 16
    block = per_seq(span, width)
    return call(
        leave_body,
        (seqs,),
        (
            meta, own, other, columns, *kept_far(normed, tokens), gain, *kept_far(grad_queries), query_w,
            *kept_far(grad_attended), ffn_norms,
        ),
        [shape(tokens.shape), shape((ring, tall, span))],
        [block, result(ring, tall, span)],
        [
            distance, distance, whole(rows, span), block, block, vector(width), block,
            whole(width, width), block, whole(8, width),
        ],
        [
            pltpu.VMEM((span, rows), LOW),
            pltpu.VMEM((rows, span), F32),
            pltpu.VMEM((8, width), F32),
            pltpu.VMEM((rows, width), LOW),
        ],
        scalars=1,
        limit=20,
        cost=5,
    )


def swap(value, axis, mask):
    size = lax.axis_size(axis)
    return lax.ppermute(value, axis, [(i, i ^ mask) for i in range(size)])


def pick(value, at):
    return lax.dynamic_index_in_dim(value, at, 0, keepdims=False)


def bits_of(axis):
    return (lax.axis_size(axis) - 1).bit_length()


def bit(axis, at):
    return (lax.axis_index(axis) >> at) & 1


def after(values, ticket):
    return lax.optimization_barrier((values, ticket))[0]


def in_order(mine, other, at):
    return jnp.where(at == 0, jnp.stack([mine, other]), jnp.stack([other, mine]))


def krow_orders():
    count = bits_of("krow")
    return [list(range(1, count)), list(range(count - 1, 0, -1))]


def distance_masks():
    count = bits_of("krow")
    masks = [bit("krow", 0)]
    for order in krow_orders():
        masks.append(sum(bit("krow", at) << (count - 2 - d) for d, at in enumerate(order)))
    return jnp.stack(masks).astype(jnp.int32)


def sum_everywhere(sent, halved, parted):
    orders = krow_orders()
    flight = [swap(x, "krow", 1) for x in sent]
    kept = yield sent
    ticket = yield kept
    for digit in range(len(orders[0])):
        flight, kept = after((flight, kept), ticket)
        half = kept[0].shape[0] // 2
        sent = [k[half:] + f[half:] for k, f in zip(kept, flight)]
        kept = [k[:half] + f[:half] for k, f in zip(kept, flight)]
        flight = [swap(x, "krow", 1 << o[digit]) for x, o in zip(sent, orders)]
        ticket = yield (sent, kept)
    flight, kept = after((flight, kept), ticket)
    values = [(k + f)[0] for k, f in zip(kept, flight)]
    count = bits_of("dp")
    strides = [list(range(count)), list(range(count - 1, -1, -1))]
    sides = [bit("dp", stride[0]) for stride in strides]
    for stage in range(count):
        sent = kept = values
        if stage < halved:
            halves = [v.reshape(2, -1, v.shape[-1]) for v in values]
            sent = [pick(h, 1 - side) for h, side in zip(halves, sides)]
            kept = [pick(h, side) for h, side in zip(halves, sides)]
        flight = [swap(x, "dp", 1 << o[stage]) for x, o in zip(sent, strides)]
        ticket = yield (sent, kept)
        flight, kept = after((flight, kept), ticket)
        values = [k + f for k, f in zip(kept, flight)]
    if halved:
        flight = [swap(x, "dp", 1 << o[0]) for x, o in zip(values, strides)]
        ticket = yield values
        flight, values = after((flight, values), ticket)
        values = [
            in_order(v, f, side).reshape(-1, v.shape[-1])
            for v, f, side in zip(values, flight, sides)
        ]
    values = [v[None] for v in values]
    for digit in reversed(range(1, len(orders[0]))):
        flight = [swap(v, "krow", 1 << o[digit]) for v, o in zip(values, orders)]
        ticket = yield values
        flight, values = after((flight, values), ticket)
        values = [jnp.concatenate([v, f]) for v, f in zip(values, flight)]
    early = [swap(v, "krow", 1) for v in values] if parted else []
    flight = [swap(v, "krow", 1 << o[0]) for v, o in zip(values, orders)]
    ticket = yield values
    flight, values, early = after((flight, values, early), ticket)
    if parted:
        late = [swap(f, "krow", 1) for f in flight]
        ticket = yield (flight, values, early)
        yield after([x for color in zip(values, flight, early, late) for x in color], ticket)
    else:
        values = [jnp.concatenate([v, f]) for v, f in zip(values, flight)]
        flight = [swap(v, "krow", 1) for v in values]
        ticket = yield values
        yield after([x for color in zip(values, flight) for x in color], ticket)


def sum_krow(sent, kept):
    pairs = kept.shape[0]
    flight = swap(sent, "krow", 1)
    ticket = yield kept
    kept, flight = after((kept, flight), ticket)
    half = [k.astype(F32) + f.astype(F32) for k, f in zip(kept, flight)]
    sent = [h.astype(LOW) for h in half[1:]]
    flight = [swap(x, "krow", 2 * pair) for pair, x in enumerate(sent, 1)]
    kept = half[0]
    ticket = yield (kept, sent)
    kept, flight = after((kept, flight), ticket)
    total = sum([f.astype(F32) for f in flight], kept).astype(LOW)
    flight = [swap(total, "krow", 2 * pair) for pair in range(1, pairs)]
    ticket = yield total
    total, flight = after((total, flight), ticket)
    own = jnp.stack([total, *flight])
    flight = swap(own, "krow", 1)
    ticket = yield own
    yield after((own, flight), ticket)


def sum_terms(packed, share):
    span = packed.shape[2]
    flight = lax.all_to_all(packed, "krow", 0, 0, tiled=True)
    ticket = yield packed
    flight = after(flight, ticket)
    norms = jnp.sum(flight[:, share:].astype(F32), axis=0).astype(LOW)
    value = jnp.concatenate([flight[:, :share].reshape(-1, span), norms])
    for at in range(bits_of("dp")):
        flight = swap(value, "dp", 1 << at)
        ticket = yield value
        flight, value = after((flight, value), ticket)
        value = value + flight
    norms, value = value[packed.shape[0] * share :], value.astype(F32)
    ring = packed.shape[0]
    rows = ring * share
    compress = value[:rows].reshape(ring, share, span).transpose(1, 0, 2).reshape(share, -1)
    yield (compress, norms)


class Line:
    def __init__(self, ticket):
        self.ticket = ticket

    def step(self, *sums):
        for each in sums:
            self.ticket = each.send(self.ticket)

    def run(self, kernel, *values):
        self.ticket = kernel(*after(values, self.ticket))
        return self.ticket


    def start(self, steps, *first):
        self.ticket = (self.ticket, next(steps))
        for value in first:
            self.ticket = (self.ticket, steps.send(value))
        return steps


PLAN = "S1K1AB1gQ1gg31O13gL313c31c3c3c311P33"
HALVED = {"1": 1, "3": 1}


def local(
    tokens,
    lengths,
    attn_gain,
    attn_bias,
    query_weight,
    key_weight,
    value_weight,
    out_weight,
    compress,
    ffn_gain,
    ffn_bias,
    up_weight,
    down_weight,
    cotangent,
):
    seqs, span, width = tokens.shape
    ring = lax.axis_size("krow")
    rows = compress.shape[0] * ring
    pairs = pieces = ring // 2
    flat, tall = (seqs * span, width), (seqs * rows, width)
    order = distance_masks()
    meta = jnp.concatenate([lax.axis_index("krow")[None].astype(jnp.int32), lengths])
    columns = lax.all_to_all(
        compress.reshape(compress.shape[0], ring, span), "krow", 1, 0, tiled=False
    ).reshape(rows, span)
    cotangent_flat = cotangent.reshape(flat)
    normed = enter(tokens, attn_gain, attn_bias)
    kept, sent = summarize(pairs, meta, columns, normed)
    line = Line((kept, sent))
    summing = line.start(sum_krow(sent, kept))
    line.step(summing)
    grad_active = line.run(grad_active_of, cotangent_flat, down_weight)
    line.step(summing)
    queries = line.run(project, normed, query_weight)
    line.step(summing, summing)
    summary, keys, values, probs, mixed, attended, lifted, inverse = attend(
        meta, tokens, queries, *line.ticket, key_weight, value_weight, out_weight, ffn_gain,
        ffn_bias,
    )
    line.ticket = lifted

    def as_pieces(arrays):
        return [x.reshape(pieces, -1, width) for x in arrays]

    known, sums, results = {}, {}, {}

    def run_feed(own):
        name = ("sent", "kept")[own]
        known[f"active_{name}"], known[f"hidden_{name}"], *known[f"{name}_1"] = line.run(
            lambda lifted: feed(
                own, pieces, order, lifted.reshape(flat), cotangent_flat, grad_active, up_weight
            ),
            lifted,
        )

    def run_a():
        known["grad_attended"], known["grad_branch"], known["grad_mixed"], known["ffn_norms"] = (
            line.run(
                lambda *hiddens: feed_back(
                    order, hiddens, up_weight, cotangent, attended, inverse, ffn_gain, out_weight
                ),
                known["hidden_sent"],
                known["hidden_kept"],
            )
        )

    def run_b():
        *known["grads"], known["kept_g"], known["sent_g"] = line.run(
            lambda grad_mixed: attend_back(
                pairs, meta, grad_mixed, queries, keys, values, probs, key_weight, value_weight
            ),
            known["grad_mixed"],
        )

    def run_q():
        out = line.run(
            lambda branch, grad_queries, grad_keys, grad_values: squares(
                pieces, order, normed.reshape(flat), summary.reshape(tall), mixed.reshape(flat),
                grad_queries.reshape(flat), grad_keys.reshape(tall), grad_values.reshape(tall),
                branch.reshape(flat),
            ),
            known["grad_branch"],
            *known["grads"],
        )
        known["sent_3"], known["kept_3"] = out[:2], out[2:]

    def run_o():
        known["block_out"] = line.run(
            lambda *actives: block_out_of(order, down_weight, attended, *actives),
            known["active_sent"],
            known["active_kept"],
        )

    def run_l():
        finish("g")
        known["tokens_grad"], known["terms"] = line.run(
            lambda own, other: leave(
                ring, meta, own, other, columns, normed, tokens, attn_gain, known["grads"][0],
                query_weight, known["grad_attended"], known["ffn_norms"],
            ),
            *results["g"],
        )

    def run_p():
        finish("1")
        pairs_held = down_weight.shape[0] // width // 2
        steps = width // QUAD
        forms = ((pieces, pairs_held, steps, QUAD // pieces, width), (pieces, pairs_held, -1, width))
        arrays = [x.reshape(forms[at // 2]) for at, x in enumerate(results["1"])]
        known["feed"] = line.run(
            lambda *arrays: place_feed(order, down_weight.shape, up_weight.shape, *arrays),
            *arrays,
        )

    def begin(name):
        if name == "g":
            return sum_krow(known["sent_g"], known["kept_g"])
        if name == "c":
            return sum_terms(known["terms"], rows // ring)
        return sum_everywhere(as_pieces(known[f"sent_{name}"]), HALVED[name], name == "3")

    def advance(name):
        if name not in sums:
            sums[name] = [begin(name), 0]
            with jax.named_scope(f"sum_{name}_0"):
                line.start(sums[name][0])
        else:
            if sums[name][1] == 1 and name in HALVED:
                sums[name][0].send(as_pieces(known[f"kept_{name}"]))
            try:
                with jax.named_scope(f"sum_{name}_{sums[name][1]}"):
                    line.step(sums[name][0])
                results[name] = line.ticket
            except StopIteration:
                return False
        sums[name][1] += 1
        return True

    def finish(name):
        while advance(name):
            pass

    kernels = {
        "S": lambda: run_feed(0), "K": lambda: run_feed(1), "A": run_a, "B": run_b, "Q": run_q,
        "O": run_o, "L": run_l, "P": run_p,
    }
    for name in PLAN:
        if name in kernels:
            kernels[name]()
        else:
            advance(name)
    for name in "c3":
        finish(name)
    down_grad, up_grad, others = known["feed"]
    arrays = [x.reshape(pieces // 2, 2, -1, width) for x in results["3"]]
    compress_grad, norms = results["c"]
    *attn_grads, gain_1, bias_1, gain_2, bias_2, grad_norm = place_squares(
        order, others, norms, *arrays
    )
    block_out, tokens_grad = known["block_out"], known["tokens_grad"]
    return (
        block_out,
        tokens_grad,
        gain_1,
        bias_1,
        *attn_grads,
        compress_grad,
        gain_2,
        bias_2,
        up_grad,
        down_grad,
        grad_norm.reshape(()),
    )


def solution(mesh):
    rows, held = P("dp", "krow", None), P("krow", None)
    in_specs = (rows, P("dp"), P(), P(), P(), P(), P(), P(), held, P(), P(), P(), P(), rows)
    out_specs = (rows, rows, P(), P(), P(), P(), P(), P(), held, P(), P(), P(), P(), P())
    return jax.shard_map(local, mesh=mesh, in_specs=in_specs, out_specs=out_specs, check_vma=False)
```
